256 devices in a mesh: rounds: 8 (over z), tiles: 32 (over y, x, core).
Axes of the slice: x: 4, y: 4, z: 8, core: 2. Of those that a mesh axis runs over, the one named last changes fastest.
Arguments:
- syndromes: int32 [8, 2, 8, 64, 64], P(None, None, 'rounds', 'tiles'), may hold values 0 or 1
- labels: int32 [2, 8], P(None, 'rounds'), may hold values from 0 to 1
- stab_gate: bfloat16 [64, 64, 512], P('tiles'), may hold values from -6 to 6
- bit_gate: float32 [512], replicated, may hold values from -6 to 6
- forget_bias: float32 [128], replicated, may hold values from -1 to 4
- conv_weight: bfloat16 [3, 3, 128, 512], replicated, may hold values from -0.375 to 0.375
- query: float32 [128], replicated, may hold values from -12 to 12
- readout_weight: float32 [128], replicated, may hold values from -6 to 6
Outputs:
- grad_conv: float32 [3, 3, 128, 512], replicated
- grad_stab: float32 [64, 64, 512], P('tiles')
- grad_bit: float32 [512], replicated
- grad_forget: float32 [128], replicated
- grad_query: float32 [128], replicated
- grad_readout: float32 [128], replicated
- loss: float32 [], replicated
The draws below stay inside these ranges and needn't reach their ends.
All inputs are finite; a program needn't handle non-finite values. No bound on the sum of `syndromes` on one device may be relied on, other than what follows from the above.
Results may differ from the reference program's by a relative error of at most 0.014.
Values may be sent and summed in bfloat16 or wider, within the bound.
No kernel may reach another device: no remote copies, remote signals or barrier semaphores. Data moves between devices by JAX's collectives and lax.ppermute only.
A program may use at most 64 MiB of HBM per device.

```python
import math
import jax
import jax.numpy as jnp
from jax import lax

CHANNELS = 128
GATE_UNITS = 512
GRID_C = 64
GRID_R = 64
SHOTS = 8
MICRO = 2
ROUNDS = 8


def with_ends(values, key, least, largest):
    extent = values.shape
    spot = [jax.random.randint(jax.random.fold_in(key, axis), (), 0, extent[axis]) for axis in range(len(extent))]
    values = values.at[tuple(spot)].set(least)
    longest = extent.index(max(extent))
    spot[longest] = (spot[longest] + 1) % extent[longest]
    return values.at[tuple(spot)].set(largest)


def block_levels(own_key, extent, cuts, least, high):
    def one(dim, shards_of):
        steps = jax.random.uniform(jax.random.fold_in(jax.random.fold_in(own_key, 6), dim), (shards_of,), jnp.float32, least / len(cuts), high / len(cuts))
        return jnp.repeat(jnp.exp(steps), extent[dim] // shards_of).reshape((-1,) + (1,) * (len(extent) - dim - 1))

    gain = one(*cuts[0])
    for cut in cuts[1:]:
        gain = gain * one(*cut)
    return gain


def scatter_about(own_key, dims, width, most, shards=(), dtype=jnp.bfloat16):
    entries = jax.random.normal(own_key, dims, jnp.float32) * width
    if len(shards) > 0:
        entries = block_levels(own_key, dims, shards, -0.22, 0.18) * entries
    return jnp.clip(entries, min=-most, max=most).astype(dtype)


def setup_inputs(seed: int = 0) -> dict:
    keys = jax.random.split(jax.random.key(seed), 9)
    syndromes = with_ends((jax.random.randint(keys[0], (ROUNDS, MICRO, SHOTS, GRID_R, GRID_C), 0, 4) < 1).astype(jnp.int32), jax.random.fold_in(keys[0], 1), 0, 1)
    labels = with_ends(jax.random.randint(keys[1], (MICRO, SHOTS), 0, 2), jax.random.fold_in(keys[1], 1), 0, 1).astype(jnp.int32)
    stab_gate = scatter_about(keys[2], (GRID_R, GRID_C, GATE_UNITS), 1.0, 6.0, ((0, 32),))
    bit_gate = scatter_about(keys[3], (GATE_UNITS,), 1.0, 6.0, (), jnp.float32)
    forget_bias = jnp.clip(jax.random.uniform(keys[4], (CHANNELS,), jnp.float32, -1.0, 4.0), -1.0, 4.0)
    conv_weight = scatter_about(keys[5], (3, 3, CHANNELS, GATE_UNITS), (2 * CHANNELS) ** -0.5, 0.375)
    query = scatter_about(keys[6], (CHANNELS,), 2.0, 12.0, (), jnp.float32)
    readout_weight = scatter_about(keys[7], (CHANNELS,), 1.0, 6.0, (), jnp.float32)
    return dict(syndromes=syndromes, labels=labels, stab_gate=stab_gate, bit_gate=bit_gate, forget_bias=forget_bias, conv_weight=conv_weight, query=query, readout_weight=readout_weight)


def make_patches(padded):
    row_count = padded.shape[1] - 2
    col_count = padded.shape[2] - 2
    pieces = [padded[:, a:a + row_count, b:b + col_count, :] for a in range(3) for b in range(3)]
    return jnp.concatenate(pieces, axis=-1).reshape(-1, 9 * padded.shape[3])

def cell_forward(gate_input, cell_prev, channels):
    input_gate = jax.nn.sigmoid(gate_input[:, :channels])
    forget = jax.nn.sigmoid(gate_input[:, channels:2 * channels])
    candidate = jnp.tanh(gate_input[:, 2 * channels:3 * channels])
    output_gate = jax.nn.sigmoid(gate_input[:, 3 * channels:])
    cell_new = forget * cell_prev + input_gate * candidate
    hidden_new = (output_gate * jnp.tanh(cell_new)).astype(jnp.bfloat16)
    gate_values = jnp.concatenate([input_gate, forget, candidate, output_gate], axis=1)
    return (gate_values, cell_new, hidden_new)

def cell_backward(gate_values, cell_prev, cell_new, d_hidden, d_cell, channels):
    input_gate = gate_values[:, :channels]
    forget = gate_values[:, channels:2 * channels]
    candidate = gate_values[:, 2 * channels:3 * channels]
    output_gate = gate_values[:, 3 * channels:]
    squash = jnp.tanh(cell_new)
    d_total = d_cell + d_hidden * output_gate * (1.0 - squash * squash)
    d_gates = jnp.concatenate([d_total * candidate * input_gate * (1.0 - input_gate), d_total * cell_prev * forget * (1.0 - forget), d_total * input_gate * (1.0 - candidate * candidate), d_hidden * squash * output_gate * (1.0 - output_gate)], axis=1).astype(jnp.bfloat16)
    return (d_gates, d_total * forget)

def column_total(products, col_count, row_shift):
    result = products[:, :, 2:2 + col_count, row_shift, 0]
    for col_shift in range(1, 3):
        result = result + products[:, :, 2 - col_shift:2 - col_shift + col_count, row_shift, col_shift]
    return result

def reference(syndromes, labels, stab_gate, bit_gate, forget_bias, conv_weight, query, readout_weight):
    channels = CHANNELS
    gate_units = GATE_UNITS
    lattice = GRID_R * GRID_C
    weight_matrix = conv_weight.reshape(9 * channels, gate_units)
    stab_rows = stab_gate.reshape(lattice, gate_units).astype(jnp.float32)
    forget_shift = jnp.concatenate([jnp.zeros((channels,), jnp.float32), forget_bias, jnp.zeros((2 * channels,), jnp.float32)])
    score_scale = 1.0 / math.sqrt(channels)
    fired_all = jnp.transpose(syndromes.reshape(ROUNDS, MICRO * SHOTS, lattice), (1, 0, 2))
    targets = labels.reshape(MICRO * SHOTS).astype(jnp.float32)

    def forward_round(recurrent, fired_bits):
        hidden_prev, cell_prev = recurrent
        hidden_pad = jnp.pad(hidden_prev, ((0, 0), (1, 1), (1, 1), (0, 0)))
        gate_input = jnp.dot(make_patches(hidden_pad), weight_matrix, preferred_element_type=jnp.float32)
        gate_input = gate_input + stab_rows + fired_bits.astype(jnp.float32)[:, None] * bit_gate + forget_shift
        gate_values, cell_new, hidden_new = cell_forward(gate_input, cell_prev, channels)
        return ((hidden_new.reshape(1, GRID_R, GRID_C, channels), cell_new), (hidden_pad, gate_values, cell_prev, cell_new, fired_bits))

    def backward_round(state_carry, saved_items):
        d_hidden, d_cell, grad_weight, grad_stab, grad_fired, grad_keep = state_carry
        hidden_pad, gate_values, cell_prev, cell_new, fired_bits = saved_items
        d_gates, d_cell_prev = cell_backward(gate_values, cell_prev, cell_new, d_hidden, d_cell, channels)
        grad_weight = grad_weight + lax.dot_general(make_patches(hidden_pad), d_gates, (((0,), (0,)), ((), ())), preferred_element_type=jnp.float32)
        grad_stab = grad_stab + d_gates.astype(jnp.float32)
        grad_fired = grad_fired + jnp.dot(fired_bits.astype(jnp.bfloat16)[None, :], d_gates, preferred_element_type=jnp.float32)[0]
        grad_keep = grad_keep + lax.optimization_barrier(jnp.sum(d_gates[:, channels:2 * channels].astype(jnp.float32), axis=0))
        d_pad = jnp.pad(d_gates.reshape(1, GRID_R, GRID_C, gate_units), ((0, 0), (1, 1), (1, 1), (0, 0)))
        products = lax.dot_general(d_pad, weight_matrix, (((3,), (1,)), ((), ())), preferred_element_type=jnp.float32)
        products = products.reshape(1, GRID_R + 2, GRID_C + 2, 3, 3, channels)
        d_prev = column_total(products[:, 2:2 + GRID_R], GRID_C, 0)
        for row_shift in range(1, 3):
            d_prev = d_prev + column_total(products[:, 2 - row_shift:2 - row_shift + GRID_R], GRID_C, row_shift)
        return ((d_prev.reshape(lattice, channels), d_cell_prev, grad_weight, grad_stab, grad_fired, grad_keep), None)

    def one_shot(totals, inputs):
        fired_rounds, target = inputs
        initial = (jnp.zeros((1, GRID_R, GRID_C, channels), jnp.bfloat16), jnp.zeros((lattice, channels), jnp.float32))
        (hidden_last, unused_cell), saved = lax.scan(forward_round, initial, fired_rounds)
        hidden_full = hidden_last.reshape(lattice, channels).astype(jnp.float32)
        scores = lax.optimization_barrier(jnp.sum(hidden_full * query, axis=1)) * score_scale
        exp_score = jnp.exp(scores)
        total_exp = jnp.sum(exp_score)
        pooled = lax.optimization_barrier(jnp.sum(exp_score[:, None] * hidden_full, axis=0)) / total_exp
        logit_value = jnp.sum(pooled * readout_weight)
        loss_term = jax.nn.softplus(logit_value) - target * logit_value
        d_logit = jax.nn.sigmoid(logit_value) - target
        d_pooled = d_logit * readout_weight
        weight = exp_score / total_exp
        d_score = weight * (lax.optimization_barrier(jnp.sum(hidden_full * d_pooled, axis=1)) - jnp.sum(pooled * d_pooled))
        d_hidden = weight[:, None] * d_pooled + d_score[:, None] * query * score_scale
        query_term = score_scale * lax.optimization_barrier(jnp.sum(d_score[:, None] * hidden_full, axis=0))
        readout_term = d_logit * pooled
        grad_weight, grad_stab, grad_fired, grad_keep, grad_query, grad_readout, loss_total = totals
        start_back = (d_hidden, jnp.zeros((lattice, channels), jnp.float32), grad_weight, grad_stab, grad_fired, grad_keep)
        back_state, unused_out = lax.scan(backward_round, start_back, saved, reverse=True)
        return ((back_state[2], back_state[3], back_state[4], back_state[5], grad_query + query_term, grad_readout + readout_term, loss_total + loss_term), None)
    zero_totals = (jnp.zeros((9 * channels, gate_units), jnp.float32), jnp.zeros((lattice, gate_units), jnp.float32), jnp.zeros((gate_units,), jnp.float32), jnp.zeros((channels,), jnp.float32), jnp.zeros((channels,), jnp.float32), jnp.zeros((channels,), jnp.float32), jnp.zeros((), jnp.float32))
    totals, unused_out = lax.scan(one_shot, zero_totals, (fired_all, targets))
    return (totals[0].reshape(3, 3, channels, gate_units), totals[1].reshape(GRID_R, GRID_C, gate_units), totals[2], totals[3], totals[4], totals[5], totals[6])
```

```python
import math

import jax
import jax.numpy as jnp
from jax import lax
from jax.sharding import PartitionSpec as P


def swap(values, axis, mask):
    count = lax.axis_size(axis)
    return lax.ppermute(values, axis, [(i, i ^ mask) for i in range(count)])


def tree_sum(parts):
    while len(parts) > 1:
        parts = [parts[i] + parts[i + 1] for i in range(0, len(parts), 2)]
    return parts[0]


def pick(blocks, index):
    return lax.dynamic_index_in_dim(blocks, index, 0, keepdims=False)


def swap_sum(values, axis, masks):
    return tree_sum([values] + [swap(values, axis, m) for m in masks])


def unxor(parts, place):
    bit = 1
    while bit < len(parts):
        flip = (place & bit) != 0
        parts = [jnp.where(flip, parts[i ^ bit], parts[i]) for i in range(len(parts))]
        bit *= 2
    return parts


def tile_groups(count):
    groups = []
    start = 2
    while start < count:
        size = min(4, count // start)
        groups.append((start, size))
        start *= size
    return groups


def split_words(values):
    high = values.astype(jnp.bfloat16)
    low = (values - high.astype(jnp.float32)).astype(jnp.bfloat16)
    return jnp.concatenate([high, low], axis=0)


def join_words(words):
    half = words.shape[0] // 2
    return words[:half].astype(jnp.float32) + words[half:].astype(jnp.float32)


def scatter_stage(blocks, axis, masks, place, extra=None):
    got = [pick(blocks, place)]
    extras = [] if extra is None else [extra]
    rows = blocks.shape[1]
    words = None if extra is None else split_words(extra)
    for k in range(1, len(masks) + 1):
        sent = pick(blocks, place ^ k).astype(jnp.bfloat16)
        if words is not None:
            sent = jnp.concatenate([sent, words], axis=0)
        back = swap(sent, axis, masks[k - 1])
        got.append(back[:rows].astype(jnp.float32))
        if words is not None:
            extras.append(join_words(back[rows:]))
    total = tree_sum(got)
    if extra is None:
        return total, None
    extras[0] = join_words(words)
    return total, tree_sum(extras)


def gather_stage(piece, axis, masks, place):
    parts = [piece] + [swap(piece, axis, m) for m in masks]
    return jnp.concatenate(unxor(parts, place), axis=0)


def reduce_all(weight_rows, small, stab_rows):
    tiles = lax.axis_size("tiles")
    planes = lax.axis_size("rounds")
    tile = lax.axis_index("tiles")
    plane = lax.axis_index("rounds")
    plane_masks = list(range(1, planes))
    groups = tile_groups(tiles)
    orders = (groups, groups[::-1])
    core = tile & 1

    stab_blocks = stab_rows.reshape(planes, -1, stab_rows.shape[-1])
    stab_piece, unused = scatter_stage(stab_blocks, "rounds", plane_masks, plane)

    halves = weight_rows.reshape(2, -1, 128)
    piece, small = scatter_stage(halves, "tiles", [1], core, small)
    rows = piece.shape[0] // 2
    pieces = [piece[:rows], piece[rows:]]
    for step in range(len(groups)):
        for color in range(2):
            start, size = orders[color][step]
            blocks = pieces[color].reshape(size, -1, 128)
            masks = [start * k for k in range(1, size)]
            place = (tile // start) % size
            pieces[color], added = scatter_stage(
                blocks, "tiles", masks, place, small if color == 0 else None
            )
            if color == 0:
                small = added
    rows = pieces[0].shape[0]
    message = jnp.concatenate(
        [pieces[0].astype(jnp.bfloat16), pieces[1].astype(jnp.bfloat16), split_words(small)], axis=0
    )
    messages = [message] + [swap(message, "rounds", m) for m in plane_masks]
    total = tree_sum([m[: 2 * rows].astype(jnp.float32) for m in messages]).astype(jnp.bfloat16)
    small = tree_sum([join_words(m[2 * rows :]) for m in messages])
    stab_total = gather_stage(stab_piece.astype(jnp.bfloat16), "rounds", plane_masks, plane)

    pieces = [total[:rows], total[rows:]]
    for step in range(len(groups) - 1, -1, -1):
        for color in range(2):
            start, size = orders[color][step]
            masks = [start * k for k in range(1, size)]
            place = (tile // start) % size
            pieces[color] = gather_stage(pieces[color], "tiles", masks, place)
    piece = jnp.concatenate(pieces, axis=0)
    weight_total = gather_stage(piece, "tiles", [1], core)
    return weight_total, small, stab_total


def with_halo(cells, sides, width):
    for axis, dim in sides:
        count = lax.axis_size(axis)
        place = lax.axis_index(axis)
        head = lax.slice_in_dim(cells, 0, width, axis=dim)
        tail = lax.slice_in_dim(cells, cells.shape[dim] - width, cells.shape[dim], axis=dim)
        cells = jnp.concatenate(
            [
                jnp.where(
                    place == 0,
                    jnp.zeros_like(tail),
                    lax.ppermute(tail, axis, [(i, (i + 1) % count) for i in range(count)]),
                ),
                cells,
                jnp.where(
                    place == count - 1,
                    jnp.zeros_like(head),
                    lax.ppermute(head, axis, [((i + 1) % count, i) for i in range(count)]),
                ),
            ],
            axis=dim,
        )
    return cells


def make_patches(padded):
    row_count = padded.shape[1] - 2
    col_count = padded.shape[2] - 2
    pieces = [
        padded[:, a : a + row_count, b : b + col_count, :] for a in range(3) for b in range(3)
    ]
    return jnp.concatenate(pieces, axis=-1).reshape(-1, 9 * padded.shape[3])


def pad_columns(d_field):
    return jnp.pad(d_field, ((0, 0), (0, 0), (1, 1), (0, 0)))


def cell_forward(gate_input, cell_prev, channels):
    input_gate = jax.nn.sigmoid(gate_input[:, :channels])
    forget = jax.nn.sigmoid(gate_input[:, channels : 2 * channels])
    candidate = jnp.tanh(gate_input[:, 2 * channels : 3 * channels])
    output_gate = jax.nn.sigmoid(gate_input[:, 3 * channels :])
    cell_new = forget * cell_prev + input_gate * candidate
    hidden_new = (output_gate * jnp.tanh(cell_new)).astype(jnp.bfloat16)
    gate_values = jnp.concatenate([input_gate, forget, candidate, output_gate], axis=1)
    return (gate_values, cell_new, hidden_new)


def cell_backward(gate_values, cell_prev, cell_new, d_hidden, d_cell, channels):
    input_gate = gate_values[:, :channels]
    forget = gate_values[:, channels : 2 * channels]
    candidate = gate_values[:, 2 * channels : 3 * channels]
    output_gate = gate_values[:, 3 * channels :]
    squash = jnp.tanh(cell_new)
    d_total = d_cell + d_hidden * output_gate * (1.0 - squash * squash)
    d_gates = jnp.concatenate(
        [
            d_total * candidate * input_gate * (1.0 - input_gate),
            d_total * cell_prev * forget * (1.0 - forget),
            d_total * input_gate * (1.0 - candidate * candidate),
            d_hidden * squash * output_gate * (1.0 - output_gate),
        ],
        axis=1,
    ).astype(jnp.bfloat16)
    return (d_gates, d_total * forget)


def column_total(products, col_count, row_shift):
    result = products[:, :, 2 : 2 + col_count, row_shift, 0]
    for col_shift in range(1, 3):
        result = (
            result + products[:, :, 2 - col_shift : 2 - col_shift + col_count, row_shift, col_shift]
        )
    return result


def transpose_products(d_field, weight_matrix, channels):
    products = lax.dot_general(
        d_field, weight_matrix, (((3,), (1,)), ((), ())), preferred_element_type=jnp.float32
    )
    return products.reshape(d_field.shape[:3] + (3, 3, channels))


def per_device(
    syndromes, labels, stab_gate, bit_gate, forget_bias, conv_weight, query, readout_weight
):
    round_count, micro_count, shots_each, tile_rows, columns = syndromes.shape
    shot_count = micro_count * shots_each
    channels = conv_weight.shape[2]
    gate_units = conv_weight.shape[3]
    tile_sites = tile_rows * columns
    flat_rows = shot_count * tile_sites
    weight_matrix = conv_weight.reshape(9 * channels, gate_units)
    stab_rows = stab_gate.reshape(1, tile_sites, gate_units).astype(jnp.float32)
    forget_shift = jnp.concatenate(
        [jnp.zeros((channels,), jnp.float32), forget_bias, jnp.zeros((2 * channels,), jnp.float32)]
    )
    score_scale = 1.0 / math.sqrt(channels)
    field_shape = (shot_count, tile_rows, columns, channels)
    gate_shape = (shot_count, tile_rows, columns, gate_units)
    lead_tile = (lax.axis_index("tiles") == 0).astype(jnp.float32)

    def forward_round(recurrent, fired_bits):
        hidden_prev, cell_prev = recurrent
        hidden_rows = with_halo(hidden_prev, (("tiles", 1),), 1)
        hidden_pad = pad_columns(hidden_rows)
        gate_input = jnp.dot(
            make_patches(hidden_pad), weight_matrix, preferred_element_type=jnp.float32
        )
        gate_input = (
            gate_input.reshape(shot_count, tile_sites, gate_units)
            + stab_rows
            + fired_bits.astype(jnp.float32).reshape(shot_count, tile_sites, 1) * bit_gate
            + forget_shift
        )
        gate_values, cell_new, hidden_new = cell_forward(
            gate_input.reshape(flat_rows, gate_units), cell_prev, channels
        )
        return (
            (hidden_new.reshape(field_shape), cell_new),
            (hidden_pad, gate_values, cell_prev, cell_new, fired_bits),
        )

    def backward_round(state_carry, saved_items):
        d_hidden, d_cell, grad_weight, grad_stab_part, grad_fired, grad_keep = state_carry
        hidden_pad, gate_values, cell_prev, cell_new, fired_bits = saved_items
        d_gates, d_cell_prev = cell_backward(
            gate_values, cell_prev, cell_new, d_hidden, d_cell, channels
        )
        grad_weight = grad_weight + lax.dot_general(
            make_patches(hidden_pad),
            d_gates,
            (((0,), (0,)), ((), ())),
            preferred_element_type=jnp.float32,
        )
        grad_stab_part = grad_stab_part + jnp.sum(
            d_gates.reshape(shot_count, tile_sites, gate_units).astype(jnp.float32), axis=0
        )
        fired_row = fired_bits.astype(jnp.bfloat16).reshape(1, flat_rows)
        grad_fired = grad_fired + jnp.dot(fired_row, d_gates, preferred_element_type=jnp.float32)[0]
        grad_keep = grad_keep + jnp.sum(
            d_gates[:, channels : 2 * channels].astype(jnp.float32), axis=0
        )
        d_field = d_gates.reshape(gate_shape)
        d_rows = with_halo(d_field, (("tiles", 1),), 1)
        products = transpose_products(pad_columns(d_rows), weight_matrix, channels)
        d_hidden_prev = column_total(products[:, 2 : 2 + tile_rows], columns, 0)
        for row_shift in range(1, 3):
            d_hidden_prev = d_hidden_prev + column_total(
                products[:, 2 - row_shift : 2 - row_shift + tile_rows], columns, row_shift
            )
        return (
            (
                d_hidden_prev.reshape(flat_rows, channels),
                d_cell_prev,
                grad_weight,
                grad_stab_part,
                grad_fired,
                grad_keep,
            ),
            None,
        )

    def one_batch(totals, inputs):
        fired_rounds, batch_labels = inputs
        initial = (
            jnp.zeros(field_shape, jnp.bfloat16),
            jnp.zeros((flat_rows, channels), jnp.float32),
        )
        (hidden_last, unused_cell), saved = lax.scan(forward_round, initial, fired_rounds)
        hidden_full = hidden_last.astype(jnp.float32).reshape(shot_count, tile_sites, channels)
        scores = jnp.sum(hidden_full * query, axis=2) * score_scale
        exp_score = jnp.exp(scores)
        part_total = jnp.sum(exp_score, axis=1)
        part_numer = jnp.sum(exp_score[..., None] * hidden_full, axis=1)
        sums = jnp.concatenate(
            [part_numer, jnp.broadcast_to(part_total[:, None], part_numer.shape)], axis=0
        )
        tile_count = lax.axis_size("tiles")
        sums = swap_sum(sums, "tiles", [1])
        for start, size in tile_groups(tile_count):
            sums = swap_sum(sums, "tiles", [start * k for k in range(1, size)])
        numer = sums[:shot_count]
        total_exp = sums[shot_count:, 0]
        pooled = numer / total_exp[:, None]
        logit_value = jnp.sum(pooled * readout_weight, axis=1)
        targets = batch_labels.astype(jnp.float32)
        loss_part = jnp.sum(jax.nn.softplus(logit_value) - targets * logit_value)
        d_logit = jax.nn.sigmoid(logit_value) - targets
        d_pooled = d_logit[:, None] * readout_weight
        weight = exp_score / total_exp[:, None]
        d_score = weight * (
            jnp.sum(hidden_full * d_pooled[:, None, :], axis=2)
            - jnp.sum(pooled * d_pooled, axis=1)[:, None]
        )
        final_grad = (
            weight[..., None] * d_pooled[:, None, :] + d_score[..., None] * query * score_scale
        )
        query_part = score_scale * jnp.sum(d_score[..., None] * hidden_full, axis=(0, 1))
        readout_part = jnp.sum(d_logit[:, None] * pooled, axis=0)
        grad_weight, grad_stab_part, grad_fired, grad_keep, grad_query, grad_readout, loss_total = (
            totals
        )
        start_back = (
            final_grad.reshape(flat_rows, channels),
            jnp.zeros((flat_rows, channels), jnp.float32),
            grad_weight,
            grad_stab_part,
            grad_fired,
            grad_keep,
        )
        back_state, unused_out = lax.scan(backward_round, start_back, saved, reverse=True)
        return (
            (
                back_state[2],
                back_state[3],
                back_state[4],
                back_state[5],
                grad_query + query_part,
                grad_readout + readout_part,
                loss_total + loss_part,
            ),
            None,
        )

    zero_totals = (
        jnp.zeros((9 * channels, gate_units), jnp.float32),
        jnp.zeros((tile_sites, gate_units), jnp.float32),
        jnp.zeros((gate_units,), jnp.float32),
        jnp.zeros((channels,), jnp.float32),
        jnp.zeros((channels,), jnp.float32),
        jnp.zeros((channels,), jnp.float32),
        jnp.zeros((), jnp.float32),
    )
    batch_inputs = (
        syndromes.reshape(round_count, shot_count, tile_rows, columns),
        labels.reshape(shot_count),
    )
    sums, unused_out = one_batch(zero_totals, batch_inputs)
    grad_weight, grad_stab_part, grad_fired, grad_keep, grad_query, grad_readout, loss_total = sums
    loss_row = jnp.where(jnp.arange(channels) == 0, loss_total * lead_tile, 0.0)
    small = jnp.stack(
        list(grad_fired.reshape(-1, channels))
        + [grad_keep, grad_query, grad_readout * lead_tile, loss_row]
    )
    blocks = gate_units // 128
    weight_rows = jnp.swapaxes(grad_weight.reshape(9 * channels, blocks, 128), 0, 1)
    weight_total, small, stab_total = reduce_all(weight_rows.reshape(-1, 128), small, grad_stab_part)
    weight_total = jnp.swapaxes(weight_total.reshape(blocks, 9 * channels, 128), 0, 1)
    return (
        weight_total.astype(jnp.float32).reshape(3, 3, channels, gate_units),
        stab_total.astype(jnp.float32).reshape(tile_rows, columns, gate_units),
        small[:blocks].reshape(gate_units),
        small[blocks],
        small[blocks + 1],
        small[blocks + 2],
        small[blocks + 3, 0],
    )


def solution(mesh):
    in_specs = (
        P(None, None, "rounds", "tiles", None),
        P(None, "rounds"),
        P("tiles", None, None),
        P(),
        P(),
        P(),
        P(),
        P(),
    )
    out_specs = (P(), P("tiles", None, None), P(), P(), P(), P(), P())
    return jax.shard_map(
        per_device, mesh=mesh, in_specs=in_specs, out_specs=out_specs, check_vma=False
    )
```

```python
import functools
import math

import jax
import jax.numpy as jnp
from jax import lax
from jax.experimental import pallas as pl
from jax.experimental.pallas import tpu as pltpu
from jax.sharding import PartitionSpec as P


COLS = 64
CH = 128
UNITS = 512
ROUNDS = 8
OWN = 4
HALO = 8
EXT = OWN + 2 * HALO
CHUNK = 4 * COLS
MID = 12 * COLS
SCALE = 1.0 / math.sqrt(CH)
VMEM = pl.BlockSpec(memory_space=pltpu.VMEM)
SMEM = pl.BlockSpec(memory_space=pltpu.SMEM)
ANY = pl.BlockSpec(memory_space=pl.ANY)


def swap(values, axis, mask):
    count = lax.axis_size(axis)
    return lax.ppermute(values, axis, [(i, i ^ mask) for i in range(count)])


def shift(values, axis, step):
    count = lax.axis_size(axis)
    return lax.ppermute(values, axis, [(i, (i + step) % count) for i in range(count)])


def tree_sum(parts):
    while len(parts) > 1:
        parts = [parts[i] + parts[i + 1] for i in range(0, len(parts), 2)]
    return parts[0]


def tile_groups(count):
    groups = []
    start = 2
    while start < count:
        size = min(4, count // start)
        groups.append((start, size))
        start *= size
    return groups


def split_words(values):
    high = values.astype(jnp.bfloat16)
    low = (values - high.astype(jnp.float32)).astype(jnp.bfloat16)
    return jnp.concatenate([high, low], axis=0)


def gate(values):
    return 0.5 * jnp.tanh(0.5 * values) + 0.5


def rows_inside(meta, first, shape, lattice):
    row = lax.broadcasted_iota(jnp.int32, shape, 0) // COLS + (OWN * meta[0] - HALO + first)
    return jnp.logical_and(row >= 0, row < lattice)


def column_of(shape):
    return lax.broadcasted_iota(jnp.int32, shape, 0) % COLS


def forward_kernel(
    lattice, meta, a_ref, b_ref, w_ref, bit_ref, forget_ref, q_ref,
    gates_out, hist_out, stats_out, bits_out,
    stab, raw, bits, hc, cell, stage, in_sem, gate_sem, hist_sem,
):
    core = meta[1]
    copies = []
    for k in range(5):
        for side, ref in ((core, a_ref), (1 - core, b_ref)):
            n = len(copies)
            copies.append(
                pltpu.make_async_copy(
                    ref.at[k, pl.ds(0, 2 * COLS)],
                    stab.at[pl.ds(pl.multiple_of(k * CHUNK + side * 2 * COLS, 2 * COLS), 2 * COLS)],
                    in_sem.at[n],
                )
            )
            copies.append(
                pltpu.make_async_copy(
                    ref.at[k, pl.ds(2 * COLS, 16)], raw.at[2 * k + side], in_sem.at[n + 1]
                )
            )
    for copy in copies:
        copy.start()
    edge = jnp.zeros((COLS, 3 * CH), jnp.bfloat16)
    for slot in range(2):
        hc[slot, pl.ds(0, COLS)] = edge
        hc[slot, pl.ds((EXT + 1) * COLS, COLS)] = edge
    cell[...] = jnp.zeros_like(cell)
    for copy in copies:
        copy.wait()
    for i in range(10):
        words = raw[i].astype(jnp.float32)
        bits[i] = jnp.where(core == 0, words[0:8, 0:CH], words[8:16, 0:CH])
    for i in range(2):
        bits_out[i] = bits[HALO // 2 + i]

    def gate_copy(t):
        return pltpu.make_async_copy(
            stage.at[t % 2, pl.ds(4 * COLS, MID)], gates_out.at[t], gate_sem.at[t % 2]
        )

    def hist_copy(t):
        return pltpu.make_async_copy(
            hc.at[t % 2, pl.ds(8 * COLS, 6 * COLS)], hist_out.at[t], hist_sem.at[t % 2]
        )

    def run_round(t, first):
        low = 0 if first else (t // 2) * 2
        count = 5 if first else 5 - t // 2
        now = 0 if first else t % 2
        pick = lax.broadcasted_iota(jnp.int32, (8, CH), 0) == t

        def chunk(i, carry):
            row = low + 4 * i
            at = pl.multiple_of(row * COLS, 2 * COLS)
            pre = stab[pl.ds(at, CHUNK)].astype(jnp.float32)
            if not first:
                for a in range(3):
                    pre = pre + jnp.dot(
                        hc[1 - now, pl.ds(pl.multiple_of((row + a) * COLS, COLS), CHUNK)],
                        w_ref[pl.ds(a * 3 * CH, 3 * CH)],
                        preferred_element_type=jnp.float32,
                    )
            one = pick.astype(jnp.float32)
            fired = jnp.concatenate(
                [
                    lax.dot_general(
                        bits[row // 2 + p], one, (((0,), (0,)), ((), ())),
                        preferred_element_type=jnp.float32,
                    )
                    for p in range(2)
                ],
                axis=0,
            )
            g_in = gate(pre[:, 0:CH] + fired * bit_ref[:, 0:CH])
            g_keep = gate(pre[:, CH : 2 * CH] + fired * bit_ref[:, CH : 2 * CH] + forget_ref[...])
            g_new = jnp.tanh(pre[:, 2 * CH : 3 * CH] + fired * bit_ref[:, 2 * CH : 3 * CH])
            g_out = gate(pre[:, 3 * CH :] + fired * bit_ref[:, 3 * CH :])
            c_new = g_keep * cell[pl.ds(at, CHUNK)] + g_in * g_new
            cell[pl.ds(at, CHUNK)] = c_new
            stage[now, pl.ds(at, CHUNK), 0:CH] = g_in
            stage[now, pl.ds(at, CHUNK), CH : 2 * CH] = g_keep
            stage[now, pl.ds(at, CHUNK), 2 * CH : 3 * CH] = g_new
            stage[now, pl.ds(at, CHUNK), 3 * CH : 4 * CH] = g_out
            stage[now, pl.ds(at, CHUNK), 4 * CH :] = c_new
            shape = (CHUNK, CH)
            hidden = jnp.where(
                rows_inside(meta, row, shape, lattice), g_out * jnp.tanh(c_new), 0.0
            )
            col = column_of(shape)
            left = jnp.where(col == 0, 0.0, pltpu.roll(hidden, 1, 0))
            right = jnp.where(col == COLS - 1, 0.0, pltpu.roll(hidden, CHUNK - 1, 0))
            to = pl.multiple_of((row + 1) * COLS, COLS)
            hc[now, pl.ds(to, CHUNK), 0:CH] = left.astype(jnp.bfloat16)
            hc[now, pl.ds(to, CHUNK), CH : 2 * CH] = hidden.astype(jnp.bfloat16)
            hc[now, pl.ds(to, CHUNK), 2 * CH :] = right.astype(jnp.bfloat16)
            return carry

        lax.fori_loop(0, count, chunk, 0)
        gate_copy(t).start()
        hist_copy(t).start()

    run_round(0, True)

    def later(t, carry):
        @pl.when(t >= 2)
        def _():
            gate_copy(t - 2).wait()
            hist_copy(t - 2).wait()

        run_round(t, False)
        return carry

    lax.fori_loop(1, ROUNDS, later, 0)
    hidden = hc[1, pl.ds((HALO + 1) * COLS, CHUNK), CH : 2 * CH].astype(jnp.float32)
    weight = jnp.exp(jnp.sum(hidden * q_ref[...], axis=1, keepdims=True) * SCALE)
    stats_out[...] = jnp.zeros_like(stats_out)
    stats_out[0:1, :] = jnp.sum(weight * hidden, axis=0, keepdims=True)
    stats_out[1:2, :] = jnp.broadcast_to(jnp.sum(weight, axis=0, keepdims=True), (1, CH))
    for t in (ROUNDS - 2, ROUNDS - 1):
        gate_copy(t).wait()
        hist_copy(t).wait()


def backward_rounds(
    lattice, meta, rounds, w_ref, gates, gates_ref, sems, d_hid, d_cell, d_pre, dp_out, ready=0
):
    last = rounds[-1]
    for slot, t in list(enumerate(rounds))[ready:]:
        pltpu.make_async_copy(gates_ref.at[t], gates.at[slot], sems.at[slot]).wait()
    if last > 0:
        pltpu.make_async_copy(
            gates_ref.at[last - 1, :, pl.ds(4 * CH, CH)],
            gates.at[len(rounds), :, pl.ds(4 * CH, CH)],
            sems.at[len(rounds)],
        ).wait()
    edge = jnp.zeros((COLS, UNITS), jnp.bfloat16)
    d_pre[pl.ds(0, COLS)] = edge
    d_pre[pl.ds(13 * COLS, COLS)] = edge
    for slot, t in enumerate(rounds):

        def adjoint(i, carry, slot=slot, t=t):
            at = pl.ds(pl.multiple_of(i * CHUNK, CHUNK), CHUNK)
            g_in = gates[slot, at, 0:CH]
            g_keep = gates[slot, at, CH : 2 * CH]
            g_new = gates[slot, at, 2 * CH : 3 * CH]
            g_out = gates[slot, at, 3 * CH : 4 * CH]
            squash = jnp.tanh(gates[slot, at, 4 * CH :])
            dh = d_hid[at]
            total = d_cell[at] + dh * g_out * (1.0 - squash * squash)
            d_cell[at] = total * g_keep
            to = pl.ds(pl.multiple_of(i * CHUNK + COLS, COLS), CHUNK)
            d_pre[to, 0:CH] = (total * g_new * g_in * (1.0 - g_in)).astype(jnp.bfloat16)
            if t > 0:
                c_old = gates[slot + 1, at, 4 * CH :]
                keep = (total * c_old * g_keep * (1.0 - g_keep)).astype(jnp.bfloat16)
            else:
                keep = jnp.zeros((CHUNK, CH), jnp.bfloat16)
            d_pre[to, CH : 2 * CH] = keep
            d_pre[to, 2 * CH : 3 * CH] = (total * g_in * (1.0 - g_new * g_new)).astype(jnp.bfloat16)
            d_pre[to, 3 * CH :] = (dh * squash * g_out * (1.0 - g_out)).astype(jnp.bfloat16)
            return carry

        def spread(i, carry):
            total = None
            for a in range(3):
                part = lax.dot_general(
                    d_pre[pl.ds(pl.multiple_of(i * CHUNK + (2 - a) * COLS, COLS), CHUNK)],
                    w_ref[pl.ds(a * 3 * CH, 3 * CH)],
                    (((1,), (1,)), ((), ())),
                    preferred_element_type=jnp.float32,
                )
                total = part if total is None else total + part
            shape = (CHUNK, CH)
            col = column_of(shape)
            ahead = jnp.where(col == COLS - 1, 0.0, pltpu.roll(total[:, 0:CH], CHUNK - 1, 0))
            behind = jnp.where(col == 0, 0.0, pltpu.roll(total[:, 2 * CH :], 1, 0))
            dh = total[:, CH : 2 * CH] + ahead + behind
            inside = rows_inside(meta, 4 + 4 * i, shape, lattice)
            d_hid[pl.ds(pl.multiple_of(i * CHUNK, CHUNK), CHUNK)] = jnp.where(inside, dh, 0.0)
            return carry

        if t == 0:
            adjoint(1, 0)
        else:
            lax.fori_loop(0, 3, adjoint, 0)
        dp_out[slot] = d_pre[pl.ds(CHUNK + COLS, CHUNK)]
        if t > 0:
            if t == last or t == 1:
                spread(1, 0)
            else:
                lax.fori_loop(0, 3, spread, 0)


def start_gates(rounds, gates, gates_ref, sems):
    last = rounds[-1]
    for slot, t in enumerate(rounds):
        pltpu.make_async_copy(gates_ref.at[t], gates.at[slot], sems.at[slot]).start()
    if last > 0:
        pltpu.make_async_copy(
            gates_ref.at[last - 1, :, pl.ds(4 * CH, CH)],
            gates.at[len(rounds), :, pl.ds(4 * CH, CH)],
            sems.at[len(rounds)],
        ).start()


def first_backward(
    lattice, rounds, parts, meta, label_ref, *refs
):
    stat_refs = refs[:parts]
    (q_ref, r_ref, w_ref, gates_ref, hid_out, cell_out, edge_out, dp_out, small_out,
     gates, d_hid, d_cell, d_pre, sems) = refs[parts:]
    start_gates(rounds, gates, gates_ref, sems)
    sums = tree_sum([ref[...] for ref in stat_refs])
    total = sums[1:2, :]
    pooled = sums[0:1, :] / total
    read = r_ref[...]
    query = q_ref[...]
    logit = jnp.sum(pooled * read, axis=1, keepdims=True)
    label = label_ref[...]
    loss = jnp.maximum(logit, 0.0) + jnp.log1p(jnp.exp(-jnp.abs(logit))) - label * logit
    d_logit = 1.0 / (1.0 + jnp.exp(-logit)) - label
    d_pooled = d_logit * read
    spare = jnp.sum(pooled * d_pooled, axis=1, keepdims=True)
    pltpu.make_async_copy(gates_ref.at[rounds[0]], gates.at[0], sems.at[0]).wait()
    lead = meta[0] == 0
    small_out[...] = jnp.zeros_like(small_out)
    for i in range(3):
        at = pl.ds(i * CHUNK, CHUNK)
        hidden = gates[0, at, 3 * CH : 4 * CH] * jnp.tanh(gates[0, at, 4 * CH :])
        hidden = hidden.astype(jnp.bfloat16).astype(jnp.float32)
        weight = jnp.exp(jnp.sum(hidden * query, axis=1, keepdims=True) * SCALE) / total[:, 0:1]
        d_score = weight * (jnp.sum(hidden * d_pooled, axis=1, keepdims=True) - spare)
        grad = weight * d_pooled + d_score * (query * SCALE)
        inside = rows_inside(meta, 4 + 4 * i, (CHUNK, CH), lattice)
        d_hid[at] = jnp.where(inside, grad, 0.0)
        if i == 1:
            small_out[5:6, :] = SCALE * jnp.sum(d_score * hidden, axis=0, keepdims=True)
    d_cell[...] = jnp.zeros_like(d_cell)
    lane = lax.broadcasted_iota(jnp.int32, (1, CH), 1)
    small_out[6:7, :] = jnp.where(lead, d_logit * pooled, 0.0)
    small_out[7:8, :] = jnp.where(jnp.logical_and(lead, lane == 0), loss, 0.0)
    backward_rounds(
        lattice, meta, rounds, w_ref, gates, gates_ref, sems, d_hid, d_cell, d_pre, dp_out, ready=1
    )
    own = pl.ds(CHUNK, CHUNK)
    hid_out[...] = d_hid[own]
    cell_out[...] = d_cell[own]
    edge_out[:, 0:CH] = d_hid[own].astype(jnp.bfloat16)
    edge_out[:, CH:] = d_cell[own].astype(jnp.bfloat16)


def load_adjoint(meta, lattice, rows, below, above, hid_in, cell_in, d_hid, d_cell):
    size = rows * COLS
    blank = jnp.zeros((CHUNK, CH), jnp.float32)
    if rows < 4:
        for i in (0, 2):
            d_hid[pl.ds(i * CHUNK, CHUNK)] = blank
            d_cell[pl.ds(i * CHUNK, CHUNK)] = blank
    for first, ref in ((CHUNK - size, below), (2 * CHUNK, above)):
        inside = rows_inside(meta, 4 + first // COLS, (size, CH), lattice)
        d_hid[pl.ds(first, size)] = jnp.where(inside, ref[:, 0:CH].astype(jnp.float32), 0.0)
        d_cell[pl.ds(first, size)] = jnp.where(inside, ref[:, CH:].astype(jnp.float32), 0.0)
    d_hid[pl.ds(CHUNK, CHUNK)] = hid_in[...]
    d_cell[pl.ds(CHUNK, CHUNK)] = cell_in[...]


def middle_backward(
    lattice, rounds, rows, meta, below, above, hid_in, cell_in, w_ref, gates_ref,
    hid_out, cell_out, edge_out, dp_out, gates, d_hid, d_cell, d_pre, sems,
):
    start_gates(rounds, gates, gates_ref, sems)
    load_adjoint(meta, lattice, rows, below, above, hid_in, cell_in, d_hid, d_cell)
    backward_rounds(lattice, meta, rounds, w_ref, gates, gates_ref, sems, d_hid, d_cell, d_pre, dp_out)
    own = pl.ds(CHUNK, CHUNK)
    hid_out[...] = d_hid[own]
    cell_out[...] = d_cell[own]
    edge_out[:, 0:CH] = d_hid[own].astype(jnp.bfloat16)
    edge_out[:, CH:] = d_cell[own].astype(jnp.bfloat16)


def last_backward(
    lattice, rounds, rows, meta, below, above, hid_in, cell_in, w_ref, dp_one, dp_two, small_in,
    gates_ref, dp_out, mine_out, other_out, small_out, gates, d_hid, d_cell, d_pre, total, sems,
):
    start_gates(rounds, gates, gates_ref, sems)
    load_adjoint(meta, lattice, rows, below, above, hid_in, cell_in, d_hid, d_cell)
    backward_rounds(lattice, meta, rounds, w_ref, gates, gates_ref, sems, d_hid, d_cell, d_pre, dp_out)
    summed = None
    for ref, count in ((dp_one, 1), (dp_two, 2), (dp_out, len(rounds))):
        for i in range(count):
            part = ref[i].astype(jnp.float32)
            summed = part if summed is None else summed + part
    total[...] = summed
    core = meta[1]
    half = 2 * COLS
    mine_out[...] = total[pl.ds(pl.multiple_of(core * half, half), half)]
    other_out[...] = total[pl.ds(pl.multiple_of((1 - core) * half, half), half)].astype(jnp.bfloat16)
    small_out[...] = small_in[...]
    small_out[4:5, :] = jnp.sum(total[:, CH : 2 * CH], axis=0, keepdims=True)


def weight_kernel(
    pieces, bits_ref, small_ref, dp_one, dp_two, dp_three, hist_ref, out_ref,
    dp, grad, fired_sum, dp_sem,
):
    copies = []
    for ref, low in ((dp_one, 7), (dp_two, 6), (dp_three, 4)):
        for i in range(ref.shape[0]):
            copies.append(pltpu.make_async_copy(ref.at[i], dp.at[low - i], dp_sem.at[low - i]))
    for copy in copies:
        copy.start()
    grad[...] = jnp.zeros_like(grad)
    for copy in copies:
        copy.wait()
    word = jnp.concatenate([bits_ref[0], bits_ref[1]], axis=1)

    def add_fired(t):
        rows = jnp.where(lax.broadcasted_iota(jnp.int32, word.shape, 0) == t, word, 0.0)
        return jnp.dot(rows.astype(jnp.bfloat16), dp[t], preferred_element_type=jnp.float32)

    fired_sum[...] = add_fired(0)

    def add_round(t, carry):
        fired_sum[...] += add_fired(t)
        for a in range(3):
            grad[pl.ds(a * 3 * CH, 3 * CH)] += lax.dot_general(
                hist_ref[t - 1, pl.ds(a * COLS, CHUNK)],
                dp[t],
                (((0,), (0,)), ((), ())),
                preferred_element_type=jnp.float32,
            )
        return carry

    lax.fori_loop(1, ROUNDS, add_round, 0)
    fired = jnp.sum(fired_sum[...], axis=0, keepdims=True)
    rows = [fired[:, g * CH : (g + 1) * CH] for g in range(4)]
    small = jnp.concatenate(rows + [small_ref[4:8, :]], axis=0)
    words = split_words(small)
    per = pieces // 4
    size = 9 * CH // per
    for n in range(pieces):
        g, m = n // per, n % per
        out_ref[n, 0:size, :] = grad[pl.ds(m * size, size), g * CH : (g + 1) * CH].astype(jnp.bfloat16)
        out_ref[n, size:, :] = words


def final_kernel(pieces, planes, conv_ref, stab_ref, conv_out, stab_out):
    per = pieces // 4
    size = 9 * CH // per
    for n in range(pieces):
        g, m = n // per, n % per
        conv_out[pl.ds(m * size, size), g * CH : (g + 1) * CH] = conv_ref[n].astype(jnp.float32)
    rows = 2 * COLS // planes
    for z in range(planes):
        for g in range(4):
            stab_out[pl.ds(z * rows, rows), g * CH : (g + 1) * CH] = stab_ref[
                z, pl.ds(g * rows, rows)
            ].astype(jnp.float32)


def f32(*shape):
    return jax.ShapeDtypeStruct(shape, jnp.float32)


def b16(*shape):
    return jax.ShapeDtypeStruct(shape, jnp.bfloat16)


def call(kernel, in_specs, out_shape, out_specs, scratch, flops):
    return pl.pallas_call(
        kernel,
        in_specs=in_specs,
        out_shape=out_shape,
        out_specs=out_specs,
        scratch_shapes=scratch,
        cost_estimate=pl.CostEstimate(flops=flops, bytes_accessed=4_000_000, transcendentals=0),
        compiler_params=pltpu.CompilerParams(vmem_limit_bytes=48 * 1024 * 1024),
    )


def segment_scratch(count, extra):
    return [
        pltpu.VMEM((count, MID, 5 * CH), jnp.float32),
        pltpu.VMEM((MID, CH), jnp.float32),
        pltpu.VMEM((MID, CH), jnp.float32),
        pltpu.VMEM((14 * COLS, UNITS), jnp.bfloat16),
        *extra,
        pltpu.SemaphoreType.DMA((count + 1,)),
    ]


def per_device(
    syndromes, labels, stab_gate, bit_gate, forget_bias, conv_weight, query, readout_weight
):
    tiles = lax.axis_size("tiles")
    planes = lax.axis_size("rounds")
    tile = lax.axis_index("tiles")
    core = tile & 1
    lattice = 2 * tiles
    meta = jnp.stack([tile // 2, core]).astype(jnp.int32)
    weights = conv_weight.reshape(9 * CH, UNITS)
    bit_row = bit_gate.reshape(1, UNITS)
    forget_row = forget_bias.reshape(1, CH)
    query_row = query.reshape(1, CH)
    read_row = readout_weight.reshape(1, CH)

    words = jnp.swapaxes(syndromes[:, :, 0], 0, 1).astype(jnp.bfloat16).reshape(16, 2 * COLS)
    words = jnp.pad(words, ((0, 0), (0, UNITS - 2 * COLS)))
    own = jnp.concatenate([stab_gate.reshape(2 * COLS, UNITS), words], axis=0)
    near = [shift(own, "tiles", step) for step in (4, 2)]
    far = [shift(own, "tiles", step) for step in (-2, -4)]
    mine = jnp.stack(near + [own] + far)
    theirs = swap(mine, "tiles", 1)

    gates, hist, stats, bits = call(
        functools.partial(forward_kernel, lattice),
        [SMEM, ANY, ANY, VMEM, VMEM, VMEM, VMEM],
        (f32(ROUNDS, MID, 5 * CH), b16(ROUNDS, 6 * COLS, 3 * CH), f32(8, CH), f32(2, 8, CH)),
        (ANY, ANY, VMEM, VMEM),
        [
            pltpu.VMEM((EXT * COLS, UNITS), jnp.bfloat16),
            pltpu.VMEM((10, 16, UNITS), jnp.bfloat16),
            pltpu.VMEM((10, 8, CH), jnp.float32),
            pltpu.VMEM((2, (EXT + 2) * COLS, 3 * CH), jnp.bfloat16),
            pltpu.VMEM((EXT * COLS, CH), jnp.float32),
            pltpu.VMEM((2, EXT * COLS, 5 * CH), jnp.float32),
            pltpu.SemaphoreType.DMA((20,)),
            pltpu.SemaphoreType.DMA((2,)),
            pltpu.SemaphoreType.DMA((2,)),
        ],
        8_000_000_000,
    )(meta, mine, theirs, weights, bit_row, forget_row, query_row)

    parts = [stats]
    for start, size in tile_groups(tiles):
        stats = tree_sum(parts)
        parts = [stats] + [swap(stats, "tiles", start * k) for k in range(1, size)]

    label = jnp.where(core == 0, labels[0], labels[1]).astype(jnp.float32).reshape(1, 1)
    first = [7]
    d_hid, d_cell, edge, dp_one, small = call(
        functools.partial(first_backward, lattice, first, len(parts)),
        [SMEM, VMEM] + [VMEM] * len(parts) + [VMEM, VMEM, VMEM, ANY],
        (f32(CHUNK, CH), f32(CHUNK, CH), b16(CHUNK, 2 * CH), b16(1, CHUNK, UNITS), f32(8, CH)),
        (VMEM,) * 5,
        segment_scratch(2, []),
        1_000_000_000,
    )(meta, label, *parts, query_row, read_row, weights, gates)

    half = 2 * COLS
    below = shift(edge[half:], "tiles", 2)
    above = shift(edge[:half], "tiles", -2)
    middle = [6, 5]
    d_hid, d_cell, edge, dp_two = call(
        functools.partial(middle_backward, lattice, middle, 2),
        [SMEM] + [VMEM] * 5 + [ANY],
        (f32(CHUNK, CH), f32(CHUNK, CH), b16(CHUNK, 2 * CH), b16(2, CHUNK, UNITS)),
        (VMEM,) * 4,
        segment_scratch(3, []),
        2_000_000_000,
    )(meta, below, above, d_hid, d_cell, weights, gates)

    below = shift(edge, "tiles", 2)
    above = shift(edge, "tiles", -2)
    last = [4, 3, 2, 1, 0]
    dp_three, stab_mine, stab_other, small = call(
        functools.partial(last_backward, lattice, last, 4),
        [SMEM] + [VMEM] * 8 + [ANY],
        (b16(5, CHUNK, UNITS), f32(half, UNITS), b16(half, UNITS), f32(8, CH)),
        (VMEM,) * 4,
        segment_scratch(5, [pltpu.VMEM((CHUNK, UNITS), jnp.float32)]),
        4_000_000_000,
    )(meta, below, above, d_hid, d_cell, weights, dp_one, dp_two, small, gates)

    message = call(
        functools.partial(weight_kernel, tiles),
        [VMEM, VMEM, ANY, ANY, ANY, VMEM],
        b16(tiles, 36 * CH // tiles + 16, CH),
        VMEM,
        [
            pltpu.VMEM((ROUNDS, CHUNK, UNITS), jnp.bfloat16),
            pltpu.VMEM((9 * CH, UNITS), jnp.float32),
            pltpu.VMEM((8, UNITS), jnp.float32),
            pltpu.SemaphoreType.DMA((ROUNDS,)),
        ],
        3_000_000_000,
    )(bits, small, dp_one, dp_two, dp_three, hist)

    stab = stab_mine + swap(stab_other, "tiles", 1).astype(jnp.float32)
    rows = half // planes
    stab = jnp.swapaxes(stab.astype(jnp.bfloat16).reshape(planes, rows, 4, CH), 1, 2)
    stab = lax.all_to_all(stab.reshape(planes, 4 * rows, CH), "rounds", 0, 0, tiled=True)
    stab = jnp.sum(stab.astype(jnp.float32), axis=0).astype(jnp.bfloat16)

    size = 36 * CH // tiles
    back = lax.all_to_all(message, "tiles", 0, 0, tiled=True).astype(jnp.float32)
    piece = jnp.sum(back[:, :size], axis=0)
    small = jnp.sum(back[:, size : size + 8] + back[:, size + 8 :], axis=0)
    joint = jnp.concatenate([piece.astype(jnp.bfloat16), split_words(small), stab], axis=0)
    joint = jnp.broadcast_to(joint[None], (planes,) + joint.shape)
    joint = lax.all_to_all(joint, "rounds", 0, 0, tiled=True)
    sums = joint[:, : size + 16].astype(jnp.float32)
    piece = jnp.sum(sums[:, :size], axis=0).astype(jnp.bfloat16)
    small = jnp.sum(sums[:, size : size + 8] + sums[:, size + 8 :], axis=0)
    stab_all = joint[:, size + 16 :]
    conv_all = lax.all_to_all(
        jnp.broadcast_to(piece[None], (tiles, size, CH)), "tiles", 0, 0, tiled=True
    )
    grad_conv, grad_stab = call(
        functools.partial(final_kernel, tiles, planes),
        [VMEM, VMEM],
        (f32(9 * CH, UNITS), f32(half, UNITS)),
        (VMEM, VMEM),
        [],
        1_000_000,
    )(conv_all, stab_all)
    return (
        grad_conv.reshape(3, 3, CH, UNITS),
        grad_stab.reshape(2, COLS, UNITS),
        small[:4].reshape(UNITS),
        small[4],
        small[5],
        small[6],
        small[7, 0],
    )


def solution(mesh):
    in_specs = (
        P(None, None, "rounds", "tiles", None),
        P(None, "rounds"),
        P("tiles", None, None),
        P(),
        P(),
        P(),
        P(),
        P(),
    )
    out_specs = (P(), P("tiles", None, None), P(), P(), P(), P(), P())
    return jax.shard_map(
        per_device, mesh=mesh, in_specs=in_specs, out_specs=out_specs, check_vma=False
    )
```

```python
import functools
import math

import jax
import jax.numpy as jnp
from jax import lax
from jax.experimental import pallas as pl
from jax.experimental.pallas import tpu as pltpu
from jax.sharding import PartitionSpec as P


COLS = 64
CH = 128
UNITS = 512
ROUNDS = 8
OWN = 4
HALO = 8
EXT = OWN + 2 * HALO
CHUNK = 4 * COLS
MID = 12 * COLS
SCALE = 1.0 / math.sqrt(CH)
VMEM = pl.BlockSpec(memory_space=pltpu.VMEM)
SMEM = pl.BlockSpec(memory_space=pltpu.SMEM)
ANY = pl.BlockSpec(memory_space=pl.ANY)


def swap(values, axis, mask):
    count = lax.axis_size(axis)
    return lax.ppermute(values, axis, [(i, i ^ mask) for i in range(count)])


def shift(values, axis, step):
    count = lax.axis_size(axis)
    return lax.ppermute(values, axis, [(i, (i + step) % count) for i in range(count)])


def tree_sum(parts):
    while len(parts) > 1:
        parts = [parts[i] + parts[i + 1] for i in range(0, len(parts), 2)]
    return parts[0]


def tile_groups(count):
    groups = []
    start = 2
    while start < count:
        size = min(4, count // start)
        groups.append((start, size))
        start *= size
    return groups


def split_words(values):
    high = values.astype(jnp.bfloat16)
    low = (values - high.astype(jnp.float32)).astype(jnp.bfloat16)
    return jnp.concatenate([high, low], axis=0)


def gate(values):
    return 0.5 * jnp.tanh(0.5 * values) + 0.5


def rows_inside(meta, first, shape, lattice):
    site = lax.broadcasted_iota(jnp.int32, shape, 0)
    low = (HALO - OWN * meta[0] - first) * COLS
    return jnp.logical_and(site >= low, site < low + lattice * COLS)


def column_of(shape):
    return lax.broadcasted_iota(jnp.int32, shape, 0) & (COLS - 1)


def forward_kernel(
    lattice, meta, a_ref, b_ref, w_ref, bit_ref, forget_ref, q_ref,
    gates_out, hist_out, stats_out, bits_out,
    stab, raw, bits, fired, w_all, hc, cell, stage, in_sem, gate_sem, hist_sem,
):
    core = meta[1]
    copies = []
    for k in range(5):
        for side, ref in ((core, a_ref), (1 - core, b_ref)):
            n = len(copies)
            copies.append(
                pltpu.make_async_copy(
                    ref.at[k, pl.ds(0, 2 * COLS)],
                    stab.at[pl.ds(pl.multiple_of(k * CHUNK + side * 2 * COLS, 2 * COLS), 2 * COLS)],
                    in_sem.at[n],
                )
            )
            copies.append(
                pltpu.make_async_copy(
                    ref.at[k, pl.ds(2 * COLS, 16)], raw.at[2 * k + side], in_sem.at[n + 1]
                )
            )
    for copy in copies:
        copy.start()
    edge = jnp.zeros((COLS, 3 * CH), jnp.bfloat16)
    for slot in range(2):
        hc[slot, pl.ds(0, COLS)] = edge
        hc[slot, pl.ds((EXT + 1) * COLS, COLS)] = edge
    cell[...] = jnp.zeros_like(cell)
    for copy in copies:
        copy.wait()
    for i in range(10):
        words = raw[i].astype(jnp.float32)
        bits[i] = jnp.where(core == 0, words[0:8, 0:CH], words[8:16, 0:CH])
    for i in range(2):
        bits_out[i] = bits[HALO // 2 + i]
    lane = lax.broadcasted_iota(jnp.int32, (8, CH), 1)
    spread = jnp.logical_and((lane & 7) == lax.broadcasted_iota(jnp.int32, (8, CH), 0), lane < 24)
    spread = spread.astype(jnp.float32)
    ones = jnp.logical_and(lane[0:1] >= 24, lane[0:1] < 27).astype(jnp.float32)
    for i in range(10):
        columns = lax.dot_general(
            bits[i], spread, (((0,), (0,)), ((), ())), preferred_element_type=jnp.float32
        )
        fired[pl.ds(i * CH, CH)] = (columns + ones).astype(jnp.bfloat16)
    w_all[pl.ds(0, 9 * CH)] = w_ref[...]
    rest_bit = bit_ref[...]
    rest_keep = jnp.concatenate(
        [jnp.zeros((1, CH), jnp.float32), forget_ref[...], jnp.zeros((1, 2 * CH), jnp.float32)],
        axis=1,
    )
    sink = []
    for w in range(3):
        word = rest_bit.astype(jnp.bfloat16).astype(jnp.float32)
        rest_bit = rest_bit - word
        sink.append(jnp.broadcast_to(word, (8, UNITS)))
    place = lax.broadcasted_iota(jnp.int32, (8, UNITS), 0)
    last = jnp.zeros((8, UNITS), jnp.float32)
    for w in range(3):
        word = rest_keep.astype(jnp.bfloat16).astype(jnp.float32)
        rest_keep = rest_keep - word
        last = jnp.where(place == w, word, last)
    sink.append(last)
    sink.append(jnp.zeros((CH - 32, UNITS), jnp.float32))
    w_all[pl.ds(9 * CH, CH)] = jnp.concatenate(sink, axis=0).astype(jnp.bfloat16)

    def gate_copy(t):
        return pltpu.make_async_copy(
            stage.at[t % 2, pl.ds(4 * COLS, MID)], gates_out.at[t], gate_sem.at[t % 2]
        )

    def hist_copy(t):
        return pltpu.make_async_copy(
            hc.at[t % 2, pl.ds(8 * COLS, 6 * COLS)], hist_out.at[t], hist_sem.at[t % 2]
        )

    def run_round(t, first):
        low = 0 if first else (t // 2) * 2
        count = 5 if first else 5 - t // 2
        now = 0 if first else t % 2
        lane = lax.broadcasted_iota(jnp.int32, (1, CH), 1)
        wanted = jnp.logical_or((lane & 7) == t, lane >= 24).astype(jnp.bfloat16)

        def chunk(i, carry):
            row = low + 4 * i
            at = pl.multiple_of(row * COLS, 2 * COLS)
            pre = stab[pl.ds(at, CHUNK)].astype(jnp.float32)
            extra = fired[pl.ds(at, CHUNK)] * wanted
            if not first:
                taps = jnp.concatenate(
                    [
                        hc[1 - now, pl.ds(pl.multiple_of((row + a) * COLS, COLS), CHUNK)]
                        for a in range(3)
                    ]
                    + [extra],
                    axis=1,
                )
                pre = pre + jnp.dot(taps, w_all[...], preferred_element_type=jnp.float32)
            else:
                pre = pre + jnp.dot(
                    extra, w_all[pl.ds(9 * CH, CH)], preferred_element_type=jnp.float32
                )
            g_in = gate(pre[:, 0:CH])
            g_keep = gate(pre[:, CH : 2 * CH])
            g_new = jnp.tanh(pre[:, 2 * CH : 3 * CH])
            g_out = gate(pre[:, 3 * CH :])
            c_new = g_keep * cell[pl.ds(at, CHUNK)] + g_in * g_new
            cell[pl.ds(at, CHUNK)] = c_new
            stage[now, pl.ds(at, CHUNK), 0:CH] = g_in
            stage[now, pl.ds(at, CHUNK), CH : 2 * CH] = g_keep
            stage[now, pl.ds(at, CHUNK), 2 * CH : 3 * CH] = g_new
            stage[now, pl.ds(at, CHUNK), 3 * CH : 4 * CH] = g_out
            stage[now, pl.ds(at, CHUNK), 4 * CH :] = c_new
            shape = (CHUNK, CH)
            hidden = jnp.where(
                rows_inside(meta, row, shape, lattice), g_out * jnp.tanh(c_new), 0.0
            )
            col = column_of(shape)
            left = jnp.where(col == 0, 0.0, pltpu.roll(hidden, 1, 0))
            right = jnp.where(col == COLS - 1, 0.0, pltpu.roll(hidden, CHUNK - 1, 0))
            to = pl.multiple_of((row + 1) * COLS, COLS)
            hc[now, pl.ds(to, CHUNK), 0:CH] = left.astype(jnp.bfloat16)
            hc[now, pl.ds(to, CHUNK), CH : 2 * CH] = hidden.astype(jnp.bfloat16)
            hc[now, pl.ds(to, CHUNK), 2 * CH :] = right.astype(jnp.bfloat16)
            return carry

        lax.fori_loop(0, count, chunk, 0)
        gate_copy(t).start()
        hist_copy(t).start()

    run_round(0, True)

    def later(t, carry):
        @pl.when(t >= 2)
        def _():
            gate_copy(t - 2).wait()
            hist_copy(t - 2).wait()

        run_round(t, False)
        return carry

    lax.fori_loop(1, ROUNDS, later, 0)
    hidden = hc[1, pl.ds((HALO + 1) * COLS, CHUNK), CH : 2 * CH].astype(jnp.float32)
    weight = jnp.exp(jnp.sum(hidden * q_ref[...], axis=1, keepdims=True) * SCALE)
    stats_out[...] = jnp.zeros_like(stats_out)
    stats_out[0:1, :] = jnp.sum(weight * hidden, axis=0, keepdims=True)
    stats_out[1:2, :] = jnp.broadcast_to(jnp.sum(weight, axis=0, keepdims=True), (1, CH))
    for t in (ROUNDS - 2, ROUNDS - 1):
        gate_copy(t).wait()
        hist_copy(t).wait()


def backward_rounds(
    lattice, meta, rounds, w_ref, gates, gates_ref, sems, d_hid, d_cell, d_pre, dp_out, ready=0
):
    last = rounds[-1]
    for slot, t in list(enumerate(rounds))[ready:]:
        pltpu.make_async_copy(gates_ref.at[t], gates.at[slot], sems.at[slot]).wait()
    if last > 0:
        pltpu.make_async_copy(
            gates_ref.at[last - 1, :, pl.ds(4 * CH, CH)],
            gates.at[len(rounds), :, pl.ds(4 * CH, CH)],
            sems.at[len(rounds)],
        ).wait()
    edge = jnp.zeros((COLS, UNITS), jnp.bfloat16)
    d_pre[pl.ds(0, COLS)] = edge
    d_pre[pl.ds(13 * COLS, COLS)] = edge
    for slot, t in enumerate(rounds):

        def adjoint(i, carry, slot=slot, t=t):
            at = pl.ds(pl.multiple_of(i * CHUNK, CHUNK), CHUNK)
            g_in = gates[slot, at, 0:CH]
            g_keep = gates[slot, at, CH : 2 * CH]
            g_new = gates[slot, at, 2 * CH : 3 * CH]
            g_out = gates[slot, at, 3 * CH : 4 * CH]
            squash = jnp.tanh(gates[slot, at, 4 * CH :])
            dh = d_hid[at]
            total = d_cell[at] + dh * g_out * (1.0 - squash * squash)
            d_cell[at] = total * g_keep
            to = pl.ds(pl.multiple_of(i * CHUNK + COLS, COLS), CHUNK)
            d_pre[to, 0:CH] = (total * g_new * g_in * (1.0 - g_in)).astype(jnp.bfloat16)
            if t > 0:
                c_old = gates[slot + 1, at, 4 * CH :]
                keep = (total * c_old * g_keep * (1.0 - g_keep)).astype(jnp.bfloat16)
            else:
                keep = jnp.zeros((CHUNK, CH), jnp.bfloat16)
            d_pre[to, CH : 2 * CH] = keep
            d_pre[to, 2 * CH : 3 * CH] = (total * g_in * (1.0 - g_new * g_new)).astype(jnp.bfloat16)
            d_pre[to, 3 * CH :] = (dh * squash * g_out * (1.0 - g_out)).astype(jnp.bfloat16)
            return carry

        def spread(i, carry):
            total = None
            for a in range(3):
                part = lax.dot_general(
                    d_pre[pl.ds(pl.multiple_of(i * CHUNK + (2 - a) * COLS, COLS), CHUNK)],
                    w_ref[pl.ds(a * 3 * CH, 3 * CH)],
                    (((1,), (1,)), ((), ())),
                    preferred_element_type=jnp.float32,
                )
                total = part if total is None else total + part
            shape = (CHUNK, CH)
            col = column_of(shape)
            ahead = jnp.where(col == COLS - 1, 0.0, pltpu.roll(total[:, 0:CH], CHUNK - 1, 0))
            behind = jnp.where(col == 0, 0.0, pltpu.roll(total[:, 2 * CH :], 1, 0))
            dh = total[:, CH : 2 * CH] + ahead + behind
            inside = rows_inside(meta, 4 + 4 * i, shape, lattice)
            d_hid[pl.ds(pl.multiple_of(i * CHUNK, CHUNK), CHUNK)] = jnp.where(inside, dh, 0.0)
            return carry

        if t == 0:
            adjoint(1, 0)
        else:
            lax.fori_loop(0, 3, adjoint, 0)
        dp_out[slot] = d_pre[pl.ds(CHUNK + COLS, CHUNK)]
        if t > 0:
            if t == last or t == 1:
                spread(1, 0)
            else:
                lax.fori_loop(0, 3, spread, 0)


def start_gates(rounds, gates, gates_ref, sems):
    last = rounds[-1]
    for slot, t in enumerate(rounds):
        pltpu.make_async_copy(gates_ref.at[t], gates.at[slot], sems.at[slot]).start()
    if last > 0:
        pltpu.make_async_copy(
            gates_ref.at[last - 1, :, pl.ds(4 * CH, CH)],
            gates.at[len(rounds), :, pl.ds(4 * CH, CH)],
            sems.at[len(rounds)],
        ).start()


def first_backward(
    lattice, rounds, parts, meta, label_ref, *refs
):
    stat_refs = refs[:parts]
    (q_ref, r_ref, w_ref, gates_ref, hid_out, cell_out, edge_out, dp_out, small_out,
     gates, d_hid, d_cell, d_pre, sems) = refs[parts:]
    start_gates(rounds, gates, gates_ref, sems)
    sums = tree_sum([ref[...] for ref in stat_refs])
    total = sums[1:2, :]
    pooled = sums[0:1, :] / total
    read = r_ref[...]
    query = q_ref[...]
    logit = jnp.sum(pooled * read, axis=1, keepdims=True)
    label = label_ref[...]
    loss = jnp.maximum(logit, 0.0) + jnp.log1p(jnp.exp(-jnp.abs(logit))) - label * logit
    d_logit = 1.0 / (1.0 + jnp.exp(-logit)) - label
    d_pooled = d_logit * read
    spare = jnp.sum(pooled * d_pooled, axis=1, keepdims=True)
    pltpu.make_async_copy(gates_ref.at[rounds[0]], gates.at[0], sems.at[0]).wait()
    lead = meta[0] == 0
    small_out[...] = jnp.zeros_like(small_out)
    for i in range(3):
        at = pl.ds(i * CHUNK, CHUNK)
        hidden = gates[0, at, 3 * CH : 4 * CH] * jnp.tanh(gates[0, at, 4 * CH :])
        hidden = hidden.astype(jnp.bfloat16).astype(jnp.float32)
        weight = jnp.exp(jnp.sum(hidden * query, axis=1, keepdims=True) * SCALE) / total[:, 0:1]
        d_score = weight * (jnp.sum(hidden * d_pooled, axis=1, keepdims=True) - spare)
        grad = weight * d_pooled + d_score * (query * SCALE)
        inside = rows_inside(meta, 4 + 4 * i, (CHUNK, CH), lattice)
        d_hid[at] = jnp.where(inside, grad, 0.0)
        if i == 1:
            small_out[5:6, :] = SCALE * jnp.sum(d_score * hidden, axis=0, keepdims=True)
    d_cell[...] = jnp.zeros_like(d_cell)
    lane = lax.broadcasted_iota(jnp.int32, (1, CH), 1)
    small_out[6:7, :] = jnp.where(lead, d_logit * pooled, 0.0)
    small_out[7:8, :] = jnp.where(jnp.logical_and(lead, lane == 0), loss, 0.0)
    backward_rounds(
        lattice, meta, rounds, w_ref, gates, gates_ref, sems, d_hid, d_cell, d_pre, dp_out, ready=1
    )
    own = pl.ds(CHUNK, CHUNK)
    hid_out[...] = d_hid[own]
    cell_out[...] = d_cell[own]
    edge_out[:, 0:CH] = d_hid[own].astype(jnp.bfloat16)
    edge_out[:, CH:] = d_cell[own].astype(jnp.bfloat16)


def load_adjoint(meta, lattice, rows, below, above, hid_in, cell_in, d_hid, d_cell):
    size = rows * COLS
    blank = jnp.zeros((CHUNK, CH), jnp.float32)
    if rows < 4:
        for i in (0, 2):
            d_hid[pl.ds(i * CHUNK, CHUNK)] = blank
            d_cell[pl.ds(i * CHUNK, CHUNK)] = blank
    for first, ref in ((CHUNK - size, below), (2 * CHUNK, above)):
        inside = rows_inside(meta, 4 + first // COLS, (size, CH), lattice)
        d_hid[pl.ds(first, size)] = jnp.where(inside, ref[:, 0:CH].astype(jnp.float32), 0.0)
        d_cell[pl.ds(first, size)] = jnp.where(inside, ref[:, CH:].astype(jnp.float32), 0.0)
    d_hid[pl.ds(CHUNK, CHUNK)] = hid_in[...]
    d_cell[pl.ds(CHUNK, CHUNK)] = cell_in[...]


def middle_backward(
    lattice, rounds, rows, meta, below, above, hid_in, cell_in, w_ref, gates_ref,
    hid_out, cell_out, edge_out, dp_out, gates, d_hid, d_cell, d_pre, sems,
):
    start_gates(rounds, gates, gates_ref, sems)
    load_adjoint(meta, lattice, rows, below, above, hid_in, cell_in, d_hid, d_cell)
    backward_rounds(lattice, meta, rounds, w_ref, gates, gates_ref, sems, d_hid, d_cell, d_pre, dp_out)
    own = pl.ds(CHUNK, CHUNK)
    hid_out[...] = d_hid[own]
    cell_out[...] = d_cell[own]
    edge_out[:, 0:CH] = d_hid[own].astype(jnp.bfloat16)
    edge_out[:, CH:] = d_cell[own].astype(jnp.bfloat16)


def last_backward(
    lattice, rounds, rows, meta, below, above, hid_in, cell_in, w_ref, dp_one, dp_two, small_in,
    gates_ref, dp_out, mine_out, other_out, small_out, gates, d_hid, d_cell, d_pre, total, sems,
):
    start_gates(rounds, gates, gates_ref, sems)
    load_adjoint(meta, lattice, rows, below, above, hid_in, cell_in, d_hid, d_cell)
    backward_rounds(lattice, meta, rounds, w_ref, gates, gates_ref, sems, d_hid, d_cell, d_pre, dp_out)
    summed = None
    for ref, count in ((dp_one, 1), (dp_two, 2), (dp_out, len(rounds))):
        for i in range(count):
            part = ref[i].astype(jnp.float32)
            summed = part if summed is None else summed + part
    total[...] = summed
    core = meta[1]
    half = 2 * COLS
    mine_out[...] = total[pl.ds(pl.multiple_of(core * half, half), half)]
    other_out[...] = total[pl.ds(pl.multiple_of((1 - core) * half, half), half)].astype(jnp.bfloat16)
    small_out[...] = small_in[...]
    small_out[4:5, :] = jnp.sum(total[:, CH : 2 * CH], axis=0, keepdims=True)


def weight_kernel(
    pieces, meta, bits_ref, small_ref, dp_one, dp_two, dp_three, hist_ref, keep_ref, send_ref,
    dp, grad, fired_sum, dp_sem,
):
    copies = []
    for ref, low in ((dp_one, 7), (dp_two, 6), (dp_three, 4)):
        for i in range(ref.shape[0]):
            copies.append(pltpu.make_async_copy(ref.at[i], dp.at[low - i], dp_sem.at[low - i]))
    for copy in copies:
        copy.start()
    grad[...] = jnp.zeros_like(grad)
    for copy in copies:
        copy.wait()
    word = jnp.concatenate([bits_ref[0], bits_ref[1]], axis=1)

    def add_fired(t):
        rows = jnp.where(lax.broadcasted_iota(jnp.int32, word.shape, 0) == t, word, 0.0)
        return jnp.dot(rows.astype(jnp.bfloat16), dp[t], preferred_element_type=jnp.float32)

    fired_sum[...] = add_fired(0)

    def add_round(t, carry):
        fired_sum[...] += add_fired(t)
        for a in range(3):
            grad[pl.ds(a * 3 * CH, 3 * CH)] += lax.dot_general(
                hist_ref[t - 1, pl.ds(a * COLS, CHUNK)],
                dp[t],
                (((0,), (0,)), ((), ())),
                preferred_element_type=jnp.float32,
            )
        return carry

    lax.fori_loop(1, ROUNDS, add_round, 0)
    fired = jnp.sum(fired_sum[...], axis=0, keepdims=True)
    rows = [fired[:, g * CH : (g + 1) * CH] for g in range(4)]
    words = split_words(jnp.concatenate(rows + [small_ref[4:8, :]], axis=0))
    both = words[0:8].astype(jnp.float32) + words[8:16].astype(jnp.float32)
    core = meta[1]
    per = pieces // 4
    size = 9 * CH // per
    for n in range(pieces // 2):
        g, m = n // per, n % per
        mine = pl.ds(pl.multiple_of((2 * core + g) * CH, CH), CH)
        other = pl.ds(pl.multiple_of((2 - 2 * core + g) * CH, CH), CH)
        keep_ref[n, 0:size, :] = grad[pl.ds(m * size, size), mine]
        keep_ref[n, size : size + 8, :] = both
        send_ref[n, 0:size, :] = grad[pl.ds(m * size, size), other].astype(jnp.bfloat16)
        send_ref[n, size:, :] = words


def final_kernel(pieces, planes, meta, mine_ref, other_ref, stab_ref, conv_out, stab_out):
    core = meta[1]
    per = pieces // 4
    size = 9 * CH // per
    for n in range(pieces // 2):
        g, m = n // per, n % per
        mine = pl.ds(pl.multiple_of((2 * core + g) * CH, CH), CH)
        other = pl.ds(pl.multiple_of((2 - 2 * core + g) * CH, CH), CH)
        conv_out[pl.ds(m * size, size), mine] = mine_ref[n].astype(jnp.float32)
        conv_out[pl.ds(m * size, size), other] = other_ref[n].astype(jnp.float32)
    rows = 2 * COLS // planes
    for z in range(planes):
        for g in range(4):
            stab_out[pl.ds(z * rows, rows), g * CH : (g + 1) * CH] = stab_ref[
                z, pl.ds(g * rows, rows)
            ].astype(jnp.float32)


def f32(*shape):
    return jax.ShapeDtypeStruct(shape, jnp.float32)


def b16(*shape):
    return jax.ShapeDtypeStruct(shape, jnp.bfloat16)


def call(kernel, in_specs, out_shape, out_specs, scratch, flops):
    return pl.pallas_call(
        kernel,
        in_specs=in_specs,
        out_shape=out_shape,
        out_specs=out_specs,
        scratch_shapes=scratch,
        cost_estimate=pl.CostEstimate(flops=flops, bytes_accessed=4_000_000, transcendentals=0),
        compiler_params=pltpu.CompilerParams(vmem_limit_bytes=48 * 1024 * 1024),
    )


def segment_scratch(count, extra):
    return [
        pltpu.VMEM((count, MID, 5 * CH), jnp.float32),
        pltpu.VMEM((MID, CH), jnp.float32),
        pltpu.VMEM((MID, CH), jnp.float32),
        pltpu.VMEM((14 * COLS, UNITS), jnp.bfloat16),
        *extra,
        pltpu.SemaphoreType.DMA((count + 1,)),
    ]


def per_device(
    syndromes, labels, stab_gate, bit_gate, forget_bias, conv_weight, query, readout_weight
):
    tiles = lax.axis_size("tiles")
    planes = lax.axis_size("rounds")
    tile = lax.axis_index("tiles")
    core = tile & 1
    lattice = 2 * tiles
    meta = jnp.stack([tile // 2, core]).astype(jnp.int32)
    weights = conv_weight.reshape(9 * CH, UNITS)
    bit_row = bit_gate.reshape(1, UNITS)
    forget_row = forget_bias.reshape(1, CH)
    query_row = query.reshape(1, CH)
    read_row = readout_weight.reshape(1, CH)

    words = jnp.swapaxes(syndromes[:, :, 0], 0, 1).astype(jnp.bfloat16).reshape(16, 2 * COLS)
    words = jnp.pad(words, ((0, 0), (0, UNITS - 2 * COLS)))
    own = jnp.concatenate([stab_gate.reshape(2 * COLS, UNITS), words], axis=0)
    near = [shift(own, "tiles", step) for step in (4, 2)]
    far = [shift(own, "tiles", step) for step in (-2, -4)]
    mine = jnp.stack(near + [own] + far)
    theirs = swap(mine, "tiles", 1)

    gates, hist, stats, bits = call(
        functools.partial(forward_kernel, lattice),
        [SMEM, ANY, ANY, VMEM, VMEM, VMEM, VMEM],
        (f32(ROUNDS, MID, 5 * CH), b16(ROUNDS, 6 * COLS, 3 * CH), f32(8, CH), f32(2, 8, CH)),
        (ANY, ANY, VMEM, VMEM),
        [
            pltpu.VMEM((EXT * COLS, UNITS), jnp.bfloat16),
            pltpu.VMEM((10, 16, UNITS), jnp.bfloat16),
            pltpu.VMEM((10, 8, CH), jnp.float32),
            pltpu.VMEM((EXT * COLS, CH), jnp.bfloat16),
            pltpu.VMEM((10 * CH, UNITS), jnp.bfloat16),
            pltpu.VMEM((2, (EXT + 2) * COLS, 3 * CH), jnp.bfloat16),
            pltpu.VMEM((EXT * COLS, CH), jnp.float32),
            pltpu.VMEM((2, EXT * COLS, 5 * CH), jnp.float32),
            pltpu.SemaphoreType.DMA((20,)),
            pltpu.SemaphoreType.DMA((2,)),
            pltpu.SemaphoreType.DMA((2,)),
        ],
        8_000_000_000,
    )(meta, mine, theirs, weights, bit_row, forget_row, query_row)

    parts = [stats]
    for start, size in tile_groups(tiles):
        stats = tree_sum(parts)
        parts = [stats] + [swap(stats, "tiles", start * k) for k in range(1, size)]

    label = jnp.where(core == 0, labels[0], labels[1]).astype(jnp.float32).reshape(1, 1)
    first = [7]
    d_hid, d_cell, edge, dp_one, small = call(
        functools.partial(first_backward, lattice, first, len(parts)),
        [SMEM, VMEM] + [VMEM] * len(parts) + [VMEM, VMEM, VMEM, ANY],
        (f32(CHUNK, CH), f32(CHUNK, CH), b16(CHUNK, 2 * CH), b16(1, CHUNK, UNITS), f32(8, CH)),
        (VMEM,) * 5,
        segment_scratch(2, []),
        1_000_000_000,
    )(meta, label, *parts, query_row, read_row, weights, gates)

    half = 2 * COLS
    below = shift(edge[half:], "tiles", 2)
    above = shift(edge[:half], "tiles", -2)
    middle = [6, 5]
    d_hid, d_cell, edge, dp_two = call(
        functools.partial(middle_backward, lattice, middle, 2),
        [SMEM] + [VMEM] * 5 + [ANY],
        (f32(CHUNK, CH), f32(CHUNK, CH), b16(CHUNK, 2 * CH), b16(2, CHUNK, UNITS)),
        (VMEM,) * 4,
        segment_scratch(3, []),
        2_000_000_000,
    )(meta, below, above, d_hid, d_cell, weights, gates)

    below = shift(edge, "tiles", 2)
    above = shift(edge, "tiles", -2)
    last = [4, 3, 2, 1, 0]
    dp_three, stab_mine, stab_other, small = call(
        functools.partial(last_backward, lattice, last, 4),
        [SMEM] + [VMEM] * 8 + [ANY],
        (b16(5, CHUNK, UNITS), f32(half, UNITS), b16(half, UNITS), f32(8, CH)),
        (VMEM,) * 4,
        segment_scratch(5, [pltpu.VMEM((CHUNK, UNITS), jnp.float32)]),
        4_000_000_000,
    )(meta, below, above, d_hid, d_cell, weights, dp_one, dp_two, small, gates)

    size = 36 * CH // tiles
    chips = tiles // 2
    keep, send = call(
        functools.partial(weight_kernel, tiles),
        [SMEM, VMEM, VMEM, ANY, ANY, ANY, VMEM],
        (f32(chips, size + 8, CH), b16(chips, size + 16, CH)),
        (VMEM, VMEM),
        [
            pltpu.VMEM((ROUNDS, CHUNK, UNITS), jnp.bfloat16),
            pltpu.VMEM((9 * CH, UNITS), jnp.float32),
            pltpu.VMEM((8, UNITS), jnp.float32),
            pltpu.SemaphoreType.DMA((ROUNDS,)),
        ],
        3_000_000_000,
    )(meta, bits, small, dp_one, dp_two, dp_three, hist)
    send, stab_other = lax.optimization_barrier((send, stab_other))
    back = swap(send, "tiles", 1).astype(jnp.float32)
    words = split_words((keep[:, size:] + back[:, size : size + 8] + back[:, size + 8 :])[0])
    message = jnp.concatenate(
        [
            (keep[:, :size] + back[:, :size]).astype(jnp.bfloat16),
            jnp.broadcast_to(words[None], (chips,) + words.shape),
        ],
        axis=1,
    )
    sides = [list(range(side, tiles, 2)) for side in range(2)]
    back = lax.all_to_all(
        message, "tiles", 0, 0, axis_index_groups=sides, tiled=True
    ).astype(jnp.float32)
    piece = jnp.sum(back[:, :size], axis=0)
    small = jnp.sum(back[:, size : size + 8] + back[:, size + 8 :], axis=0)

    stab = stab_mine + swap(stab_other, "tiles", 1).astype(jnp.float32)
    rows = half // planes
    stab = jnp.swapaxes(stab.astype(jnp.bfloat16).reshape(planes, rows, 4, CH), 1, 2)
    stab = stab.reshape(planes, 4 * rows, CH)
    joint = jnp.concatenate([piece.astype(jnp.bfloat16), split_words(small)], axis=0)
    joint = jnp.broadcast_to(joint[None], (planes,) + joint.shape)
    joint = lax.all_to_all(
        jnp.concatenate([joint, stab], axis=1), "rounds", 0, 0, tiled=True
    ).astype(jnp.float32)
    piece = jnp.sum(joint[:, :size], axis=0).astype(jnp.bfloat16)
    small = jnp.sum(joint[:, size : size + 8] + joint[:, size + 8 : size + 16], axis=0)
    stab = jnp.sum(joint[:, size + 16 :], axis=0).astype(jnp.bfloat16)
    piece = lax.all_to_all(
        jnp.broadcast_to(piece[None], (chips, size, CH)), "tiles", 0, 0,
        axis_index_groups=sides, tiled=True,
    )
    stab_all = lax.all_to_all(
        jnp.broadcast_to(stab[None], (planes,) + stab.shape), "rounds", 0, 0, tiled=True
    )
    other = swap(piece, "tiles", 1)
    grad_conv, grad_stab = call(
        functools.partial(final_kernel, tiles, planes),
        [SMEM, VMEM, VMEM, VMEM],
        (f32(9 * CH, UNITS), f32(half, UNITS)),
        (VMEM, VMEM),
        [],
        1_000_000,
    )(meta, piece, other, stab_all)
    return (
        grad_conv.reshape(3, 3, CH, UNITS),
        grad_stab.reshape(2, COLS, UNITS),
        small[:4].reshape(UNITS),
        small[4],
        small[5],
        small[6],
        small[7, 0],
    )


def solution(mesh):
    in_specs = (
        P(None, None, "rounds", "tiles", None),
        P(None, "rounds"),
        P("tiles", None, None),
        P(),
        P(),
        P(),
        P(),
        P(),
    )
    out_specs = (P(), P("tiles", None, None), P(), P(), P(), P(), P())
    return jax.shard_map(
        per_device, mesh=mesh, in_specs=in_specs, out_specs=out_specs, check_vma=False
    )
```

```python
import functools
import math

import jax
import jax.numpy as jnp
from jax import lax
from jax.experimental import pallas as pl
from jax.experimental.pallas import tpu as pltpu
from jax.sharding import PartitionSpec as P


COLS = 64
CH = 128
UNITS = 512
ROUNDS = 8
OWN = 4
HALO = 8
EXT = OWN + 2 * HALO
CHUNK = 4 * COLS
MID = 12 * COLS
SCALE = 1.0 / math.sqrt(CH)
VMEM = pl.BlockSpec(memory_space=pltpu.VMEM)
SMEM = pl.BlockSpec(memory_space=pltpu.SMEM)
ANY = pl.BlockSpec(memory_space=pl.ANY)


def swap(values, axis, mask):
    count = lax.axis_size(axis)
    return lax.ppermute(values, axis, [(i, i ^ mask) for i in range(count)])


def shift(values, axis, step):
    count = lax.axis_size(axis)
    return lax.ppermute(values, axis, [(i, (i + step) % count) for i in range(count)])


def tree_sum(parts):
    while len(parts) > 1:
        parts = [parts[i] + parts[i + 1] for i in range(0, len(parts), 2)]
    return parts[0]


def tile_groups(count):
    groups = []
    start = 2
    while start < count:
        size = min(4, count // start)
        groups.append((start, size))
        start *= size
    return groups


def split_words(values):
    high = values.astype(jnp.bfloat16)
    low = (values - high.astype(jnp.float32)).astype(jnp.bfloat16)
    return jnp.concatenate([high, low], axis=0)


def gate(values):
    return 0.5 * jnp.tanh(0.5 * values) + 0.5


def rows_inside(meta, first, shape, lattice):
    site = lax.broadcasted_iota(jnp.int32, shape, 0)
    low = (HALO - OWN * meta[0] - first) * COLS
    return jnp.logical_and(site >= low, site < low + lattice * COLS)


def column_of(shape):
    return lax.broadcasted_iota(jnp.int32, shape, 0) & (COLS - 1)


def forward_kernel(
    lattice, meta, a_ref, b_ref, w_ref, bit_ref, forget_ref, q_ref,
    gates_out, hist_out, stats_out, bits_out,
    stab, raw, bits, fired, w_all, hc, cell, stage, in_sem, gate_sem, hist_sem,
):
    core = meta[1]
    copies = []
    for k in range(5):
        for side, ref in ((core, a_ref), (1 - core, b_ref)):
            n = len(copies)
            copies.append(
                pltpu.make_async_copy(
                    ref.at[k, pl.ds(0, 2 * COLS)],
                    stab.at[pl.ds(pl.multiple_of(k * CHUNK + side * 2 * COLS, 2 * COLS), 2 * COLS)],
                    in_sem.at[n],
                )
            )
            copies.append(
                pltpu.make_async_copy(
                    ref.at[k, pl.ds(2 * COLS, 16)], raw.at[2 * k + side], in_sem.at[n + 1]
                )
            )
    for copy in copies:
        copy.start()
    edge = jnp.zeros((COLS, 3 * CH), jnp.bfloat16)
    for slot in range(2):
        hc[slot, pl.ds(0, COLS)] = edge
        hc[slot, pl.ds((EXT + 1) * COLS, COLS)] = edge
    cell[...] = jnp.zeros_like(cell)
    for copy in copies:
        copy.wait()
    for i in range(10):
        words = raw[i].astype(jnp.float32)
        bits[i] = jnp.where(core == 0, words[0:8, 0:CH], words[8:16, 0:CH])
    for i in range(2):
        bits_out[i] = bits[HALO // 2 + i]
    lane = lax.broadcasted_iota(jnp.int32, (8, CH), 1)
    spread = jnp.logical_and((lane & 7) == lax.broadcasted_iota(jnp.int32, (8, CH), 0), lane < 24)
    spread = spread.astype(jnp.float32)
    ones = jnp.logical_and(lane[0:1] >= 24, lane[0:1] < 27).astype(jnp.float32)
    for i in range(10):
        columns = lax.dot_general(
            bits[i], spread, (((0,), (0,)), ((), ())), preferred_element_type=jnp.float32
        )
        fired[pl.ds(i * CH, CH)] = (columns + ones).astype(jnp.bfloat16)
    w_all[pl.ds(0, 9 * CH)] = w_ref[...]
    rest_bit = bit_ref[...]
    rest_keep = jnp.concatenate(
        [jnp.zeros((1, CH), jnp.float32), forget_ref[...], jnp.zeros((1, 2 * CH), jnp.float32)],
        axis=1,
    )
    sink = []
    for w in range(3):
        word = rest_bit.astype(jnp.bfloat16).astype(jnp.float32)
        rest_bit = rest_bit - word
        sink.append(jnp.broadcast_to(word, (8, UNITS)))
    place = lax.broadcasted_iota(jnp.int32, (8, UNITS), 0)
    last = jnp.zeros((8, UNITS), jnp.float32)
    for w in range(3):
        word = rest_keep.astype(jnp.bfloat16).astype(jnp.float32)
        rest_keep = rest_keep - word
        last = jnp.where(place == w, word, last)
    sink.append(last)
    sink.append(jnp.zeros((CH - 32, UNITS), jnp.float32))
    w_all[pl.ds(9 * CH, CH)] = jnp.concatenate(sink, axis=0).astype(jnp.bfloat16)

    def gate_copy(t):
        return pltpu.make_async_copy(
            stage.at[t % 2, pl.ds(4 * COLS, MID)], gates_out.at[t], gate_sem.at[t % 2]
        )

    def hist_copy(t):
        return pltpu.make_async_copy(
            hc.at[t % 2, pl.ds(8 * COLS, 6 * COLS)], hist_out.at[t], hist_sem.at[t % 2]
        )

    def run_round(t, first):
        low = 0 if first else (t // 2) * 2
        count = 5 if first else 5 - t // 2
        now = 0 if first else t % 2
        lane = lax.broadcasted_iota(jnp.int32, (1, CH), 1)
        wanted = jnp.logical_or((lane & 7) == t, lane >= 24).astype(jnp.bfloat16)

        def chunk(i, carry):
            row = low + 4 * i
            at = pl.multiple_of(row * COLS, 2 * COLS)
            pre = stab[pl.ds(at, CHUNK)].astype(jnp.float32)
            extra = fired[pl.ds(at, CHUNK)] * wanted
            if not first:
                taps = jnp.concatenate(
                    [
                        hc[1 - now, pl.ds(pl.multiple_of((row + a) * COLS, COLS), CHUNK)]
                        for a in range(3)
                    ]
                    + [extra],
                    axis=1,
                )
                pre = pre + jnp.dot(taps, w_all[...], preferred_element_type=jnp.float32)
            else:
                pre = pre + jnp.dot(
                    extra, w_all[pl.ds(9 * CH, CH)], preferred_element_type=jnp.float32
                )
            g_in = gate(pre[:, 0:CH])
            g_keep = gate(pre[:, CH : 2 * CH])
            g_new = jnp.tanh(pre[:, 2 * CH : 3 * CH])
            g_out = gate(pre[:, 3 * CH :])
            c_new = g_keep * cell[pl.ds(at, CHUNK)] + g_in * g_new
            cell[pl.ds(at, CHUNK)] = c_new
            stage[now, pl.ds(at, CHUNK), 0:CH] = g_in
            stage[now, pl.ds(at, CHUNK), CH : 2 * CH] = g_keep
            stage[now, pl.ds(at, CHUNK), 2 * CH : 3 * CH] = g_new
            stage[now, pl.ds(at, CHUNK), 3 * CH : 4 * CH] = g_out
            stage[now, pl.ds(at, CHUNK), 4 * CH :] = c_new
            shape = (CHUNK, CH)
            hidden = jnp.where(
                rows_inside(meta, row, shape, lattice), g_out * jnp.tanh(c_new), 0.0
            )
            col = column_of(shape)
            left = jnp.where(col == 0, 0.0, pltpu.roll(hidden, 1, 0))
            right = jnp.where(col == COLS - 1, 0.0, pltpu.roll(hidden, CHUNK - 1, 0))
            to = pl.multiple_of((row + 1) * COLS, COLS)
            hc[now, pl.ds(to, CHUNK), 0:CH] = left.astype(jnp.bfloat16)
            hc[now, pl.ds(to, CHUNK), CH : 2 * CH] = hidden.astype(jnp.bfloat16)
            hc[now, pl.ds(to, CHUNK), 2 * CH :] = right.astype(jnp.bfloat16)
            return carry

        lax.fori_loop(0, count, chunk, 0)
        gate_copy(t).start()
        hist_copy(t).start()

    run_round(0, True)

    def later(t, carry):
        @pl.when(t >= 2)
        def _():
            gate_copy(t - 2).wait()
            hist_copy(t - 2).wait()

        run_round(t, False)
        return carry

    lax.fori_loop(1, ROUNDS, later, 0)
    hidden = hc[1, pl.ds((HALO + 1) * COLS, CHUNK), CH : 2 * CH].astype(jnp.float32)
    weight = jnp.exp(jnp.sum(hidden * q_ref[...], axis=1, keepdims=True) * SCALE)
    stats_out[...] = jnp.zeros_like(stats_out)
    stats_out[0:1, :] = jnp.sum(weight * hidden, axis=0, keepdims=True)
    stats_out[1:2, :] = jnp.broadcast_to(jnp.sum(weight, axis=0, keepdims=True), (1, CH))
    for t in (ROUNDS - 2, ROUNDS - 1):
        gate_copy(t).wait()
        hist_copy(t).wait()


def backward_rounds(
    lattice, meta, rounds, w_ref, gates, gates_ref, sems, d_hid, d_cell, d_pre, dp_out, ready=0
):
    last = rounds[-1]
    for slot, t in list(enumerate(rounds))[ready:]:
        pltpu.make_async_copy(gates_ref.at[t], gates.at[slot], sems.at[slot]).wait()
    if last > 0:
        pltpu.make_async_copy(
            gates_ref.at[last - 1, :, pl.ds(4 * CH, CH)],
            gates.at[len(rounds), :, pl.ds(4 * CH, CH)],
            sems.at[len(rounds)],
        ).wait()
    edge = jnp.zeros((COLS, UNITS), jnp.bfloat16)
    d_pre[pl.ds(0, COLS)] = edge
    d_pre[pl.ds(13 * COLS, COLS)] = edge
    for slot, t in enumerate(rounds):

        def adjoint(i, carry, slot=slot, t=t):
            at = pl.ds(pl.multiple_of(i * CHUNK, CHUNK), CHUNK)
            g_in = gates[slot, at, 0:CH]
            g_keep = gates[slot, at, CH : 2 * CH]
            g_new = gates[slot, at, 2 * CH : 3 * CH]
            g_out = gates[slot, at, 3 * CH : 4 * CH]
            squash = jnp.tanh(gates[slot, at, 4 * CH :])
            dh = d_hid[at]
            total = d_cell[at] + dh * g_out * (1.0 - squash * squash)
            d_cell[at] = total * g_keep
            to = pl.ds(pl.multiple_of(i * CHUNK + COLS, COLS), CHUNK)
            d_pre[to, 0:CH] = (total * g_new * g_in * (1.0 - g_in)).astype(jnp.bfloat16)
            if t > 0:
                c_old = gates[slot + 1, at, 4 * CH :]
                keep = (total * c_old * g_keep * (1.0 - g_keep)).astype(jnp.bfloat16)
            else:
                keep = jnp.zeros((CHUNK, CH), jnp.bfloat16)
            d_pre[to, CH : 2 * CH] = keep
            d_pre[to, 2 * CH : 3 * CH] = (total * g_in * (1.0 - g_new * g_new)).astype(jnp.bfloat16)
            d_pre[to, 3 * CH :] = (dh * squash * g_out * (1.0 - g_out)).astype(jnp.bfloat16)
            return carry

        def spread(i, carry):
            total = None
            for a in range(3):
                part = lax.dot_general(
                    d_pre[pl.ds(pl.multiple_of(i * CHUNK + (2 - a) * COLS, COLS), CHUNK)],
                    w_ref[pl.ds(a * 3 * CH, 3 * CH)],
                    (((1,), (1,)), ((), ())),
                    preferred_element_type=jnp.float32,
                )
                total = part if total is None else total + part
            shape = (CHUNK, CH)
            col = column_of(shape)
            ahead = jnp.where(col == COLS - 1, 0.0, pltpu.roll(total[:, 0:CH], CHUNK - 1, 0))
            behind = jnp.where(col == 0, 0.0, pltpu.roll(total[:, 2 * CH :], 1, 0))
            dh = total[:, CH : 2 * CH] + ahead + behind
            inside = rows_inside(meta, 4 + 4 * i, shape, lattice)
            d_hid[pl.ds(pl.multiple_of(i * CHUNK, CHUNK), CHUNK)] = jnp.where(inside, dh, 0.0)
            return carry

        if t == 0:
            adjoint(1, 0)
        else:
            lax.fori_loop(0, 3, adjoint, 0)
        dp_out[slot] = d_pre[pl.ds(CHUNK + COLS, CHUNK)]
        if t > 0:
            if t == last or t == 1:
                spread(1, 0)
            else:
                lax.fori_loop(0, 3, spread, 0)


def start_gates(rounds, gates, gates_ref, sems):
    last = rounds[-1]
    for slot, t in enumerate(rounds):
        pltpu.make_async_copy(gates_ref.at[t], gates.at[slot], sems.at[slot]).start()
    if last > 0:
        pltpu.make_async_copy(
            gates_ref.at[last - 1, :, pl.ds(4 * CH, CH)],
            gates.at[len(rounds), :, pl.ds(4 * CH, CH)],
            sems.at[len(rounds)],
        ).start()


def first_backward(
    lattice, rounds, parts, meta, label_ref, *refs
):
    stat_refs = refs[:parts]
    (q_ref, r_ref, w_ref, gates_ref, hid_out, cell_out, edge_out, dp_out, small_out,
     gates, d_hid, d_cell, d_pre, sems) = refs[parts:]
    start_gates(rounds, gates, gates_ref, sems)
    sums = tree_sum([ref[...] for ref in stat_refs])
    total = sums[1:2, :]
    pooled = sums[0:1, :] / total
    read = r_ref[...]
    query = q_ref[...]
    logit = jnp.sum(pooled * read, axis=1, keepdims=True)
    label = label_ref[...]
    loss = jnp.maximum(logit, 0.0) + jnp.log1p(jnp.exp(-jnp.abs(logit))) - label * logit
    d_logit = 1.0 / (1.0 + jnp.exp(-logit)) - label
    d_pooled = d_logit * read
    spare = jnp.sum(pooled * d_pooled, axis=1, keepdims=True)
    pltpu.make_async_copy(gates_ref.at[rounds[0]], gates.at[0], sems.at[0]).wait()
    lead = meta[0] == 0
    small_out[...] = jnp.zeros_like(small_out)
    for i in range(3):
        at = pl.ds(i * CHUNK, CHUNK)
        hidden = gates[0, at, 3 * CH : 4 * CH] * jnp.tanh(gates[0, at, 4 * CH :])
        hidden = hidden.astype(jnp.bfloat16).astype(jnp.float32)
        weight = jnp.exp(jnp.sum(hidden * query, axis=1, keepdims=True) * SCALE) / total[:, 0:1]
        d_score = weight * (jnp.sum(hidden * d_pooled, axis=1, keepdims=True) - spare)
        grad = weight * d_pooled + d_score * (query * SCALE)
        inside = rows_inside(meta, 4 + 4 * i, (CHUNK, CH), lattice)
        d_hid[at] = jnp.where(inside, grad, 0.0)
        if i == 1:
            small_out[5:6, :] = SCALE * jnp.sum(d_score * hidden, axis=0, keepdims=True)
    d_cell[...] = jnp.zeros_like(d_cell)
    lane = lax.broadcasted_iota(jnp.int32, (1, CH), 1)
    small_out[6:7, :] = jnp.where(lead, d_logit * pooled, 0.0)
    small_out[7:8, :] = jnp.where(jnp.logical_and(lead, lane == 0), loss, 0.0)
    backward_rounds(
        lattice, meta, rounds, w_ref, gates, gates_ref, sems, d_hid, d_cell, d_pre, dp_out, ready=1
    )
    own = pl.ds(CHUNK, CHUNK)
    hid_out[...] = d_hid[own]
    cell_out[...] = d_cell[own]
    edge_out[:, 0:CH] = d_hid[own].astype(jnp.bfloat16)
    edge_out[:, CH:] = d_cell[own].astype(jnp.bfloat16)


def load_adjoint(meta, lattice, rows, below, above, hid_in, cell_in, d_hid, d_cell):
    size = rows * COLS
    blank = jnp.zeros((CHUNK, CH), jnp.float32)
    if rows < 4:
        for i in (0, 2):
            d_hid[pl.ds(i * CHUNK, CHUNK)] = blank
            d_cell[pl.ds(i * CHUNK, CHUNK)] = blank
    for first, ref in ((CHUNK - size, below), (2 * CHUNK, above)):
        inside = rows_inside(meta, 4 + first // COLS, (size, CH), lattice)
        d_hid[pl.ds(first, size)] = jnp.where(inside, ref[:, 0:CH].astype(jnp.float32), 0.0)
        d_cell[pl.ds(first, size)] = jnp.where(inside, ref[:, CH:].astype(jnp.float32), 0.0)
    d_hid[pl.ds(CHUNK, CHUNK)] = hid_in[...]
    d_cell[pl.ds(CHUNK, CHUNK)] = cell_in[...]


def middle_backward(
    lattice, rounds, rows, meta, below, above, hid_in, cell_in, w_ref, gates_ref,
    hid_out, cell_out, edge_out, dp_out, gates, d_hid, d_cell, d_pre, sems,
):
    start_gates(rounds, gates, gates_ref, sems)
    load_adjoint(meta, lattice, rows, below, above, hid_in, cell_in, d_hid, d_cell)
    backward_rounds(lattice, meta, rounds, w_ref, gates, gates_ref, sems, d_hid, d_cell, d_pre, dp_out)
    own = pl.ds(CHUNK, CHUNK)
    hid_out[...] = d_hid[own]
    cell_out[...] = d_cell[own]
    edge_out[:, 0:CH] = d_hid[own].astype(jnp.bfloat16)
    edge_out[:, CH:] = d_cell[own].astype(jnp.bfloat16)


def last_backward(
    lattice, rounds, rows, meta, below, above, hid_in, cell_in, w_ref, dp_one, dp_two, small_in,
    gates_ref, dp_out, mine_out, other_out, small_out, gates, d_hid, d_cell, d_pre, total, sems,
):
    start_gates(rounds, gates, gates_ref, sems)
    load_adjoint(meta, lattice, rows, below, above, hid_in, cell_in, d_hid, d_cell)
    backward_rounds(lattice, meta, rounds, w_ref, gates, gates_ref, sems, d_hid, d_cell, d_pre, dp_out)
    summed = None
    for ref, count in ((dp_one, 1), (dp_two, 2), (dp_out, len(rounds))):
        for i in range(count):
            part = ref[i].astype(jnp.float32)
            summed = part if summed is None else summed + part
    total[...] = summed
    core = meta[1]
    half = 2 * COLS
    mine_out[...] = total[pl.ds(pl.multiple_of(core * half, half), half)]
    other_out[...] = total[pl.ds(pl.multiple_of((1 - core) * half, half), half)].astype(jnp.bfloat16)
    small_out[...] = small_in[...]
    small_out[4:5, :] = jnp.sum(total[:, CH : 2 * CH], axis=0, keepdims=True)


def weight_kernel(
    pieces, meta, bits_ref, small_ref, dp_one, dp_two, dp_three, hist_ref, keep_ref, send_ref,
    dp, grad, fired_sum, dp_sem,
):
    copies = []
    for ref, low in ((dp_one, 7), (dp_two, 6), (dp_three, 4)):
        for i in range(ref.shape[0]):
            copies.append(pltpu.make_async_copy(ref.at[i], dp.at[low - i], dp_sem.at[low - i]))
    for copy in copies:
        copy.start()
    grad[...] = jnp.zeros_like(grad)
    for copy in copies:
        copy.wait()
    word = jnp.concatenate([bits_ref[0], bits_ref[1]], axis=1)

    def add_fired(t):
        rows = jnp.where(lax.broadcasted_iota(jnp.int32, word.shape, 0) == t, word, 0.0)
        return jnp.dot(rows.astype(jnp.bfloat16), dp[t], preferred_element_type=jnp.float32)

    fired_sum[...] = add_fired(0)

    def add_round(t, carry):
        fired_sum[...] += add_fired(t)
        for a in range(3):
            grad[pl.ds(a * 3 * CH, 3 * CH)] += lax.dot_general(
                hist_ref[t - 1, pl.ds(a * COLS, CHUNK)],
                dp[t],
                (((0,), (0,)), ((), ())),
                preferred_element_type=jnp.float32,
            )
        return carry

    lax.fori_loop(1, ROUNDS, add_round, 0)
    fired = jnp.sum(fired_sum[...], axis=0, keepdims=True)
    rows = [fired[:, g * CH : (g + 1) * CH] for g in range(4)]
    words = split_words(jnp.concatenate(rows + [small_ref[4:8, :]], axis=0))
    both = words[0:8].astype(jnp.float32) + words[8:16].astype(jnp.float32)
    core = meta[1]
    per = pieces // 4
    size = 9 * CH // per
    for n in range(pieces // 2):
        g, m = n // per, n % per
        mine = pl.ds(pl.multiple_of((2 * core + g) * CH, CH), CH)
        other = pl.ds(pl.multiple_of((2 - 2 * core + g) * CH, CH), CH)
        keep_ref[n, 0:size, :] = grad[pl.ds(m * size, size), mine]
        keep_ref[n, size : size + 8, :] = both
        send_ref[n, 0:size, :] = grad[pl.ds(m * size, size), other].astype(jnp.bfloat16)
        send_ref[n, size:, :] = words


def final_kernel(pieces, planes, meta, mine_ref, other_ref, stab_ref, conv_out, stab_out):
    core = meta[1]
    per = pieces // 4
    size = 9 * CH // per
    for n in range(pieces // 2):
        g, m = n // per, n % per
        mine = pl.ds(pl.multiple_of((2 * core + g) * CH, CH), CH)
        other = pl.ds(pl.multiple_of((2 - 2 * core + g) * CH, CH), CH)
        conv_out[pl.ds(m * size, size), mine] = mine_ref[n].astype(jnp.float32)
        conv_out[pl.ds(m * size, size), other] = other_ref[n].astype(jnp.float32)
    rows = 2 * COLS // planes
    for z in range(planes):
        for g in range(4):
            stab_out[pl.ds(z * rows, rows), g * CH : (g + 1) * CH] = stab_ref[
                z, pl.ds(g * rows, rows)
            ].astype(jnp.float32)


def f32(*shape):
    return jax.ShapeDtypeStruct(shape, jnp.float32)


def b16(*shape):
    return jax.ShapeDtypeStruct(shape, jnp.bfloat16)


def call(kernel, in_specs, out_shape, out_specs, scratch, flops):
    return pl.pallas_call(
        kernel,
        in_specs=in_specs,
        out_shape=out_shape,
        out_specs=out_specs,
        scratch_shapes=scratch,
        cost_estimate=pl.CostEstimate(flops=flops, bytes_accessed=4_000_000, transcendentals=0),
        compiler_params=pltpu.CompilerParams(vmem_limit_bytes=48 * 1024 * 1024),
    )


def segment_scratch(count, extra):
    return [
        pltpu.VMEM((count, MID, 5 * CH), jnp.float32),
        pltpu.VMEM((MID, CH), jnp.float32),
        pltpu.VMEM((MID, CH), jnp.float32),
        pltpu.VMEM((14 * COLS, UNITS), jnp.bfloat16),
        *extra,
        pltpu.SemaphoreType.DMA((count + 1,)),
    ]


def per_device(
    syndromes, labels, stab_gate, bit_gate, forget_bias, conv_weight, query, readout_weight
):
    tiles = lax.axis_size("tiles")
    planes = lax.axis_size("rounds")
    tile = lax.axis_index("tiles")
    core = tile & 1
    lattice = 2 * tiles
    meta = jnp.stack([tile // 2, core]).astype(jnp.int32)
    weights = conv_weight.reshape(9 * CH, UNITS)
    bit_row = bit_gate.reshape(1, UNITS)
    forget_row = forget_bias.reshape(1, CH)
    query_row = query.reshape(1, CH)
    read_row = readout_weight.reshape(1, CH)

    words = jnp.swapaxes(syndromes[:, :, 0], 0, 1).astype(jnp.bfloat16).reshape(16, 2 * COLS)
    words = jnp.pad(words, ((0, 0), (0, UNITS - 2 * COLS)))
    own = jnp.concatenate([stab_gate.reshape(2 * COLS, UNITS), words], axis=0)
    near = [shift(own, "tiles", step) for step in (4, 2)]
    far = [shift(own, "tiles", step) for step in (-2, -4)]
    mine = jnp.stack(near + [own] + far)
    theirs = swap(mine, "tiles", 1)

    gates, hist, stats, bits = call(
        functools.partial(forward_kernel, lattice),
        [SMEM, ANY, ANY, VMEM, VMEM, VMEM, VMEM],
        (f32(ROUNDS, MID, 5 * CH), b16(ROUNDS, 6 * COLS, 3 * CH), f32(8, CH), f32(2, 8, CH)),
        (ANY, ANY, VMEM, VMEM),
        [
            pltpu.VMEM((EXT * COLS, UNITS), jnp.bfloat16),
            pltpu.VMEM((10, 16, UNITS), jnp.bfloat16),
            pltpu.VMEM((10, 8, CH), jnp.float32),
            pltpu.VMEM((EXT * COLS, CH), jnp.bfloat16),
            pltpu.VMEM((10 * CH, UNITS), jnp.bfloat16),
            pltpu.VMEM((2, (EXT + 2) * COLS, 3 * CH), jnp.bfloat16),
            pltpu.VMEM((EXT * COLS, CH), jnp.float32),
            pltpu.VMEM((2, EXT * COLS, 5 * CH), jnp.float32),
            pltpu.SemaphoreType.DMA((20,)),
            pltpu.SemaphoreType.DMA((2,)),
            pltpu.SemaphoreType.DMA((2,)),
        ],
        8_000_000_000,
    )(meta, mine, theirs, weights, bit_row, forget_row, query_row)

    parts = [stats]
    for start, size in tile_groups(tiles):
        stats = tree_sum(parts)
        parts = [stats] + [swap(stats, "tiles", start * k) for k in range(1, size)]

    label = jnp.where(core == 0, labels[0], labels[1]).astype(jnp.float32).reshape(1, 1)
    first = [7]
    d_hid, d_cell, edge, dp_one, small = call(
        functools.partial(first_backward, lattice, first, len(parts)),
        [SMEM, VMEM] + [VMEM] * len(parts) + [VMEM, VMEM, VMEM, ANY],
        (f32(CHUNK, CH), f32(CHUNK, CH), b16(CHUNK, 2 * CH), b16(1, CHUNK, UNITS), f32(8, CH)),
        (VMEM,) * 5,
        segment_scratch(2, []),
        1_000_000_000,
    )(meta, label, *parts, query_row, read_row, weights, gates)

    half = 2 * COLS
    below = shift(edge[half:], "tiles", 2)
    above = shift(edge[:half], "tiles", -2)
    middle = [6, 5]
    d_hid, d_cell, edge, dp_two = call(
        functools.partial(middle_backward, lattice, middle, 2),
        [SMEM] + [VMEM] * 5 + [ANY],
        (f32(CHUNK, CH), f32(CHUNK, CH), b16(CHUNK, 2 * CH), b16(2, CHUNK, UNITS)),
        (VMEM,) * 4,
        segment_scratch(3, []),
        2_000_000_000,
    )(meta, below, above, d_hid, d_cell, weights, gates)

    below = shift(edge, "tiles", 2)
    above = shift(edge, "tiles", -2)
    last = [4, 3, 2, 1, 0]
    dp_three, stab_mine, stab_other, small = call(
        functools.partial(last_backward, lattice, last, 4),
        [SMEM] + [VMEM] * 8 + [ANY],
        (b16(5, CHUNK, UNITS), f32(half, UNITS), b16(half, UNITS), f32(8, CH)),
        (VMEM,) * 4,
        segment_scratch(5, [pltpu.VMEM((CHUNK, UNITS), jnp.float32)]),
        4_000_000_000,
    )(meta, below, above, d_hid, d_cell, weights, dp_one, dp_two, small, gates)

    size = 36 * CH // tiles
    chips = tiles // 2
    keep, send = call(
        functools.partial(weight_kernel, tiles),
        [SMEM, VMEM, VMEM, ANY, ANY, ANY, VMEM],
        (f32(chips, size + 8, CH), b16(chips, size + 16, CH)),
        (VMEM, VMEM),
        [
            pltpu.VMEM((ROUNDS, CHUNK, UNITS), jnp.bfloat16),
            pltpu.VMEM((9 * CH, UNITS), jnp.float32),
            pltpu.VMEM((8, UNITS), jnp.float32),
            pltpu.SemaphoreType.DMA((ROUNDS,)),
        ],
        3_000_000_000,
    )(meta, bits, small, dp_one, dp_two, dp_three, hist)
    send, stab_other = lax.optimization_barrier((send, stab_other))
    back = swap(send, "tiles", 1).astype(jnp.float32)
    words = split_words((keep[:, size:] + back[:, size : size + 8] + back[:, size + 8 :])[0])
    message = jnp.concatenate(
        [
            (keep[:, :size] + back[:, :size]).astype(jnp.bfloat16),
            jnp.broadcast_to(words[None], (chips,) + words.shape),
        ],
        axis=1,
    )
    sides = [list(range(side, tiles, 2)) for side in range(2)]
    back = lax.all_to_all(
        message, "tiles", 0, 0, axis_index_groups=sides, tiled=True
    ).astype(jnp.float32)
    piece = jnp.sum(back[:, :size], axis=0)
    small = jnp.sum(back[:, size : size + 8] + back[:, size + 8 :], axis=0)

    stab = stab_mine + swap(stab_other, "tiles", 1).astype(jnp.float32)
    rows = half // planes
    stab = jnp.swapaxes(stab.astype(jnp.bfloat16).reshape(planes, rows, 4, CH), 1, 2)
    stab = stab.reshape(planes, 4 * rows, CH)
    part = size // planes
    words = split_words(small)
    joint = jnp.concatenate(
        [
            stab,
            jnp.broadcast_to(words[None], (planes,) + words.shape),
            piece.astype(jnp.bfloat16).reshape(planes, part, CH),
        ],
        axis=1,
    )
    joint = lax.all_to_all(joint, "rounds", 0, 0, tiled=True).astype(jnp.float32)
    lines = 4 * rows
    small = jnp.sum(joint[:, lines : lines + 8] + joint[:, lines + 8 : lines + 16], axis=0)
    done = jnp.concatenate(
        [jnp.sum(joint[:, :lines], axis=0), jnp.sum(joint[:, lines + 16 :], axis=0)], axis=0
    ).astype(jnp.bfloat16)
    joint = lax.all_to_all(
        jnp.broadcast_to(done[None], (planes,) + done.shape), "rounds", 0, 0, tiled=True
    )
    stab_all = joint[:, :lines]
    piece = joint[:, lines:].reshape(size, CH)
    piece = lax.all_to_all(
        jnp.broadcast_to(piece[None], (chips, size, CH)), "tiles", 0, 0,
        axis_index_groups=sides, tiled=True,
    )
    other = swap(piece, "tiles", 1)
    grad_conv, grad_stab = call(
        functools.partial(final_kernel, tiles, planes),
        [SMEM, VMEM, VMEM, VMEM],
        (f32(9 * CH, UNITS), f32(half, UNITS)),
        (VMEM, VMEM),
        [],
        1_000_000,
    )(meta, piece, other, stab_all)
    return (
        grad_conv.reshape(3, 3, CH, UNITS),
        grad_stab.reshape(2, COLS, UNITS),
        small[:4].reshape(UNITS),
        small[4],
        small[5],
        small[6],
        small[7, 0],
    )


def solution(mesh):
    in_specs = (
        P(None, None, "rounds", "tiles", None),
        P(None, "rounds"),
        P("tiles", None, None),
        P(),
        P(),
        P(),
        P(),
        P(),
    )
    out_specs = (P(), P("tiles", None, None), P(), P(), P(), P(), P())
    return jax.shard_map(
        per_device, mesh=mesh, in_specs=in_specs, out_specs=out_specs, check_vma=False
    )
```

```python
import functools
import math

import jax
import jax.numpy as jnp
from jax import lax
from jax.experimental import pallas as pl
from jax.experimental.pallas import tpu as pltpu
from jax.sharding import PartitionSpec as P


COLS = 64
CH = 128
UNITS = 512
ROUNDS = 8
OWN = 4
HALO = 8
EXT = OWN + 2 * HALO
CHUNK = 4 * COLS
MID = 12 * COLS
SCALE = 1.0 / math.sqrt(CH)
VMEM = pl.BlockSpec(memory_space=pltpu.VMEM)
SMEM = pl.BlockSpec(memory_space=pltpu.SMEM)
ANY = pl.BlockSpec(memory_space=pl.ANY)


def swap(values, axis, mask):
    count = lax.axis_size(axis)
    return lax.ppermute(values, axis, [(i, i ^ mask) for i in range(count)])


def shift(values, axis, step):
    count = lax.axis_size(axis)
    return lax.ppermute(values, axis, [(i, (i + step) % count) for i in range(count)])


def tree_sum(parts):
    while len(parts) > 1:
        parts = [parts[i] + parts[i + 1] for i in range(0, len(parts), 2)]
    return parts[0]


def tile_groups(count):
    groups = []
    start = 2
    while start < count:
        size = min(4, count // start)
        groups.append((start, size))
        start *= size
    return groups


def split_words(values):
    high = values.astype(jnp.bfloat16)
    low = (values - high.astype(jnp.float32)).astype(jnp.bfloat16)
    return jnp.concatenate([high, low], axis=0)


def gate(values):
    return 0.5 * jnp.tanh(0.5 * values) + 0.5


def rows_inside(meta, first, shape, lattice):
    site = lax.broadcasted_iota(jnp.int32, shape, 0)
    low = (HALO - OWN * meta[0] - first) * COLS
    return jnp.logical_and(site >= low, site < low + lattice * COLS)


def column_of(shape):
    return lax.broadcasted_iota(jnp.int32, shape, 0) & (COLS - 1)


def forward_kernel(
    lattice, meta, a_ref, b_ref, w_ref, bit_ref, forget_ref, q_ref,
    gates_out, hist_out, stats_out, bits_out,
    stab, raw, bits, fired, w_all, hc, cell, in_sem, hist_sem,
):
    core = meta[1]
    copies = []
    for k in range(5):
        for side, ref in ((core, a_ref), (1 - core, b_ref)):
            n = len(copies)
            copies.append(
                pltpu.make_async_copy(
                    ref.at[k, pl.ds(0, 2 * COLS)],
                    stab.at[pl.ds(pl.multiple_of(k * CHUNK + side * 2 * COLS, 2 * COLS), 2 * COLS)],
                    in_sem.at[n],
                )
            )
            copies.append(
                pltpu.make_async_copy(
                    ref.at[k, pl.ds(2 * COLS, 16)], raw.at[2 * k + side], in_sem.at[n + 1]
                )
            )
    for copy in copies:
        copy.start()
    edge = jnp.zeros((COLS, 3 * CH), jnp.bfloat16)
    for slot in range(2):
        hc[slot, pl.ds(0, COLS)] = edge
        hc[slot, pl.ds((EXT + 1) * COLS, COLS)] = edge
    cell[...] = jnp.zeros_like(cell)
    for copy in copies:
        copy.wait()
    for i in range(10):
        words = raw[i].astype(jnp.float32)
        bits[i] = jnp.where(core == 0, words[0:8, 0:CH], words[8:16, 0:CH])
    for i in range(2):
        bits_out[i] = bits[HALO // 2 + i]
    lane = lax.broadcasted_iota(jnp.int32, (8, CH), 1)
    spread = jnp.logical_and((lane & 7) == lax.broadcasted_iota(jnp.int32, (8, CH), 0), lane < 24)
    spread = spread.astype(jnp.float32)
    ones = jnp.logical_and(lane[0:1] >= 24, lane[0:1] < 27).astype(jnp.float32)
    for i in range(10):
        columns = lax.dot_general(
            bits[i], spread, (((0,), (0,)), ((), ())), preferred_element_type=jnp.float32
        )
        fired[pl.ds(i * CH, CH)] = (columns + ones).astype(jnp.bfloat16)
    w_all[pl.ds(0, 9 * CH)] = w_ref[...]
    rest_bit = bit_ref[...]
    rest_keep = jnp.concatenate(
        [jnp.zeros((1, CH), jnp.float32), forget_ref[...], jnp.zeros((1, 2 * CH), jnp.float32)],
        axis=1,
    )
    sink = []
    for w in range(3):
        word = rest_bit.astype(jnp.bfloat16).astype(jnp.float32)
        rest_bit = rest_bit - word
        sink.append(jnp.broadcast_to(word, (8, UNITS)))
    place = lax.broadcasted_iota(jnp.int32, (8, UNITS), 0)
    last = jnp.zeros((8, UNITS), jnp.float32)
    for w in range(3):
        word = rest_keep.astype(jnp.bfloat16).astype(jnp.float32)
        rest_keep = rest_keep - word
        last = jnp.where(place == w, word, last)
    sink.append(last)
    sink.append(jnp.zeros((CH - 32, UNITS), jnp.float32))
    w_all[pl.ds(9 * CH, CH)] = jnp.concatenate(sink, axis=0).astype(jnp.bfloat16)

    def hist_copy(t):
        return pltpu.make_async_copy(
            hc.at[t % 2, pl.ds(8 * COLS, 6 * COLS)], hist_out.at[t], hist_sem.at[t % 2]
        )

    def run_round(t, first):
        low = 0 if first else (t // 2) * 2
        count = 5 if first else 5 - t // 2
        now = 0 if first else t % 2
        lane = lax.broadcasted_iota(jnp.int32, (1, CH), 1)
        wanted = jnp.logical_or((lane & 7) == t, lane >= 24).astype(jnp.bfloat16)

        def chunk(i, carry):
            row = low + 4 * i
            at = pl.multiple_of(row * COLS, 2 * COLS)
            pre = stab[pl.ds(at, CHUNK)].astype(jnp.float32)
            extra = fired[pl.ds(at, CHUNK)] * wanted
            if not first:
                taps = jnp.concatenate(
                    [
                        hc[1 - now, pl.ds(pl.multiple_of((row + a) * COLS, COLS), CHUNK)]
                        for a in range(3)
                    ]
                    + [extra],
                    axis=1,
                )
                pre = pre + jnp.dot(taps, w_all[...], preferred_element_type=jnp.float32)
            else:
                pre = pre + jnp.dot(
                    extra, w_all[pl.ds(9 * CH, CH)], preferred_element_type=jnp.float32
                )
            g_in = gate(pre[:, 0:CH])
            g_keep = gate(pre[:, CH : 2 * CH])
            g_new = jnp.tanh(pre[:, 2 * CH : 3 * CH])
            g_out = gate(pre[:, 3 * CH :])
            c_new = g_keep * cell[pl.ds(at, CHUNK)] + g_in * g_new
            cell[pl.ds(at, CHUNK)] = c_new
            for p in range(2):
                part = slice(p * 2 * COLS, (p + 1) * 2 * COLS)

                @pl.when(jnp.logical_and(row + 2 * p >= 4, row + 2 * p < 16))
                def _(p=p, part=part):
                    to = pl.ds(pl.multiple_of((row + 2 * p - 4) * COLS, 2 * COLS), 2 * COLS)
                    gates_out[t, to, 0:CH] = g_in[part]
                    gates_out[t, to, CH : 2 * CH] = g_keep[part]
                    gates_out[t, to, 2 * CH : 3 * CH] = g_new[part]
                    gates_out[t, to, 3 * CH : 4 * CH] = g_out[part]
                    gates_out[t, to, 4 * CH :] = c_new[part]

            shape = (CHUNK, CH)
            hidden = jnp.where(
                rows_inside(meta, row, shape, lattice), g_out * jnp.tanh(c_new), 0.0
            )
            col = column_of(shape)
            left = jnp.where(col == 0, 0.0, pltpu.roll(hidden, 1, 0))
            right = jnp.where(col == COLS - 1, 0.0, pltpu.roll(hidden, CHUNK - 1, 0))
            to = pl.multiple_of((row + 1) * COLS, COLS)
            hc[now, pl.ds(to, CHUNK), 0:CH] = left.astype(jnp.bfloat16)
            hc[now, pl.ds(to, CHUNK), CH : 2 * CH] = hidden.astype(jnp.bfloat16)
            hc[now, pl.ds(to, CHUNK), 2 * CH :] = right.astype(jnp.bfloat16)
            return carry

        lax.fori_loop(0, count, chunk, 0)
        hist_copy(t).start()

    run_round(0, True)

    def later(t, carry):
        @pl.when(t >= 2)
        def _():
            hist_copy(t - 2).wait()

        run_round(t, False)
        return carry

    lax.fori_loop(1, ROUNDS, later, 0)
    hidden = hc[1, pl.ds((HALO + 1) * COLS, CHUNK), CH : 2 * CH].astype(jnp.float32)
    weight = jnp.exp(jnp.sum(hidden * q_ref[...], axis=1, keepdims=True) * SCALE)
    stats_out[...] = jnp.zeros_like(stats_out)
    stats_out[0:1, :] = jnp.sum(weight * hidden, axis=0, keepdims=True)
    stats_out[1:2, :] = jnp.broadcast_to(jnp.sum(weight, axis=0, keepdims=True), (1, CH))
    for t in (ROUNDS - 2, ROUNDS - 1):
        hist_copy(t).wait()


def backward_rounds(lattice, meta, rounds, w_ref, gates, d_hid, d_cell, d_pre, dp_out):
    last = rounds[-1]
    edge = jnp.zeros((COLS, UNITS), jnp.bfloat16)
    d_pre[pl.ds(0, COLS)] = edge
    d_pre[pl.ds(13 * COLS, COLS)] = edge
    for slot, t in enumerate(rounds):

        def adjoint(i, carry, t=t):
            at = pl.ds(pl.multiple_of(i * CHUNK, CHUNK), CHUNK)
            g_in = gates[t, at, 0:CH]
            g_keep = gates[t, at, CH : 2 * CH]
            g_new = gates[t, at, 2 * CH : 3 * CH]
            g_out = gates[t, at, 3 * CH : 4 * CH]
            squash = jnp.tanh(gates[t, at, 4 * CH :])
            dh = d_hid[at]
            total = d_cell[at] + dh * g_out * (1.0 - squash * squash)
            d_cell[at] = total * g_keep
            to = pl.ds(pl.multiple_of(i * CHUNK + COLS, COLS), CHUNK)
            d_pre[to, 0:CH] = (total * g_new * g_in * (1.0 - g_in)).astype(jnp.bfloat16)
            if t > 0:
                c_old = gates[t - 1, at, 4 * CH :]
                keep = (total * c_old * g_keep * (1.0 - g_keep)).astype(jnp.bfloat16)
            else:
                keep = jnp.zeros((CHUNK, CH), jnp.bfloat16)
            d_pre[to, CH : 2 * CH] = keep
            d_pre[to, 2 * CH : 3 * CH] = (total * g_in * (1.0 - g_new * g_new)).astype(jnp.bfloat16)
            d_pre[to, 3 * CH :] = (dh * squash * g_out * (1.0 - g_out)).astype(jnp.bfloat16)
            return carry

        def spread(i, carry):
            total = None
            for a in range(3):
                part = lax.dot_general(
                    d_pre[pl.ds(pl.multiple_of(i * CHUNK + (2 - a) * COLS, COLS), CHUNK)],
                    w_ref[pl.ds(a * 3 * CH, 3 * CH)],
                    (((1,), (1,)), ((), ())),
                    preferred_element_type=jnp.float32,
                )
                total = part if total is None else total + part
            shape = (CHUNK, CH)
            col = column_of(shape)
            ahead = jnp.where(col == COLS - 1, 0.0, pltpu.roll(total[:, 0:CH], CHUNK - 1, 0))
            behind = jnp.where(col == 0, 0.0, pltpu.roll(total[:, 2 * CH :], 1, 0))
            dh = total[:, CH : 2 * CH] + ahead + behind
            inside = rows_inside(meta, 4 + 4 * i, shape, lattice)
            d_hid[pl.ds(pl.multiple_of(i * CHUNK, CHUNK), CHUNK)] = jnp.where(inside, dh, 0.0)
            return carry

        if t == 0:
            adjoint(1, 0)
        else:
            lax.fori_loop(0, 3, adjoint, 0)
        dp_out[slot] = d_pre[pl.ds(CHUNK + COLS, CHUNK)]
        if t > 0:
            if t == last or t == 1:
                spread(1, 0)
            else:
                lax.fori_loop(0, 3, spread, 0)


def first_backward(
    lattice, rounds, parts, meta, *refs
):
    stat_refs = refs[:parts]
    (q_ref, r_ref, w_ref, gates, hid_out, cell_out, low_out, high_out, dp_out, small_out,
     d_hid, d_cell, d_pre) = refs[parts:]
    sums = tree_sum([ref[...] for ref in stat_refs])
    total = sums[1:2, :]
    pooled = sums[0:1, :] / total
    read = r_ref[...]
    query = q_ref[...]
    logit = jnp.sum(pooled * read, axis=1, keepdims=True)
    label = meta[2].astype(jnp.float32)
    loss = jnp.maximum(logit, 0.0) + jnp.log1p(jnp.exp(-jnp.abs(logit))) - label * logit
    d_logit = 1.0 / (1.0 + jnp.exp(-logit)) - label
    d_pooled = d_logit * read
    spare = jnp.sum(pooled * d_pooled, axis=1, keepdims=True)
    lead = meta[0] == 0
    small_out[...] = jnp.zeros_like(small_out)
    for i in range(3):
        at = pl.ds(i * CHUNK, CHUNK)
        hidden = gates[rounds[0], at, 3 * CH : 4 * CH] * jnp.tanh(gates[rounds[0], at, 4 * CH :])
        hidden = hidden.astype(jnp.bfloat16).astype(jnp.float32)
        weight = jnp.exp(jnp.sum(hidden * query, axis=1, keepdims=True) * SCALE) / total[:, 0:1]
        d_score = weight * (jnp.sum(hidden * d_pooled, axis=1, keepdims=True) - spare)
        grad = weight * d_pooled + d_score * (query * SCALE)
        inside = rows_inside(meta, 4 + 4 * i, (CHUNK, CH), lattice)
        d_hid[at] = jnp.where(inside, grad, 0.0)
        if i == 1:
            small_out[5:6, :] = SCALE * jnp.sum(d_score * hidden, axis=0, keepdims=True)
    d_cell[...] = jnp.zeros_like(d_cell)
    lane = lax.broadcasted_iota(jnp.int32, (1, CH), 1)
    small_out[6:7, :] = jnp.where(lead, d_logit * pooled, 0.0)
    small_out[7:8, :] = jnp.where(jnp.logical_and(lead, lane == 0), loss, 0.0)
    backward_rounds(lattice, meta, rounds, w_ref, gates, d_hid, d_cell, d_pre, dp_out)
    own = pl.ds(CHUNK, CHUNK)
    hid_out[...] = d_hid[own]
    cell_out[...] = d_cell[own]
    for out, at in ((low_out, CHUNK), (high_out, CHUNK + 2 * COLS)):
        out[:, 0:CH] = d_hid[pl.ds(at, 2 * COLS)].astype(jnp.bfloat16)
        out[:, CH:] = d_cell[pl.ds(at, 2 * COLS)].astype(jnp.bfloat16)


def load_adjoint(meta, lattice, rows, below, above, hid_in, cell_in, d_hid, d_cell):
    size = rows * COLS
    blank = jnp.zeros((CHUNK, CH), jnp.float32)
    if rows < 4:
        for i in (0, 2):
            d_hid[pl.ds(i * CHUNK, CHUNK)] = blank
            d_cell[pl.ds(i * CHUNK, CHUNK)] = blank
    for first, ref in ((CHUNK - size, below), (2 * CHUNK, above)):
        inside = rows_inside(meta, 4 + first // COLS, (size, CH), lattice)
        d_hid[pl.ds(first, size)] = jnp.where(inside, ref[:, 0:CH].astype(jnp.float32), 0.0)
        d_cell[pl.ds(first, size)] = jnp.where(inside, ref[:, CH:].astype(jnp.float32), 0.0)
    d_hid[pl.ds(CHUNK, CHUNK)] = hid_in[...]
    d_cell[pl.ds(CHUNK, CHUNK)] = cell_in[...]


def middle_backward(
    lattice, rounds, rows, meta, below, above, hid_in, cell_in, w_ref, gates,
    hid_out, cell_out, edge_out, dp_out, d_hid, d_cell, d_pre,
):
    load_adjoint(meta, lattice, rows, below, above, hid_in, cell_in, d_hid, d_cell)
    backward_rounds(lattice, meta, rounds, w_ref, gates, d_hid, d_cell, d_pre, dp_out)
    own = pl.ds(CHUNK, CHUNK)
    hid_out[...] = d_hid[own]
    cell_out[...] = d_cell[own]
    edge_out[:, 0:CH] = d_hid[own].astype(jnp.bfloat16)
    edge_out[:, CH:] = d_cell[own].astype(jnp.bfloat16)


def last_backward(
    lattice, rounds, rows, meta, below, above, hid_in, cell_in, w_ref, dp_one, dp_two, small_in,
    gates, dp_out, mine_out, other_out, small_out, d_hid, d_cell, d_pre, total,
):
    load_adjoint(meta, lattice, rows, below, above, hid_in, cell_in, d_hid, d_cell)
    backward_rounds(lattice, meta, rounds, w_ref, gates, d_hid, d_cell, d_pre, dp_out)
    summed = None
    for ref, count in ((dp_one, 1), (dp_two, 2), (dp_out, len(rounds))):
        for i in range(count):
            part = ref[i].astype(jnp.float32)
            summed = part if summed is None else summed + part
    total[...] = summed
    core = meta[1]
    half = 2 * COLS
    mine_out[...] = total[pl.ds(pl.multiple_of(core * half, half), half)]
    other_out[...] = total[pl.ds(pl.multiple_of((1 - core) * half, half), half)].astype(jnp.bfloat16)
    small_out[...] = small_in[...]
    small_out[4:5, :] = jnp.sum(total[:, CH : 2 * CH], axis=0, keepdims=True)


def add_kernel(*refs):
    refs[-1][...] = tree_sum([ref[...] for ref in refs[:-1]])


def weight_kernel(
    pieces, meta, bits_ref, small_ref, dp_one, dp_two, dp_three, hist_ref, keep_ref, send_ref,
    dp, grad, fired_sum, dp_sem,
):
    copies = []
    for ref, low in ((dp_one, 7), (dp_two, 6), (dp_three, 4)):
        for i in range(ref.shape[0]):
            copies.append(pltpu.make_async_copy(ref.at[i], dp.at[low - i], dp_sem.at[low - i]))
    for copy in copies:
        copy.start()
    grad[...] = jnp.zeros_like(grad)
    for copy in copies:
        copy.wait()
    word = jnp.concatenate([bits_ref[0], bits_ref[1]], axis=1)

    def add_fired(t):
        rows = jnp.where(lax.broadcasted_iota(jnp.int32, word.shape, 0) == t, word, 0.0)
        return jnp.dot(rows.astype(jnp.bfloat16), dp[t], preferred_element_type=jnp.float32)

    fired_sum[...] = add_fired(0)

    def add_round(t, carry):
        fired_sum[...] += add_fired(t)
        for a in range(3):
            grad[pl.ds(a * 3 * CH, 3 * CH)] += lax.dot_general(
                hist_ref[t - 1, pl.ds(a * COLS, CHUNK)],
                dp[t],
                (((0,), (0,)), ((), ())),
                preferred_element_type=jnp.float32,
            )
        return carry

    lax.fori_loop(1, ROUNDS, add_round, 0)
    fired = jnp.sum(fired_sum[...], axis=0, keepdims=True)
    rows = [fired[:, g * CH : (g + 1) * CH] for g in range(4)]
    words = split_words(jnp.concatenate(rows + [small_ref[4:8, :]], axis=0))
    both = words[0:8].astype(jnp.float32) + words[8:16].astype(jnp.float32)
    core = meta[1]
    per = pieces // 4
    size = 9 * CH // per
    for n in range(pieces // 2):
        g, m = n // per, n % per
        mine = pl.ds(pl.multiple_of((2 * core + g) * CH, CH), CH)
        other = pl.ds(pl.multiple_of((2 - 2 * core + g) * CH, CH), CH)
        keep_ref[n, 0:size, :] = grad[pl.ds(m * size, size), mine]
        keep_ref[n, size : size + 8, :] = both
        send_ref[n, 0:size, :] = grad[pl.ds(m * size, size), other].astype(jnp.bfloat16)
        send_ref[n, size:, :] = words


def final_kernel(
    pieces, planes, meta, mine_ref, other_ref, stab_ref, small_ref, conv_out, stab_out,
    bit_out, keep_out, query_out, read_out, loss_out,
):
    for g in range(4):
        bit_out[:, g * CH : (g + 1) * CH] = small_ref[g : g + 1, :]
    keep_out[...] = small_ref[4:5, :]
    query_out[...] = small_ref[5:6, :]
    read_out[...] = small_ref[6:7, :]
    loss_out[...] = small_ref[7:8, 0:1]
    core = meta[1]
    per = pieces // 4
    size = 9 * CH // per
    for n in range(pieces // 2):
        g, m = n // per, n % per
        mine = pl.ds(pl.multiple_of((2 * core + g) * CH, CH), CH)
        other = pl.ds(pl.multiple_of((2 - 2 * core + g) * CH, CH), CH)
        conv_out[pl.ds(m * size, size), mine] = mine_ref[n].astype(jnp.float32)
        conv_out[pl.ds(m * size, size), other] = other_ref[n].astype(jnp.float32)
    rows = 2 * COLS // planes
    for z in range(planes):
        for g in range(4):
            stab_out[pl.ds(z * rows, rows), g * CH : (g + 1) * CH] = stab_ref[
                z, pl.ds(g * rows, rows)
            ].astype(jnp.float32)


GATES = pltpu.VMEM((ROUNDS, MID, 5 * CH), jnp.float32)


def f32(*shape):
    return jax.ShapeDtypeStruct(shape, jnp.float32)


def b16(*shape):
    return jax.ShapeDtypeStruct(shape, jnp.bfloat16)


def call(kernel, in_specs, out_shape, out_specs, scratch, flops):
    return pl.pallas_call(
        kernel,
        in_specs=in_specs,
        out_shape=out_shape,
        out_specs=out_specs,
        scratch_shapes=scratch,
        cost_estimate=pl.CostEstimate(flops=flops, bytes_accessed=4_000_000, transcendentals=0),
        compiler_params=pltpu.CompilerParams(vmem_limit_bytes=24 * 1024 * 1024),
    )


def segment_scratch(extra):
    return [
        pltpu.VMEM((MID, CH), jnp.float32),
        pltpu.VMEM((MID, CH), jnp.float32),
        pltpu.VMEM((14 * COLS, UNITS), jnp.bfloat16),
        *extra,
    ]


def per_device(
    syndromes, labels, stab_gate, bit_gate, forget_bias, conv_weight, query, readout_weight
):
    tiles = lax.axis_size("tiles")
    planes = lax.axis_size("rounds")
    tile = lax.axis_index("tiles")
    core = tile & 1
    lattice = 2 * tiles
    label = jnp.where(core == 0, labels[0, 0], labels[1, 0])
    meta = jnp.stack([tile // 2, core, label]).astype(jnp.int32)
    weights = conv_weight.reshape(9 * CH, UNITS)
    bit_row = bit_gate.reshape(1, UNITS)
    forget_row = forget_bias.reshape(1, CH)
    query_row = query.reshape(1, CH)
    read_row = readout_weight.reshape(1, CH)

    words = jnp.swapaxes(syndromes[:, :, 0], 0, 1).astype(jnp.bfloat16).reshape(16, 2 * COLS)
    words = jnp.pad(words, ((0, 0), (0, UNITS - 2 * COLS)))
    own = jnp.concatenate([stab_gate.reshape(2 * COLS, UNITS), words], axis=0)
    near = [shift(own, "tiles", step) for step in (4, 2)]
    far = [shift(own, "tiles", step) for step in (-2, -4)]
    mine = jnp.stack(near + [own] + far)
    theirs = swap(mine, "tiles", 1)

    gates, hist, stats, bits = call(
        functools.partial(forward_kernel, lattice),
        [SMEM, ANY, ANY, VMEM, VMEM, VMEM, VMEM],
        (GATES, b16(ROUNDS, 6 * COLS, 3 * CH), f32(8, CH), f32(2, 8, CH)),
        (VMEM, ANY, VMEM, VMEM),
        [
            pltpu.VMEM((EXT * COLS, UNITS), jnp.bfloat16),
            pltpu.VMEM((10, 16, UNITS), jnp.bfloat16),
            pltpu.VMEM((10, 8, CH), jnp.float32),
            pltpu.VMEM((EXT * COLS, CH), jnp.bfloat16),
            pltpu.VMEM((10 * CH, UNITS), jnp.bfloat16),
            pltpu.VMEM((2, (EXT + 2) * COLS, 3 * CH), jnp.bfloat16),
            pltpu.VMEM((EXT * COLS, CH), jnp.float32),
            pltpu.SemaphoreType.DMA((20,)),
            pltpu.SemaphoreType.DMA((2,)),
        ],
        8_000_000_000,
    )(meta, mine, theirs, weights, bit_row, forget_row, query_row)

    parts = [stats]
    for start, size in tile_groups(tiles):
        if len(parts) > 1:
            stats = call(
                add_kernel, [VMEM] * len(parts), f32(8, CH), VMEM, [], 1_000
            )(*parts)
        parts = [stats] + [swap(stats, "tiles", start * k) for k in range(1, size)]

    first = [7]
    half = 2 * COLS
    d_hid, d_cell, low, high, dp_one, small = call(
        functools.partial(first_backward, lattice, first, len(parts)),
        [SMEM] + [VMEM] * len(parts) + [VMEM, VMEM, VMEM, VMEM],
        (
            f32(CHUNK, CH), f32(CHUNK, CH), b16(half, 2 * CH), b16(half, 2 * CH),
            b16(1, CHUNK, UNITS), f32(8, CH),
        ),
        (VMEM,) * 6,
        segment_scratch([]),
        1_000_000_000,
    )(meta, *parts, query_row, read_row, weights, gates)

    below = shift(high, "tiles", 2)
    above = shift(low, "tiles", -2)
    middle = [6, 5]
    d_hid, d_cell, edge, dp_two = call(
        functools.partial(middle_backward, lattice, middle, 2),
        [SMEM] + [VMEM] * 6,
        (f32(CHUNK, CH), f32(CHUNK, CH), b16(CHUNK, 2 * CH), b16(2, CHUNK, UNITS)),
        (VMEM,) * 4,
        segment_scratch([]),
        2_000_000_000,
    )(meta, below, above, d_hid, d_cell, weights, gates)

    below = shift(edge, "tiles", 2)
    above = shift(edge, "tiles", -2)
    last = [4, 3, 2, 1, 0]
    dp_three, stab_mine, stab_other, small = call(
        functools.partial(last_backward, lattice, last, 4),
        [SMEM] + [VMEM] * 9,
        (b16(5, CHUNK, UNITS), f32(half, UNITS), b16(half, UNITS), f32(8, CH)),
        (VMEM,) * 4,
        segment_scratch([pltpu.VMEM((CHUNK, UNITS), jnp.float32)]),
        4_000_000_000,
    )(meta, below, above, d_hid, d_cell, weights, dp_one, dp_two, small, gates)

    size = 36 * CH // tiles
    chips = tiles // 2
    keep, send = call(
        functools.partial(weight_kernel, tiles),
        [SMEM, VMEM, VMEM, ANY, ANY, ANY, VMEM],
        (f32(chips, size + 8, CH), b16(chips, size + 16, CH)),
        (VMEM, VMEM),
        [
            pltpu.VMEM((ROUNDS, CHUNK, UNITS), jnp.bfloat16),
            pltpu.VMEM((9 * CH, UNITS), jnp.float32),
            pltpu.VMEM((8, UNITS), jnp.float32),
            pltpu.SemaphoreType.DMA((ROUNDS,)),
        ],
        3_000_000_000,
    )(meta, bits, small, dp_one, dp_two, dp_three, hist)
    send, stab_other = lax.optimization_barrier((send, stab_other))
    back = swap(send, "tiles", 1).astype(jnp.float32)
    words = split_words((keep[:, size:] + back[:, size : size + 8] + back[:, size + 8 :])[0])
    message = jnp.concatenate(
        [
            (keep[:, :size] + back[:, :size]).astype(jnp.bfloat16),
            jnp.broadcast_to(words[None], (chips,) + words.shape),
        ],
        axis=1,
    )
    sides = [list(range(side, tiles, 2)) for side in range(2)]
    back = lax.all_to_all(
        message, "tiles", 0, 0, axis_index_groups=sides, tiled=True
    ).astype(jnp.float32)
    piece = jnp.sum(back[:, :size], axis=0)
    small = jnp.sum(back[:, size : size + 8] + back[:, size + 8 :], axis=0)

    stab = stab_mine + swap(stab_other, "tiles", 1).astype(jnp.float32)
    rows = half // planes
    stab = jnp.swapaxes(stab.astype(jnp.bfloat16).reshape(planes, rows, 4, CH), 1, 2)
    stab = stab.reshape(planes, 4 * rows, CH)
    part = size // planes
    words = split_words(small)
    joint = jnp.concatenate(
        [
            stab,
            jnp.broadcast_to(words[None], (planes,) + words.shape),
            piece.astype(jnp.bfloat16).reshape(planes, part, CH),
        ],
        axis=1,
    )
    joint = lax.all_to_all(joint, "rounds", 0, 0, tiled=True).astype(jnp.float32)
    lines = 4 * rows
    small = jnp.sum(joint[:, lines : lines + 8] + joint[:, lines + 8 : lines + 16], axis=0)
    done = jnp.concatenate(
        [jnp.sum(joint[:, :lines], axis=0), jnp.sum(joint[:, lines + 16 :], axis=0)], axis=0
    ).astype(jnp.bfloat16)
    joint = lax.all_to_all(
        jnp.broadcast_to(done[None], (planes,) + done.shape), "rounds", 0, 0, tiled=True
    )
    stab_all = joint[:, :lines]
    piece = joint[:, lines:].reshape(size, CH)
    piece = lax.all_to_all(
        jnp.broadcast_to(piece[None], (chips, size, CH)), "tiles", 0, 0,
        axis_index_groups=sides, tiled=True,
    )
    other = swap(piece, "tiles", 1)
    grad_conv, grad_stab, grad_bit, grad_keep, grad_query, grad_read, loss = call(
        functools.partial(final_kernel, tiles, planes),
        [SMEM, VMEM, VMEM, VMEM, VMEM],
        (f32(9 * CH, UNITS), f32(half, UNITS), f32(1, UNITS), f32(1, CH), f32(1, CH), f32(1, CH), f32(1, 1)),
        (VMEM,) * 7,
        [],
        1_000_000,
    )(meta, piece, other, stab_all, small)
    return (
        grad_conv.reshape(3, 3, CH, UNITS),
        grad_stab.reshape(2, COLS, UNITS),
        grad_bit.reshape(UNITS),
        grad_keep.reshape(CH),
        grad_query.reshape(CH),
        grad_read.reshape(CH),
        loss.reshape(()),
    )


def solution(mesh):
    in_specs = (
        P(None, None, "rounds", "tiles", None),
        P(None, "rounds"),
        P("tiles", None, None),
        P(),
        P(),
        P(),
        P(),
        P(),
    )
    out_specs = (P(), P("tiles", None, None), P(), P(), P(), P(), P())
    return jax.shard_map(
        per_device, mesh=mesh, in_specs=in_specs, out_specs=out_specs, check_vma=False
    )
```

```python
import functools
import math

import jax
import jax.numpy as jnp
from jax import lax
from jax.experimental import pallas as pl
from jax.experimental.pallas import tpu as pltpu
from jax.sharding import PartitionSpec as P


COLS = 64
CH = 128
UNITS = 512
ROUNDS = 8
OWN = 4
HALO = 8
EXT = OWN + 2 * HALO
CHUNK = 4 * COLS
MID = 12 * COLS
SCALE = 1.0 / math.sqrt(CH)
VMEM = pl.BlockSpec(memory_space=pltpu.VMEM)
SMEM = pl.BlockSpec(memory_space=pltpu.SMEM)
ANY = pl.BlockSpec(memory_space=pl.ANY)
HBM = pl.BlockSpec(memory_space=pltpu.HBM)


def swap(values, axis, mask):
    count = lax.axis_size(axis)
    return lax.ppermute(values, axis, [(i, i ^ mask) for i in range(count)])


def shift(values, axis, step):
    count = lax.axis_size(axis)
    return lax.ppermute(values, axis, [(i, (i + step) % count) for i in range(count)])


def tree_sum(parts):
    while len(parts) > 1:
        parts = [parts[i] + parts[i + 1] for i in range(0, len(parts), 2)]
    return parts[0]


def tile_groups(count):
    groups = []
    start = 2
    while start < count:
        size = min(4, count // start)
        groups.append((start, size))
        start *= size
    return groups


def split_words(values):
    high = values.astype(jnp.bfloat16)
    low = (values - high.astype(jnp.float32)).astype(jnp.bfloat16)
    return jnp.concatenate([high, low], axis=0)


def gate(values):
    return 0.5 * jnp.tanh(0.5 * values) + 0.5


def rows_inside(meta, first, shape, lattice):
    site = lax.broadcasted_iota(jnp.int32, shape, 0)
    low = (HALO - OWN * meta[0] - first) * COLS
    return jnp.logical_and(site >= low, site < low + lattice * COLS)


def column_of(shape):
    return lax.broadcasted_iota(jnp.int32, shape, 0) & (COLS - 1)


def forward_kernel(lattice, meta, *refs):
    mine, theirs = refs[0:5], refs[5:10]
    (
        w_ref, par_ref, gates_out, hist_out, stats_out, bits_out, w_all,
        stab, raw, bits, fired, hc, cell, in_sem, hist_sem, w_sem,
    ) = refs[10:]
    core = meta[1]
    copies = []
    for k in range(5):
        for side, ref in ((core, mine[k]), (1 - core, theirs[k])):
            n = len(copies)
            copies.append(
                pltpu.make_async_copy(
                    ref.at[pl.ds(0, 2 * COLS)],
                    stab.at[pl.ds(pl.multiple_of(k * CHUNK + side * 2 * COLS, 2 * COLS), 2 * COLS)],
                    in_sem.at[n],
                )
            )
            copies.append(
                pltpu.make_async_copy(
                    ref.at[pl.ds(2 * COLS, 16)], raw.at[2 * k + side], in_sem.at[n + 1]
                )
            )
    w_copy = pltpu.make_async_copy(w_ref, w_all.at[pl.ds(0, 9 * CH)], w_sem.at[0])
    w_copy.start()
    for copy in copies:
        copy.start()
    edge = jnp.zeros((COLS, 3 * CH), jnp.bfloat16)
    for slot in range(2):
        hc[slot, pl.ds(0, COLS)] = edge
        hc[slot, pl.ds((EXT + 1) * COLS, COLS)] = edge
    cell[...] = jnp.zeros_like(cell)
    for copy in copies:
        copy.wait()
    for i in range(10):
        words = raw[i].astype(jnp.float32)
        bits[i] = jnp.where(core == 0, words[0:8, 0:CH], words[8:16, 0:CH])
    for i in range(2):
        bits_out[i] = bits[HALO // 2 + i]
    lane = lax.broadcasted_iota(jnp.int32, (8, CH), 1)
    spread = jnp.logical_and((lane & 7) == lax.broadcasted_iota(jnp.int32, (8, CH), 0), lane < 24)
    spread = spread.astype(jnp.float32)
    ones = jnp.logical_and(lane[0:1] >= 24, lane[0:1] < 27).astype(jnp.float32)
    for i in range(10):
        columns = lax.dot_general(
            bits[i], spread, (((0,), (0,)), ((), ())), preferred_element_type=jnp.float32
        )
        fired[pl.ds(i * CH, CH)] = (columns + ones).astype(jnp.bfloat16)
    rest_bit = jnp.concatenate([par_ref[g : g + 1, :] for g in range(4)], axis=1)
    rest_keep = jnp.concatenate(
        [jnp.zeros((1, CH), jnp.float32), par_ref[4:5, :], jnp.zeros((1, 2 * CH), jnp.float32)],
        axis=1,
    )
    sink = []
    for w in range(3):
        word = rest_bit.astype(jnp.bfloat16).astype(jnp.float32)
        rest_bit = rest_bit - word
        sink.append(jnp.broadcast_to(word, (8, UNITS)))
    place = lax.broadcasted_iota(jnp.int32, (8, UNITS), 0)
    last = jnp.zeros((8, UNITS), jnp.float32)
    for w in range(3):
        word = rest_keep.astype(jnp.bfloat16).astype(jnp.float32)
        rest_keep = rest_keep - word
        last = jnp.where(place == w, word, last)
    sink.append(last)
    sink.append(jnp.zeros((CH - 32, UNITS), jnp.float32))
    w_all[pl.ds(9 * CH, CH)] = jnp.concatenate(sink, axis=0).astype(jnp.bfloat16)

    def hist_copy(t):
        return pltpu.make_async_copy(
            hc.at[t % 2, pl.ds(8 * COLS, 6 * COLS)], hist_out.at[t], hist_sem.at[t % 2]
        )

    def run_round(t, first):
        low = 0 if first else (t // 2) * 2
        count = 5 if first else 5 - t // 2
        now = 0 if first else t % 2
        lane = lax.broadcasted_iota(jnp.int32, (1, CH), 1)
        wanted = jnp.logical_or((lane & 7) == t, lane >= 24).astype(jnp.bfloat16)

        def chunk(i, carry):
            row = low + 4 * i
            at = pl.multiple_of(row * COLS, 2 * COLS)
            pre = stab[pl.ds(at, CHUNK)].astype(jnp.float32)
            extra = fired[pl.ds(at, CHUNK)] * wanted
            if not first:
                taps = jnp.concatenate(
                    [
                        hc[1 - now, pl.ds(pl.multiple_of((row + a) * COLS, COLS), CHUNK)]
                        for a in range(3)
                    ]
                    + [extra],
                    axis=1,
                )
                pre = pre + jnp.dot(taps, w_all[...], preferred_element_type=jnp.float32)
            else:
                pre = pre + jnp.dot(
                    extra, w_all[pl.ds(9 * CH, CH)], preferred_element_type=jnp.float32
                )
            g_in = gate(pre[:, 0:CH])
            g_keep = gate(pre[:, CH : 2 * CH])
            g_new = jnp.tanh(pre[:, 2 * CH : 3 * CH])
            g_out = gate(pre[:, 3 * CH :])
            c_new = g_keep * cell[pl.ds(at, CHUNK)] + g_in * g_new
            cell[pl.ds(at, CHUNK)] = c_new
            for p in range(2):
                part = slice(p * 2 * COLS, (p + 1) * 2 * COLS)

                @pl.when(jnp.logical_and(row + 2 * p >= 4, row + 2 * p < 16))
                def _(p=p, part=part):
                    to = pl.ds(pl.multiple_of((row + 2 * p - 4) * COLS, 2 * COLS), 2 * COLS)
                    gates_out[t, to, 0:CH] = g_in[part]
                    gates_out[t, to, CH : 2 * CH] = g_keep[part]
                    gates_out[t, to, 2 * CH : 3 * CH] = g_new[part]
                    gates_out[t, to, 3 * CH : 4 * CH] = g_out[part]
                    gates_out[t, to, 4 * CH :] = c_new[part]

            shape = (CHUNK, CH)
            hidden = jnp.where(
                rows_inside(meta, row, shape, lattice), g_out * jnp.tanh(c_new), 0.0
            )
            col = column_of(shape)
            left = jnp.where(col == 0, 0.0, pltpu.roll(hidden, 1, 0))
            right = jnp.where(col == COLS - 1, 0.0, pltpu.roll(hidden, CHUNK - 1, 0))
            to = pl.multiple_of((row + 1) * COLS, COLS)
            hc[now, pl.ds(to, CHUNK), 0:CH] = left.astype(jnp.bfloat16)
            hc[now, pl.ds(to, CHUNK), CH : 2 * CH] = hidden.astype(jnp.bfloat16)
            hc[now, pl.ds(to, CHUNK), 2 * CH :] = right.astype(jnp.bfloat16)
            return carry

        lax.fori_loop(0, count, chunk, 0)
        hist_copy(t).start()

    run_round(0, True)
    w_copy.wait()

    def later(t, carry):
        @pl.when(t >= 2)
        def _():
            hist_copy(t - 2).wait()

        run_round(t, False)
        return carry

    lax.fori_loop(1, ROUNDS, later, 0)
    hidden = hc[1, pl.ds((HALO + 1) * COLS, CHUNK), CH : 2 * CH].astype(jnp.float32)
    weight = jnp.exp(jnp.sum(hidden * par_ref[5:6, :], axis=1, keepdims=True) * SCALE)
    stats_out[...] = jnp.zeros_like(stats_out)
    stats_out[0:1, :] = jnp.sum(weight * hidden, axis=0, keepdims=True)
    stats_out[1:2, :] = jnp.broadcast_to(jnp.sum(weight, axis=0, keepdims=True), (1, CH))
    for t in (ROUNDS - 2, ROUNDS - 1):
        hist_copy(t).wait()


def backward_rounds(lattice, meta, rounds, w_ref, gates, d_hid, d_cell, d_pre, dp_out):
    last = rounds[-1]
    edge = jnp.zeros((COLS, UNITS), jnp.bfloat16)
    d_pre[pl.ds(0, COLS)] = edge
    d_pre[pl.ds(13 * COLS, COLS)] = edge
    for slot, t in enumerate(rounds):

        def adjoint(i, carry, t=t):
            at = pl.ds(pl.multiple_of(i * CHUNK, CHUNK), CHUNK)
            g_in = gates[t, at, 0:CH]
            g_keep = gates[t, at, CH : 2 * CH]
            g_new = gates[t, at, 2 * CH : 3 * CH]
            g_out = gates[t, at, 3 * CH : 4 * CH]
            squash = jnp.tanh(gates[t, at, 4 * CH :])
            dh = d_hid[at]
            total = d_cell[at] + dh * g_out * (1.0 - squash * squash)
            d_cell[at] = total * g_keep
            to = pl.ds(pl.multiple_of(i * CHUNK + COLS, COLS), CHUNK)
            d_pre[to, 0:CH] = (total * g_new * g_in * (1.0 - g_in)).astype(jnp.bfloat16)
            if t > 0:
                c_old = gates[t - 1, at, 4 * CH :]
                keep = (total * c_old * g_keep * (1.0 - g_keep)).astype(jnp.bfloat16)
            else:
                keep = jnp.zeros((CHUNK, CH), jnp.bfloat16)
            d_pre[to, CH : 2 * CH] = keep
            d_pre[to, 2 * CH : 3 * CH] = (total * g_in * (1.0 - g_new * g_new)).astype(jnp.bfloat16)
            d_pre[to, 3 * CH :] = (dh * squash * g_out * (1.0 - g_out)).astype(jnp.bfloat16)
            return carry

        def spread(i, carry):
            total = None
            for a in range(3):
                part = lax.dot_general(
                    d_pre[pl.ds(pl.multiple_of(i * CHUNK + (2 - a) * COLS, COLS), CHUNK)],
                    w_ref[pl.ds(a * 3 * CH, 3 * CH)],
                    (((1,), (1,)), ((), ())),
                    preferred_element_type=jnp.float32,
                )
                total = part if total is None else total + part
            shape = (CHUNK, CH)
            col = column_of(shape)
            ahead = jnp.where(col == COLS - 1, 0.0, pltpu.roll(total[:, 0:CH], CHUNK - 1, 0))
            behind = jnp.where(col == 0, 0.0, pltpu.roll(total[:, 2 * CH :], 1, 0))
            dh = total[:, CH : 2 * CH] + ahead + behind
            inside = rows_inside(meta, 4 + 4 * i, shape, lattice)
            d_hid[pl.ds(pl.multiple_of(i * CHUNK, CHUNK), CHUNK)] = jnp.where(inside, dh, 0.0)
            return carry

        if t == 0:
            adjoint(1, 0)
        else:
            lax.fori_loop(0, 3, adjoint, 0)
        dp_out[slot] = d_pre[pl.ds(CHUNK + COLS, CHUNK)]
        if t > 0:
            if t == last or t == 1:
                spread(1, 0)
            else:
                lax.fori_loop(0, 3, spread, 0)


def first_backward(
    lattice, rounds, parts, meta, *refs
):
    stat_refs = refs[:parts]
    (par_ref, w_ref, gates, hid_out, cell_out, low_out, high_out, dp_out, small_out,
     d_hid, d_cell, d_pre) = refs[parts:]
    sums = tree_sum([ref[...] for ref in stat_refs])
    total = sums[1:2, :]
    pooled = sums[0:1, :] / total
    read = par_ref[6:7, :]
    query = par_ref[5:6, :]
    logit = jnp.sum(pooled * read, axis=1, keepdims=True)
    label = meta[2].astype(jnp.float32)
    loss = jnp.maximum(logit, 0.0) + jnp.log1p(jnp.exp(-jnp.abs(logit))) - label * logit
    d_logit = 1.0 / (1.0 + jnp.exp(-logit)) - label
    d_pooled = d_logit * read
    spare = jnp.sum(pooled * d_pooled, axis=1, keepdims=True)
    lead = meta[0] == 0
    small_out[...] = jnp.zeros_like(small_out)
    for i in range(3):
        at = pl.ds(i * CHUNK, CHUNK)
        hidden = gates[rounds[0], at, 3 * CH : 4 * CH] * jnp.tanh(gates[rounds[0], at, 4 * CH :])
        hidden = hidden.astype(jnp.bfloat16).astype(jnp.float32)
        weight = jnp.exp(jnp.sum(hidden * query, axis=1, keepdims=True) * SCALE) / total[:, 0:1]
        d_score = weight * (jnp.sum(hidden * d_pooled, axis=1, keepdims=True) - spare)
        grad = weight * d_pooled + d_score * (query * SCALE)
        inside = rows_inside(meta, 4 + 4 * i, (CHUNK, CH), lattice)
        d_hid[at] = jnp.where(inside, grad, 0.0)
        if i == 1:
            small_out[5:6, :] = SCALE * jnp.sum(d_score * hidden, axis=0, keepdims=True)
    d_cell[...] = jnp.zeros_like(d_cell)
    lane = lax.broadcasted_iota(jnp.int32, (1, CH), 1)
    small_out[6:7, :] = jnp.where(lead, d_logit * pooled, 0.0)
    small_out[7:8, :] = jnp.where(jnp.logical_and(lead, lane == 0), loss, 0.0)
    backward_rounds(lattice, meta, rounds, w_ref, gates, d_hid, d_cell, d_pre, dp_out)
    own = pl.ds(CHUNK, CHUNK)
    hid_out[...] = d_hid[own]
    cell_out[...] = d_cell[own]
    for out, at in ((low_out, CHUNK), (high_out, CHUNK + 2 * COLS)):
        out[:, 0:CH] = d_hid[pl.ds(at, 2 * COLS)].astype(jnp.bfloat16)
        out[:, CH:] = d_cell[pl.ds(at, 2 * COLS)].astype(jnp.bfloat16)


def load_adjoint(meta, lattice, rows, below, above, hid_in, cell_in, d_hid, d_cell):
    size = rows * COLS
    blank = jnp.zeros((CHUNK, CH), jnp.float32)
    if rows < 4:
        for i in (0, 2):
            d_hid[pl.ds(i * CHUNK, CHUNK)] = blank
            d_cell[pl.ds(i * CHUNK, CHUNK)] = blank
    for first, ref in ((CHUNK - size, below), (2 * CHUNK, above)):
        inside = rows_inside(meta, 4 + first // COLS, (size, CH), lattice)
        d_hid[pl.ds(first, size)] = jnp.where(inside, ref[:, 0:CH].astype(jnp.float32), 0.0)
        d_cell[pl.ds(first, size)] = jnp.where(inside, ref[:, CH:].astype(jnp.float32), 0.0)
    d_hid[pl.ds(CHUNK, CHUNK)] = hid_in[...]
    d_cell[pl.ds(CHUNK, CHUNK)] = cell_in[...]


def middle_backward(
    lattice, rounds, rows, meta, below, above, hid_in, cell_in, w_ref, gates,
    hid_out, cell_out, edge_out, dp_out, d_hid, d_cell, d_pre,
):
    load_adjoint(meta, lattice, rows, below, above, hid_in, cell_in, d_hid, d_cell)
    backward_rounds(lattice, meta, rounds, w_ref, gates, d_hid, d_cell, d_pre, dp_out)
    own = pl.ds(CHUNK, CHUNK)
    hid_out[...] = d_hid[own]
    cell_out[...] = d_cell[own]
    edge_out[:, 0:CH] = d_hid[own].astype(jnp.bfloat16)
    edge_out[:, CH:] = d_cell[own].astype(jnp.bfloat16)


def last_backward(
    lattice, rounds, rows, meta, below, above, hid_in, cell_in, w_ref, dp_one, dp_two, small_in,
    gates, dp_out, mine_out, other_out, small_out, d_hid, d_cell, d_pre, total,
):
    load_adjoint(meta, lattice, rows, below, above, hid_in, cell_in, d_hid, d_cell)
    backward_rounds(lattice, meta, rounds, w_ref, gates, d_hid, d_cell, d_pre, dp_out)
    summed = None
    for ref, count in ((dp_one, 1), (dp_two, 2), (dp_out, len(rounds))):
        for i in range(count):
            part = ref[i].astype(jnp.float32)
            summed = part if summed is None else summed + part
    total[...] = summed
    core = meta[1]
    half = 2 * COLS
    mine_out[...] = total[pl.ds(pl.multiple_of(core * half, half), half)]
    other_out[...] = total[pl.ds(pl.multiple_of((1 - core) * half, half), half)].astype(jnp.bfloat16)
    small_out[...] = small_in[...]
    small_out[4:5, :] = jnp.sum(total[:, CH : 2 * CH], axis=0, keepdims=True)


def add_kernel(*refs):
    refs[-1][...] = tree_sum([ref[...] for ref in refs[:-1]])


def weight_half(side, dp_refs, hist_ref, dp, grad, dp_sem):
    copies = []
    for ref, low in zip(dp_refs, (7, 6, 4)):
        for i in range(ref.shape[0]):
            copies.append(pltpu.make_async_copy(ref.at[i], dp.at[low - i], dp_sem.at[low - i]))
    for copy in copies:
        copy.start()
    grad[...] = jnp.zeros_like(grad)
    for copy in copies:
        copy.wait()
    lanes = pl.ds(pl.multiple_of(side * 2 * CH, 2 * CH), 2 * CH)

    def add_round(t, carry):
        part = dp[t, :, lanes]
        for a in range(3):
            grad[pl.ds(a * 3 * CH, 3 * CH)] += lax.dot_general(
                hist_ref[t - 1, pl.ds(a * COLS, CHUNK)],
                part,
                (((0,), (0,)), ((), ())),
                preferred_element_type=jnp.float32,
            )
        return carry

    lax.fori_loop(1, ROUNDS, add_round, 0)


def send_kernel(
    pieces, meta, bits_ref, small_ref, dp_one, dp_two, dp_three, hist_ref, send_ref, both_ref,
    dp, grad, fired_sum, dp_sem,
):
    weight_half(1 - meta[1], (dp_one, dp_two, dp_three), hist_ref, dp, grad, dp_sem)
    word = jnp.concatenate([bits_ref[0], bits_ref[1]], axis=1)

    def add_fired(t, carry):
        rows = jnp.where(lax.broadcasted_iota(jnp.int32, word.shape, 0) == t, word, 0.0)
        fired_sum[...] += jnp.dot(
            rows.astype(jnp.bfloat16), dp[t], preferred_element_type=jnp.float32
        )
        return carry

    fired_sum[...] = jnp.zeros_like(fired_sum)
    lax.fori_loop(0, ROUNDS, add_fired, 0)
    fired = jnp.sum(fired_sum[...], axis=0, keepdims=True)
    rows = [fired[:, g * CH : (g + 1) * CH] for g in range(4)]
    words = split_words(jnp.concatenate(rows + [small_ref[4:8, :]], axis=0))
    both_ref[...] = words[0:8].astype(jnp.float32) + words[8:16].astype(jnp.float32)
    per = pieces // 4
    size = 9 * CH // per
    for n in range(pieces // 2):
        g, m = n // per, n % per
        part = grad[pl.ds(m * size, size), g * CH : (g + 1) * CH]
        send_ref[n, 0:size, :] = part.astype(jnp.bfloat16)
        send_ref[n, size:, :] = words


def keep_kernel(
    pieces, meta, dp_one, dp_two, dp_three, hist_ref, keep_ref, dp, grad, dp_sem
):
    weight_half(meta[1], (dp_one, dp_two, dp_three), hist_ref, dp, grad, dp_sem)
    per = pieces // 4
    size = 9 * CH // per
    for n in range(pieces // 2):
        g, m = n // per, n % per
        keep_ref[n] = grad[pl.ds(m * size, size), g * CH : (g + 1) * CH]


def final_kernel(
    pieces, planes, meta, mine_ref, other_ref, stab_ref, small_ref, conv_out, stab_out,
    bit_out, keep_out, query_out, read_out, loss_out,
):
    for g in range(4):
        bit_out[:, g * CH : (g + 1) * CH] = small_ref[g : g + 1, :]
    keep_out[...] = small_ref[4:5, :]
    query_out[...] = small_ref[5:6, :]
    read_out[...] = small_ref[6:7, :]
    loss_out[...] = small_ref[7:8, 0:1]
    core = meta[1]
    per = pieces // 4
    size = 9 * CH // per
    for n in range(pieces // 2):
        g, m = n // per, n % per
        mine = pl.ds(pl.multiple_of((2 * core + g) * CH, CH), CH)
        other = pl.ds(pl.multiple_of((2 - 2 * core + g) * CH, CH), CH)
        conv_out[pl.ds(m * size, size), mine] = mine_ref[n].astype(jnp.float32)
        conv_out[pl.ds(m * size, size), other] = other_ref[n].astype(jnp.float32)
    rows = 2 * COLS // planes
    for z in range(planes):
        for g in range(4):
            stab_out[pl.ds(z * rows, rows), g * CH : (g + 1) * CH] = stab_ref[
                z, pl.ds(g * rows, rows)
            ].astype(jnp.float32)


W_ALL = pltpu.VMEM((10 * CH, UNITS), jnp.bfloat16)
GATES = pltpu.VMEM((ROUNDS, MID, 5 * CH), jnp.float32)


def f32(*shape):
    return jax.ShapeDtypeStruct(shape, jnp.float32)


def b16(*shape):
    return jax.ShapeDtypeStruct(shape, jnp.bfloat16)


def call(kernel, in_specs, out_shape, out_specs, scratch, flops):
    return pl.pallas_call(
        kernel,
        in_specs=in_specs,
        out_shape=out_shape,
        out_specs=out_specs,
        scratch_shapes=scratch,
        cost_estimate=pl.CostEstimate(flops=flops, bytes_accessed=4_000_000, transcendentals=0),
        compiler_params=pltpu.CompilerParams(vmem_limit_bytes=24 * 1024 * 1024),
    )


def segment_scratch(extra):
    return [
        pltpu.VMEM((MID, CH), jnp.float32),
        pltpu.VMEM((MID, CH), jnp.float32),
        pltpu.VMEM((14 * COLS, UNITS), jnp.bfloat16),
        *extra,
    ]


def per_device(
    syndromes, labels, stab_gate, bit_gate, forget_bias, conv_weight, query, readout_weight
):
    tiles = lax.axis_size("tiles")
    planes = lax.axis_size("rounds")
    tile = lax.axis_index("tiles")
    core = tile & 1
    lattice = 2 * tiles
    label = jnp.where(core == 0, labels[0, 0], labels[1, 0])
    meta = jnp.stack([tile // 2, core, label]).astype(jnp.int32)
    weights = conv_weight.reshape(9 * CH, UNITS)
    params = jnp.concatenate(
        [bit_gate, forget_bias, query, readout_weight, jnp.zeros((CH,), jnp.float32)]
    ).reshape(8, CH)

    words = jnp.swapaxes(syndromes[:, :, 0], 0, 1).astype(jnp.bfloat16).reshape(16, 2 * COLS)
    words = jnp.pad(words, ((0, 0), (0, UNITS - 2 * COLS)))
    own = jnp.concatenate([stab_gate.reshape(2 * COLS, UNITS), words], axis=0)
    near = [shift(own, "tiles", step) for step in (4, 2)]
    far = [shift(own, "tiles", step) for step in (-2, -4)]
    mine = near + [own] + far
    theirs = [swap(piece, "tiles", 1) for piece in mine]

    gates, hist, stats, bits, w_all = call(
        functools.partial(forward_kernel, lattice),
        [SMEM] + [ANY] * 10 + [HBM, VMEM],
        (GATES, b16(ROUNDS, 6 * COLS, 3 * CH), f32(8, CH), f32(2, 8, CH), W_ALL),
        (VMEM, ANY, VMEM, VMEM, VMEM),
        [
            pltpu.VMEM((EXT * COLS, UNITS), jnp.bfloat16),
            pltpu.VMEM((10, 16, UNITS), jnp.bfloat16),
            pltpu.VMEM((10, 8, CH), jnp.float32),
            pltpu.VMEM((EXT * COLS, CH), jnp.bfloat16),
            pltpu.VMEM((2, (EXT + 2) * COLS, 3 * CH), jnp.bfloat16),
            pltpu.VMEM((EXT * COLS, CH), jnp.float32),
            pltpu.SemaphoreType.DMA((20,)),
            pltpu.SemaphoreType.DMA((2,)),
            pltpu.SemaphoreType.DMA((1,)),
        ],
        8_000_000_000,
    )(meta, *mine, *theirs, pltpu.with_memory_space_constraint(weights, pltpu.HBM), params)

    parts = [stats]
    for start, size in tile_groups(tiles):
        if len(parts) > 1:
            stats = call(
                add_kernel, [VMEM] * len(parts), f32(8, CH), VMEM, [], 1_000
            )(*parts)
        parts = [stats] + [swap(stats, "tiles", start * k) for k in range(1, size)]

    first = [7]
    half = 2 * COLS
    d_hid, d_cell, low, high, dp_one, small = call(
        functools.partial(first_backward, lattice, first, len(parts)),
        [SMEM] + [VMEM] * len(parts) + [VMEM, VMEM, VMEM],
        (
            f32(CHUNK, CH), f32(CHUNK, CH), b16(half, 2 * CH), b16(half, 2 * CH),
            b16(1, CHUNK, UNITS), f32(8, CH),
        ),
        (VMEM,) * 6,
        segment_scratch([]),
        1_000_000_000,
    )(meta, *parts, params, w_all, gates)

    below = shift(high, "tiles", 2)
    above = shift(low, "tiles", -2)
    middle = [6, 5]
    d_hid, d_cell, edge, dp_two = call(
        functools.partial(middle_backward, lattice, middle, 2),
        [SMEM] + [VMEM] * 6,
        (f32(CHUNK, CH), f32(CHUNK, CH), b16(CHUNK, 2 * CH), b16(2, CHUNK, UNITS)),
        (VMEM,) * 4,
        segment_scratch([]),
        2_000_000_000,
    )(meta, below, above, d_hid, d_cell, w_all, gates)

    below = shift(edge, "tiles", 2)
    above = shift(edge, "tiles", -2)
    last = [4, 3, 2, 1, 0]
    dp_three, stab_mine, stab_other, small = call(
        functools.partial(last_backward, lattice, last, 4),
        [SMEM] + [VMEM] * 9,
        (b16(5, CHUNK, UNITS), f32(half, UNITS), b16(half, UNITS), f32(8, CH)),
        (VMEM,) * 4,
        segment_scratch([pltpu.VMEM((CHUNK, UNITS), jnp.float32)]),
        4_000_000_000,
    )(meta, below, above, d_hid, d_cell, w_all, dp_one, dp_two, small, gates)

    size = 36 * CH // tiles
    chips = tiles // 2
    scratch = [
        pltpu.VMEM((ROUNDS, CHUNK, UNITS), jnp.bfloat16),
        pltpu.VMEM((9 * CH, 2 * CH), jnp.float32),
    ]
    send, both = call(
        functools.partial(send_kernel, tiles),
        [SMEM, VMEM, VMEM, ANY, ANY, ANY, VMEM],
        (b16(chips, size + 16, CH), f32(8, CH)),
        (VMEM, VMEM),
        scratch + [pltpu.VMEM((8, UNITS), jnp.float32), pltpu.SemaphoreType.DMA((ROUNDS,))],
        1_500_000_000,
    )(meta, bits, small, dp_one, dp_two, dp_three, hist)
    send, stab_other = lax.optimization_barrier((send, stab_other))
    back = swap(send, "tiles", 1).astype(jnp.float32)
    keep = call(
        functools.partial(keep_kernel, tiles),
        [SMEM, ANY, ANY, ANY, VMEM],
        f32(chips, size, CH),
        VMEM,
        scratch + [pltpu.SemaphoreType.DMA((ROUNDS,))],
        3_000_000_000,
    )(meta, dp_one, dp_two, dp_three, hist)
    words = split_words(both + back[0, size : size + 8] + back[0, size + 8 :])
    message = jnp.concatenate(
        [
            (keep + back[:, :size]).astype(jnp.bfloat16),
            jnp.broadcast_to(words[None], (chips,) + words.shape),
        ],
        axis=1,
    )
    sides = [list(range(side, tiles, 2)) for side in range(2)]
    back = lax.all_to_all(
        message, "tiles", 0, 0, axis_index_groups=sides, tiled=True
    ).astype(jnp.float32)
    piece = jnp.sum(back[:, :size], axis=0)
    small = jnp.sum(back[:, size : size + 8] + back[:, size + 8 :], axis=0)

    stab = stab_mine + swap(stab_other, "tiles", 1).astype(jnp.float32)
    rows = half // planes
    stab = jnp.swapaxes(stab.astype(jnp.bfloat16).reshape(planes, rows, 4, CH), 1, 2)
    stab = stab.reshape(planes, 4 * rows, CH)
    part = size // planes
    words = split_words(small)
    joint = jnp.concatenate(
        [
            stab,
            jnp.broadcast_to(words[None], (planes,) + words.shape),
            piece.astype(jnp.bfloat16).reshape(planes, part, CH),
        ],
        axis=1,
    )
    joint = lax.all_to_all(joint, "rounds", 0, 0, tiled=True).astype(jnp.float32)
    lines = 4 * rows
    small = jnp.sum(joint[:, lines : lines + 8] + joint[:, lines + 8 : lines + 16], axis=0)
    done = jnp.concatenate(
        [jnp.sum(joint[:, :lines], axis=0), jnp.sum(joint[:, lines + 16 :], axis=0)], axis=0
    ).astype(jnp.bfloat16)
    joint = lax.all_to_all(
        jnp.broadcast_to(done[None], (planes,) + done.shape), "rounds", 0, 0, tiled=True
    )
    stab_all = joint[:, :lines]
    piece = joint[:, lines:].reshape(size, CH)
    piece = lax.all_to_all(
        jnp.broadcast_to(piece[None], (chips, size, CH)), "tiles", 0, 0,
        axis_index_groups=sides, tiled=True,
    )
    other = swap(piece, "tiles", 1)
    grad_conv, grad_stab, grad_bit, grad_keep, grad_query, grad_read, loss = call(
        functools.partial(final_kernel, tiles, planes),
        [SMEM, VMEM, VMEM, VMEM, VMEM],
        (f32(9 * CH, UNITS), f32(half, UNITS), f32(1, UNITS), f32(1, CH), f32(1, CH), f32(1, CH), f32(1, 1)),
        (VMEM,) * 7,
        [],
        1_000_000,
    )(meta, piece, other, stab_all, small)
    return (
        grad_conv.reshape(3, 3, CH, UNITS),
        grad_stab.reshape(2, COLS, UNITS),
        grad_bit.reshape(UNITS),
        grad_keep.reshape(CH),
        grad_query.reshape(CH),
        grad_read.reshape(CH),
        loss.reshape(()),
    )


def solution(mesh):
    in_specs = (
        P(None, None, "rounds", "tiles", None),
        P(None, "rounds"),
        P("tiles", None, None),
        P(),
        P(),
        P(),
        P(),
        P(),
    )
    out_specs = (P(), P("tiles", None, None), P(), P(), P(), P(), P())
    return jax.shard_map(
        per_device, mesh=mesh, in_specs=in_specs, out_specs=out_specs, check_vma=False
    )
```

```python
import functools
import math

import jax
import jax.numpy as jnp
from jax import lax
from jax.experimental import pallas as pl
from jax.experimental.pallas import tpu as pltpu
from jax.sharding import PartitionSpec as P


COLS = 64
CH = 128
UNITS = 512
ROUNDS = 8
OWN = 4
HALO = 8
EXT = OWN + 2 * HALO
CHUNK = 4 * COLS
MID = 12 * COLS
SCALE = 1.0 / math.sqrt(CH)
VMEM = pl.BlockSpec(memory_space=pltpu.VMEM)
SMEM = pl.BlockSpec(memory_space=pltpu.SMEM)
ANY = pl.BlockSpec(memory_space=pl.ANY)


def swap(values, axis, mask):
    count = lax.axis_size(axis)
    return lax.ppermute(values, axis, [(i, i ^ mask) for i in range(count)])


def shift(values, axis, step):
    count = lax.axis_size(axis)
    return lax.ppermute(values, axis, [(i, (i + step) % count) for i in range(count)])


def tree_sum(parts):
    while len(parts) > 1:
        parts = [parts[i] + parts[i + 1] for i in range(0, len(parts), 2)]
    return parts[0]


def tile_groups(count):
    groups = []
    start = 2
    while start < count:
        size = min(4, count // start)
        groups.append((start, size))
        start *= size
    return groups


def split_words(values):
    high = values.astype(jnp.bfloat16)
    low = (values - high.astype(jnp.float32)).astype(jnp.bfloat16)
    return jnp.concatenate([high, low], axis=0)


def gate(values):
    return 0.5 * jnp.tanh(0.5 * values) + 0.5


def rows_inside(meta, first, shape, lattice):
    site = lax.broadcasted_iota(jnp.int32, shape, 0)
    low = (HALO - OWN * meta[0] - first) * COLS
    return jnp.logical_and(site >= low, site < low + lattice * COLS)


def column_of(shape):
    return lax.broadcasted_iota(jnp.int32, shape, 0) & (COLS - 1)


def forward_kernel(
    lattice, meta, a_ref, b_ref, w_ref, bit_ref, forget_ref, q_ref,
    gates_out, hist_out, stats_out, bits_out,
    stab, raw, bits, fired, w_all, hc, cell, in_sem, hist_sem,
):
    core = meta[1]
    copies = []
    for k in range(5):
        for side, ref in ((core, a_ref), (1 - core, b_ref)):
            n = len(copies)
            copies.append(
                pltpu.make_async_copy(
                    ref.at[k, pl.ds(0, 2 * COLS)],
                    stab.at[pl.ds(pl.multiple_of(k * CHUNK + side * 2 * COLS, 2 * COLS), 2 * COLS)],
                    in_sem.at[n],
                )
            )
            copies.append(
                pltpu.make_async_copy(
                    ref.at[k, pl.ds(2 * COLS, 8)], raw.at[2 * k + side], in_sem.at[n + 1]
                )
            )
    for copy in copies:
        copy.start()
    edge = jnp.zeros((COLS, 3 * CH), jnp.bfloat16)
    for slot in range(2):
        hc[slot, pl.ds(0, COLS)] = edge
        hc[slot, pl.ds((EXT + 1) * COLS, COLS)] = edge
    cell[...] = jnp.zeros_like(cell)
    for copy in copies:
        copy.wait()
    for i in range(10):
        words = raw[i].astype(jnp.float32)
        shot = jnp.where(core == 0, words[0:2], words[2:4])
        bits[i] = jnp.concatenate(
            [shot[t // 4 : t // 4 + 1, (t % 4) * CH : (t % 4 + 1) * CH] for t in range(8)], axis=0
        )
    for i in range(2):
        bits_out[i] = bits[HALO // 2 + i]
    lane = lax.broadcasted_iota(jnp.int32, (8, CH), 1)
    spread = jnp.logical_and((lane & 7) == lax.broadcasted_iota(jnp.int32, (8, CH), 0), lane < 24)
    spread = spread.astype(jnp.float32)
    ones = jnp.logical_and(lane[0:1] >= 24, lane[0:1] < 27).astype(jnp.float32)
    for i in range(10):
        columns = lax.dot_general(
            bits[i], spread, (((0,), (0,)), ((), ())), preferred_element_type=jnp.float32
        )
        fired[pl.ds(i * CH, CH)] = (columns + ones).astype(jnp.bfloat16)
    w_all[pl.ds(0, 9 * CH)] = w_ref[...]
    rest_bit = bit_ref[...]
    rest_keep = jnp.concatenate(
        [jnp.zeros((1, CH), jnp.float32), forget_ref[...], jnp.zeros((1, 2 * CH), jnp.float32)],
        axis=1,
    )
    sink = []
    for w in range(3):
        word = rest_bit.astype(jnp.bfloat16).astype(jnp.float32)
        rest_bit = rest_bit - word
        sink.append(jnp.broadcast_to(word, (8, UNITS)))
    place = lax.broadcasted_iota(jnp.int32, (8, UNITS), 0)
    last = jnp.zeros((8, UNITS), jnp.float32)
    for w in range(3):
        word = rest_keep.astype(jnp.bfloat16).astype(jnp.float32)
        rest_keep = rest_keep - word
        last = jnp.where(place == w, word, last)
    sink.append(last)
    sink.append(jnp.zeros((CH - 32, UNITS), jnp.float32))
    w_all[pl.ds(9 * CH, CH)] = jnp.concatenate(sink, axis=0).astype(jnp.bfloat16)

    def hist_copy(t):
        return pltpu.make_async_copy(
            hc.at[t % 2, pl.ds(8 * COLS, 6 * COLS)], hist_out.at[t], hist_sem.at[t % 2]
        )

    def run_round(t, first):
        low = 0 if first else (t // 2) * 2
        count = 5 if first else 5 - t // 2
        now = 0 if first else t % 2
        lane = lax.broadcasted_iota(jnp.int32, (1, CH), 1)
        wanted = jnp.logical_or((lane & 7) == t, lane >= 24).astype(jnp.bfloat16)

        def chunk(i, carry):
            row = low + 4 * i
            at = pl.multiple_of(row * COLS, 2 * COLS)
            pre = stab[pl.ds(at, CHUNK)].astype(jnp.float32)
            extra = fired[pl.ds(at, CHUNK)] * wanted
            if not first:
                taps = jnp.concatenate(
                    [
                        hc[1 - now, pl.ds(pl.multiple_of((row + a) * COLS, COLS), CHUNK)]
                        for a in range(3)
                    ]
                    + [extra],
                    axis=1,
                )
                pre = pre + jnp.dot(taps, w_all[...], preferred_element_type=jnp.float32)
            else:
                pre = pre + jnp.dot(
                    extra, w_all[pl.ds(9 * CH, CH)], preferred_element_type=jnp.float32
                )
            g_in = gate(pre[:, 0:CH])
            g_keep = gate(pre[:, CH : 2 * CH])
            g_new = jnp.tanh(pre[:, 2 * CH : 3 * CH])
            g_out = gate(pre[:, 3 * CH :])
            c_new = g_keep * cell[pl.ds(at, CHUNK)] + g_in * g_new
            cell[pl.ds(at, CHUNK)] = c_new
            for p in range(2):
                part = slice(p * 2 * COLS, (p + 1) * 2 * COLS)

                @pl.when(jnp.logical_and(row + 2 * p >= 4, row + 2 * p < 16))
                def _(p=p, part=part):
                    to = pl.ds(pl.multiple_of((row + 2 * p - 4) * COLS, 2 * COLS), 2 * COLS)
                    gates_out[t, to, 0:CH] = g_in[part]
                    gates_out[t, to, CH : 2 * CH] = g_keep[part]
                    gates_out[t, to, 2 * CH : 3 * CH] = g_new[part]
                    gates_out[t, to, 3 * CH : 4 * CH] = g_out[part]
                    gates_out[t, to, 4 * CH :] = c_new[part]

            shape = (CHUNK, CH)
            hidden = jnp.where(
                rows_inside(meta, row, shape, lattice), g_out * jnp.tanh(c_new), 0.0
            )
            col = column_of(shape)
            left = jnp.where(col == 0, 0.0, pltpu.roll(hidden, 1, 0))
            right = jnp.where(col == COLS - 1, 0.0, pltpu.roll(hidden, CHUNK - 1, 0))
            to = pl.multiple_of((row + 1) * COLS, COLS)
            hc[now, pl.ds(to, CHUNK), 0:CH] = left.astype(jnp.bfloat16)
            hc[now, pl.ds(to, CHUNK), CH : 2 * CH] = hidden.astype(jnp.bfloat16)
            hc[now, pl.ds(to, CHUNK), 2 * CH :] = right.astype(jnp.bfloat16)
            return carry

        lax.fori_loop(0, count, chunk, 0)
        hist_copy(t).start()

    run_round(0, True)

    def later(t, carry):
        @pl.when(t >= 2)
        def _():
            hist_copy(t - 2).wait()

        run_round(t, False)
        return carry

    lax.fori_loop(1, ROUNDS, later, 0)
    hidden = hc[1, pl.ds((HALO + 1) * COLS, CHUNK), CH : 2 * CH].astype(jnp.float32)
    weight = jnp.exp(jnp.sum(hidden * q_ref[...], axis=1, keepdims=True) * SCALE)
    stats_out[...] = jnp.zeros_like(stats_out)
    stats_out[0:1, :] = jnp.sum(weight * hidden, axis=0, keepdims=True)
    stats_out[1:2, :] = jnp.broadcast_to(jnp.sum(weight, axis=0, keepdims=True), (1, CH))
    for t in (ROUNDS - 2, ROUNDS - 1):
        hist_copy(t).wait()


def backward_rounds(lattice, meta, rounds, w_ref, gates, d_hid, d_cell, d_pre, dp_out):
    last = rounds[-1]
    edge = jnp.zeros((COLS, UNITS), jnp.bfloat16)
    d_pre[pl.ds(0, COLS)] = edge
    d_pre[pl.ds(13 * COLS, COLS)] = edge
    for slot, t in enumerate(rounds):

        def adjoint(i, carry, t=t):
            at = pl.ds(pl.multiple_of(i * CHUNK, CHUNK), CHUNK)
            g_in = gates[t, at, 0:CH]
            g_keep = gates[t, at, CH : 2 * CH]
            g_new = gates[t, at, 2 * CH : 3 * CH]
            g_out = gates[t, at, 3 * CH : 4 * CH]
            squash = jnp.tanh(gates[t, at, 4 * CH :])
            dh = d_hid[at]
            total = d_cell[at] + dh * g_out * (1.0 - squash * squash)
            d_cell[at] = total * g_keep
            to = pl.ds(pl.multiple_of(i * CHUNK + COLS, COLS), CHUNK)
            d_pre[to, 0:CH] = (total * g_new * g_in * (1.0 - g_in)).astype(jnp.bfloat16)
            if t > 0:
                c_old = gates[t - 1, at, 4 * CH :]
                keep = (total * c_old * g_keep * (1.0 - g_keep)).astype(jnp.bfloat16)
            else:
                keep = jnp.zeros((CHUNK, CH), jnp.bfloat16)
            d_pre[to, CH : 2 * CH] = keep
            d_pre[to, 2 * CH : 3 * CH] = (total * g_in * (1.0 - g_new * g_new)).astype(jnp.bfloat16)
            d_pre[to, 3 * CH :] = (dh * squash * g_out * (1.0 - g_out)).astype(jnp.bfloat16)
            return carry

        def spread(i, carry):
            total = None
            for a in range(3):
                part = lax.dot_general(
                    d_pre[pl.ds(pl.multiple_of(i * CHUNK + (2 - a) * COLS, COLS), CHUNK)],
                    w_ref[pl.ds(a * 3 * CH, 3 * CH)],
                    (((1,), (1,)), ((), ())),
                    preferred_element_type=jnp.float32,
                )
                total = part if total is None else total + part
            shape = (CHUNK, CH)
            col = column_of(shape)
            ahead = jnp.where(col == COLS - 1, 0.0, pltpu.roll(total[:, 0:CH], CHUNK - 1, 0))
            behind = jnp.where(col == 0, 0.0, pltpu.roll(total[:, 2 * CH :], 1, 0))
            dh = total[:, CH : 2 * CH] + ahead + behind
            inside = rows_inside(meta, 4 + 4 * i, shape, lattice)
            d_hid[pl.ds(pl.multiple_of(i * CHUNK, CHUNK), CHUNK)] = jnp.where(inside, dh, 0.0)
            return carry

        if t == 0:
            adjoint(1, 0)
        else:
            lax.fori_loop(0, 3, adjoint, 0)
        dp_out[slot] = d_pre[pl.ds(CHUNK + COLS, CHUNK)]
        if t > 0:
            if t == last or t == 1:
                spread(1, 0)
            else:
                lax.fori_loop(0, 3, spread, 0)


def first_backward(
    lattice, rounds, parts, meta, *refs
):
    stat_refs = refs[:parts]
    (q_ref, r_ref, w_ref, gates, hid_out, cell_out, low_out, high_out, dp_out, small_out,
     d_hid, d_cell, d_pre) = refs[parts:]
    sums = tree_sum([ref[...] for ref in stat_refs])
    total = sums[1:2, :]
    pooled = sums[0:1, :] / total
    read = r_ref[...]
    query = q_ref[...]
    logit = jnp.sum(pooled * read, axis=1, keepdims=True)
    label = meta[2].astype(jnp.float32)
    loss = jnp.maximum(logit, 0.0) + jnp.log1p(jnp.exp(-jnp.abs(logit))) - label * logit
    d_logit = 1.0 / (1.0 + jnp.exp(-logit)) - label
    d_pooled = d_logit * read
    spare = jnp.sum(pooled * d_pooled, axis=1, keepdims=True)
    lead = meta[0] == 0
    small_out[...] = jnp.zeros_like(small_out)
    for i in range(3):
        at = pl.ds(i * CHUNK, CHUNK)
        hidden = gates[rounds[0], at, 3 * CH : 4 * CH] * jnp.tanh(gates[rounds[0], at, 4 * CH :])
        hidden = hidden.astype(jnp.bfloat16).astype(jnp.float32)
        weight = jnp.exp(jnp.sum(hidden * query, axis=1, keepdims=True) * SCALE) / total[:, 0:1]
        d_score = weight * (jnp.sum(hidden * d_pooled, axis=1, keepdims=True) - spare)
        grad = weight * d_pooled + d_score * (query * SCALE)
        inside = rows_inside(meta, 4 + 4 * i, (CHUNK, CH), lattice)
        d_hid[at] = jnp.where(inside, grad, 0.0)
        if i == 1:
            small_out[5:6, :] = SCALE * jnp.sum(d_score * hidden, axis=0, keepdims=True)
    d_cell[...] = jnp.zeros_like(d_cell)
    lane = lax.broadcasted_iota(jnp.int32, (1, CH), 1)
    small_out[6:7, :] = jnp.where(lead, d_logit * pooled, 0.0)
    small_out[7:8, :] = jnp.where(jnp.logical_and(lead, lane == 0), loss, 0.0)
    backward_rounds(lattice, meta, rounds, w_ref, gates, d_hid, d_cell, d_pre, dp_out)
    own = pl.ds(CHUNK, CHUNK)
    hid_out[...] = d_hid[own]
    cell_out[...] = d_cell[own]
    for out, at in ((low_out, CHUNK), (high_out, CHUNK + 2 * COLS)):
        out[:, 0:CH] = d_hid[pl.ds(at, 2 * COLS)].astype(jnp.bfloat16)
        out[:, CH:] = d_cell[pl.ds(at, 2 * COLS)].astype(jnp.bfloat16)


def load_adjoint(meta, lattice, rows, below, above, hid_in, cell_in, d_hid, d_cell):
    size = rows * COLS
    blank = jnp.zeros((CHUNK, CH), jnp.float32)
    if rows < 4:
        for i in (0, 2):
            d_hid[pl.ds(i * CHUNK, CHUNK)] = blank
            d_cell[pl.ds(i * CHUNK, CHUNK)] = blank
    for first, ref in ((CHUNK - size, below), (2 * CHUNK, above)):
        inside = rows_inside(meta, 4 + first // COLS, (size, CH), lattice)
        d_hid[pl.ds(first, size)] = jnp.where(inside, ref[:, 0:CH].astype(jnp.float32), 0.0)
        d_cell[pl.ds(first, size)] = jnp.where(inside, ref[:, CH:].astype(jnp.float32), 0.0)
    d_hid[pl.ds(CHUNK, CHUNK)] = hid_in[...]
    d_cell[pl.ds(CHUNK, CHUNK)] = cell_in[...]


def middle_backward(
    lattice, rounds, rows, meta, below, above, hid_in, cell_in, w_ref, gates,
    hid_out, cell_out, edge_out, dp_out, d_hid, d_cell, d_pre,
):
    load_adjoint(meta, lattice, rows, below, above, hid_in, cell_in, d_hid, d_cell)
    backward_rounds(lattice, meta, rounds, w_ref, gates, d_hid, d_cell, d_pre, dp_out)
    own = pl.ds(CHUNK, CHUNK)
    hid_out[...] = d_hid[own]
    cell_out[...] = d_cell[own]
    edge_out[:, 0:CH] = d_hid[own].astype(jnp.bfloat16)
    edge_out[:, CH:] = d_cell[own].astype(jnp.bfloat16)


def last_backward(
    lattice, rounds, rows, meta, below, above, hid_in, cell_in, w_ref, dp_one, dp_two, small_in,
    gates, dp_out, mine_out, other_out, small_out, d_hid, d_cell, d_pre, total,
):
    load_adjoint(meta, lattice, rows, below, above, hid_in, cell_in, d_hid, d_cell)
    backward_rounds(lattice, meta, rounds, w_ref, gates, d_hid, d_cell, d_pre, dp_out)
    summed = None
    for ref, count in ((dp_one, 1), (dp_two, 2), (dp_out, len(rounds))):
        for i in range(count):
            part = ref[i].astype(jnp.float32)
            summed = part if summed is None else summed + part
    total[...] = summed
    core = meta[1]
    half = 2 * COLS
    mine_out[...] = total[pl.ds(pl.multiple_of(core * half, half), half)]
    other_out[...] = total[pl.ds(pl.multiple_of((1 - core) * half, half), half)].astype(jnp.bfloat16)
    small_out[...] = small_in[...]
    small_out[4:5, :] = jnp.sum(total[:, CH : 2 * CH], axis=0, keepdims=True)


def add_kernel(*refs):
    refs[-1][...] = tree_sum([ref[...] for ref in refs[:-1]])


def weight_kernel(
    pieces, meta, bits_ref, small_ref, dp_one, dp_two, dp_three, hist_ref, keep_ref, send_ref,
    dp, grad, fired_sum, dp_sem,
):
    copies = []
    for ref, low in ((dp_one, 7), (dp_two, 6), (dp_three, 4)):
        for i in range(ref.shape[0]):
            copies.append(pltpu.make_async_copy(ref.at[i], dp.at[low - i], dp_sem.at[low - i]))
    for copy in copies:
        copy.start()
    grad[...] = jnp.zeros_like(grad)
    for copy in copies:
        copy.wait()
    word = jnp.concatenate([bits_ref[0], bits_ref[1]], axis=1)

    def add_fired(t):
        rows = jnp.where(lax.broadcasted_iota(jnp.int32, word.shape, 0) == t, word, 0.0)
        return jnp.dot(rows.astype(jnp.bfloat16), dp[t], preferred_element_type=jnp.float32)

    fired_sum[...] = add_fired(0)

    def add_round(t, carry):
        fired_sum[...] += add_fired(t)
        for a in range(3):
            grad[pl.ds(a * 3 * CH, 3 * CH)] += lax.dot_general(
                hist_ref[t - 1, pl.ds(a * COLS, CHUNK)],
                dp[t],
                (((0,), (0,)), ((), ())),
                preferred_element_type=jnp.float32,
            )
        return carry

    lax.fori_loop(1, ROUNDS, add_round, 0)
    fired = jnp.sum(fired_sum[...], axis=0, keepdims=True)
    rows = [fired[:, g * CH : (g + 1) * CH] for g in range(4)]
    words = split_words(jnp.concatenate(rows + [small_ref[4:8, :]], axis=0))
    both = words[0:8].astype(jnp.float32) + words[8:16].astype(jnp.float32)
    core = meta[1]
    per = pieces // 4
    size = 9 * CH // per
    for n in range(pieces // 2):
        g, m = n // per, n % per
        mine = pl.ds(pl.multiple_of((2 * core + g) * CH, CH), CH)
        other = pl.ds(pl.multiple_of((2 - 2 * core + g) * CH, CH), CH)
        keep_ref[n, 0:size, :] = grad[pl.ds(m * size, size), mine]
        keep_ref[n, size : size + 8, :] = both
        send_ref[n, 0:size, :] = grad[pl.ds(m * size, size), other].astype(jnp.bfloat16)
        send_ref[n, size:, :] = words


def final_kernel(
    pieces, planes, meta, mine_ref, other_ref, stab_ref, small_ref, conv_out, stab_out,
    bit_out, keep_out, query_out, read_out, loss_out,
):
    for g in range(4):
        bit_out[:, g * CH : (g + 1) * CH] = small_ref[g : g + 1, :]
    keep_out[...] = small_ref[4:5, :]
    query_out[...] = small_ref[5:6, :]
    read_out[...] = small_ref[6:7, :]
    loss_out[...] = small_ref[7:8, 0:1]
    core = meta[1]
    per = pieces // 4
    size = 9 * CH // per
    for n in range(pieces // 2):
        g, m = n // per, n % per
        mine = pl.ds(pl.multiple_of((2 * core + g) * CH, CH), CH)
        other = pl.ds(pl.multiple_of((2 - 2 * core + g) * CH, CH), CH)
        conv_out[pl.ds(m * size, size), mine] = mine_ref[n].astype(jnp.float32)
        conv_out[pl.ds(m * size, size), other] = other_ref[n].astype(jnp.float32)
    rows = 2 * COLS // planes
    for z in range(planes):
        for g in range(4):
            stab_out[pl.ds(z * rows, rows), g * CH : (g + 1) * CH] = stab_ref[
                z, pl.ds(g * rows, rows)
            ].astype(jnp.float32)


GATES = pltpu.VMEM((ROUNDS, MID, 5 * CH), jnp.float32)


def f32(*shape):
    return jax.ShapeDtypeStruct(shape, jnp.float32)


def b16(*shape):
    return jax.ShapeDtypeStruct(shape, jnp.bfloat16)


def call(kernel, in_specs, out_shape, out_specs, scratch, flops):
    return pl.pallas_call(
        kernel,
        in_specs=in_specs,
        out_shape=out_shape,
        out_specs=out_specs,
        scratch_shapes=scratch,
        cost_estimate=pl.CostEstimate(flops=flops, bytes_accessed=4_000_000, transcendentals=0),
        compiler_params=pltpu.CompilerParams(vmem_limit_bytes=24 * 1024 * 1024),
    )


def segment_scratch(extra):
    return [
        pltpu.VMEM((MID, CH), jnp.float32),
        pltpu.VMEM((MID, CH), jnp.float32),
        pltpu.VMEM((14 * COLS, UNITS), jnp.bfloat16),
        *extra,
    ]


def per_device(
    syndromes, labels, stab_gate, bit_gate, forget_bias, conv_weight, query, readout_weight
):
    tiles = lax.axis_size("tiles")
    planes = lax.axis_size("rounds")
    tile = lax.axis_index("tiles")
    core = tile & 1
    lattice = 2 * tiles
    label = jnp.where(core == 0, labels[0, 0], labels[1, 0])
    meta = jnp.stack([tile // 2, core, label]).astype(jnp.int32)
    weights = conv_weight.reshape(9 * CH, UNITS)
    bit_row = bit_gate.reshape(1, UNITS)
    forget_row = forget_bias.reshape(1, CH)
    query_row = query.reshape(1, CH)
    read_row = readout_weight.reshape(1, CH)

    words = jnp.swapaxes(syndromes[:, :, 0], 0, 1).astype(jnp.bfloat16).reshape(16, 2 * COLS)
    words = jnp.pad(words.reshape(4, UNITS), ((0, 4), (0, 0)))
    own = jnp.concatenate([stab_gate.reshape(2 * COLS, UNITS), words], axis=0)
    near = [shift(own, "tiles", step) for step in (4, 2)]
    far = [shift(own, "tiles", step) for step in (-2, -4)]
    mine = jnp.stack(near + [own] + far)
    theirs = swap(mine, "tiles", 1)

    gates, hist, stats, bits = call(
        functools.partial(forward_kernel, lattice),
        [SMEM, ANY, ANY, VMEM, VMEM, VMEM, VMEM],
        (GATES, b16(ROUNDS, 6 * COLS, 3 * CH), f32(8, CH), f32(2, 8, CH)),
        (VMEM, ANY, VMEM, VMEM),
        [
            pltpu.VMEM((EXT * COLS, UNITS), jnp.bfloat16),
            pltpu.VMEM((10, 8, UNITS), jnp.bfloat16),
            pltpu.VMEM((10, 8, CH), jnp.float32),
            pltpu.VMEM((EXT * COLS, CH), jnp.bfloat16),
            pltpu.VMEM((10 * CH, UNITS), jnp.bfloat16),
            pltpu.VMEM((2, (EXT + 2) * COLS, 3 * CH), jnp.bfloat16),
            pltpu.VMEM((EXT * COLS, CH), jnp.float32),
            pltpu.SemaphoreType.DMA((20,)),
            pltpu.SemaphoreType.DMA((2,)),
        ],
        8_000_000_000,
    )(meta, mine, theirs, weights, bit_row, forget_row, query_row)

    parts = [stats]
    for start, size in tile_groups(tiles):
        if len(parts) > 1:
            stats = call(
                add_kernel, [VMEM] * len(parts), f32(8, CH), VMEM, [], 1_000
            )(*parts)
        parts = [stats] + [swap(stats, "tiles", start * k) for k in range(1, size)]

    first = [7]
    half = 2 * COLS
    d_hid, d_cell, low, high, dp_one, small = call(
        functools.partial(first_backward, lattice, first, len(parts)),
        [SMEM] + [VMEM] * len(parts) + [VMEM, VMEM, VMEM, VMEM],
        (
            f32(CHUNK, CH), f32(CHUNK, CH), b16(half, 2 * CH), b16(half, 2 * CH),
            b16(1, CHUNK, UNITS), f32(8, CH),
        ),
        (VMEM,) * 6,
        segment_scratch([]),
        1_000_000_000,
    )(meta, *parts, query_row, read_row, weights, gates)

    below = shift(high, "tiles", 2)
    above = shift(low, "tiles", -2)
    middle = [6, 5]
    d_hid, d_cell, edge, dp_two = call(
        functools.partial(middle_backward, lattice, middle, 2),
        [SMEM] + [VMEM] * 6,
        (f32(CHUNK, CH), f32(CHUNK, CH), b16(CHUNK, 2 * CH), b16(2, CHUNK, UNITS)),
        (VMEM,) * 4,
        segment_scratch([]),
        2_000_000_000,
    )(meta, below, above, d_hid, d_cell, weights, gates)

    below = shift(edge, "tiles", 2)
    above = shift(edge, "tiles", -2)
    last = [4, 3, 2, 1, 0]
    dp_three, stab_mine, stab_other, small = call(
        functools.partial(last_backward, lattice, last, 4),
        [SMEM] + [VMEM] * 9,
        (b16(5, CHUNK, UNITS), f32(half, UNITS), b16(half, UNITS), f32(8, CH)),
        (VMEM,) * 4,
        segment_scratch([pltpu.VMEM((CHUNK, UNITS), jnp.float32)]),
        4_000_000_000,
    )(meta, below, above, d_hid, d_cell, weights, dp_one, dp_two, small, gates)

    size = 36 * CH // tiles
    chips = tiles // 2
    keep, send = call(
        functools.partial(weight_kernel, tiles),
        [SMEM, VMEM, VMEM, ANY, ANY, ANY, VMEM],
        (f32(chips, size + 8, CH), b16(chips, size + 16, CH)),
        (VMEM, VMEM),
        [
            pltpu.VMEM((ROUNDS, CHUNK, UNITS), jnp.bfloat16),
            pltpu.VMEM((9 * CH, UNITS), jnp.float32),
            pltpu.VMEM((8, UNITS), jnp.float32),
            pltpu.SemaphoreType.DMA((ROUNDS,)),
        ],
        3_000_000_000,
    )(meta, bits, small, dp_one, dp_two, dp_three, hist)
    send, stab_other = lax.optimization_barrier((send, stab_other))
    back = swap(send, "tiles", 1).astype(jnp.float32)
    words = split_words((keep[:, size:] + back[:, size : size + 8] + back[:, size + 8 :])[0])
    message = jnp.concatenate(
        [
            (keep[:, :size] + back[:, :size]).astype(jnp.bfloat16),
            jnp.broadcast_to(words[None], (chips,) + words.shape),
        ],
        axis=1,
    )
    sides = [list(range(side, tiles, 2)) for side in range(2)]
    back = lax.all_to_all(
        message, "tiles", 0, 0, axis_index_groups=sides, tiled=True
    ).astype(jnp.float32)
    piece = jnp.sum(back[:, :size], axis=0)
    small = jnp.sum(back[:, size : size + 8] + back[:, size + 8 :], axis=0)

    stab = stab_mine + swap(stab_other, "tiles", 1).astype(jnp.float32)
    rows = half // planes
    stab = jnp.swapaxes(stab.astype(jnp.bfloat16).reshape(planes, rows, 4, CH), 1, 2)
    stab = stab.reshape(planes, 4 * rows, CH)
    part = size // planes
    words = split_words(small)
    joint = jnp.concatenate(
        [
            stab,
            jnp.broadcast_to(words[None], (planes,) + words.shape),
            piece.astype(jnp.bfloat16).reshape(planes, part, CH),
        ],
        axis=1,
    )
    joint = lax.all_to_all(joint, "rounds", 0, 0, tiled=True).astype(jnp.float32)
    lines = 4 * rows
    small = jnp.sum(joint[:, lines : lines + 8] + joint[:, lines + 8 : lines + 16], axis=0)
    done = jnp.concatenate(
        [jnp.sum(joint[:, :lines], axis=0), jnp.sum(joint[:, lines + 16 :], axis=0)], axis=0
    ).astype(jnp.bfloat16)
    joint = lax.all_to_all(
        jnp.broadcast_to(done[None], (planes,) + done.shape), "rounds", 0, 0, tiled=True
    )
    stab_all = joint[:, :lines]
    piece = joint[:, lines:].reshape(size, CH)
    piece = lax.all_to_all(
        jnp.broadcast_to(piece[None], (chips, size, CH)), "tiles", 0, 0,
        axis_index_groups=sides, tiled=True,
    )
    other = swap(piece, "tiles", 1)
    grad_conv, grad_stab, grad_bit, grad_keep, grad_query, grad_read, loss = call(
        functools.partial(final_kernel, tiles, planes),
        [SMEM, VMEM, VMEM, VMEM, VMEM],
        (f32(9 * CH, UNITS), f32(half, UNITS), f32(1, UNITS), f32(1, CH), f32(1, CH), f32(1, CH), f32(1, 1)),
        (VMEM,) * 7,
        [],
        1_000_000,
    )(meta, piece, other, stab_all, small)
    return (
        grad_conv.reshape(3, 3, CH, UNITS),
        grad_stab.reshape(2, COLS, UNITS),
        grad_bit.reshape(UNITS),
        grad_keep.reshape(CH),
        grad_query.reshape(CH),
        grad_read.reshape(CH),
        loss.reshape(()),
    )


def solution(mesh):
    in_specs = (
        P(None, None, "rounds", "tiles", None),
        P(None, "rounds"),
        P("tiles", None, None),
        P(),
        P(),
        P(),
        P(),
        P(),
    )
    out_specs = (P(), P("tiles", None, None), P(), P(), P(), P(), P())
    return jax.shard_map(
        per_device, mesh=mesh, in_specs=in_specs, out_specs=out_specs, check_vma=False
    )
```
